32 devices in a mesh: ctx: 2 (over core), head: 4 (over y, x), rep: 4 (over z).
Axes of the slice: x: 2, y: 2, z: 4, core: 2. Of those that a mesh axis runs over, the one named last changes fastest.
Arguments:
- queries: bfloat16 [4096, 2048], P(('rep', 'ctx'), 'head'), parts along dimension 0, may hold values from -9 to 9
- keys: bfloat16 [4096, 2048], P(('rep', 'ctx'), 'head'), parts along dimension 0, may hold values from -9 to 9
- values: bfloat16 [4096, 2048], P(('rep', 'ctx'), 'head'), parts along dimension 0, may hold values from -6 to 6
- out_weight: bfloat16 [2048, 4096], P('head', 'ctx'), may hold values from -0.125 to 0.125
- out_grad: bfloat16 [4096, 4096], P(('rep', 'ctx')), parts along dimension 0, may hold values from -6 to 6
Outputs:
- layer_out: bfloat16 [4096, 4096], P(('rep', 'ctx'), 'head'), parts along dimension 0
- query_grad: bfloat16 [4096, 2048], P(('rep', 'ctx'), 'head'), parts along dimension 0
- key_grad: bfloat16 [4096, 2048], P(('rep', 'ctx'), 'head'), parts along dimension 0
- value_grad: bfloat16 [4096, 2048], P(('rep', 'ctx'), 'head'), parts along dimension 0
- weight_grad: float32 [8192, 4096], P(('rep', 'head'), 'ctx'), parts along dimension 0
The draws below stay inside these ranges and needn't reach their ends.
There are 4 independent parts, one for each index of `rep`. The reference program is written for one: setup_inputs(seed, part) draws one part's arguments, and reference() takes and returns one part's arrays. A program takes and returns all parts, laid end to end along the dimension named above; an argument that names none is the same for every part. Nothing has to cross between parts.
All inputs are finite; a program needn't handle non-finite values.
Results may differ from the reference program's by a relative error of at most 0.012.
Values may be sent and summed in bfloat16 or wider, within the bound.
No kernel may reach another device: no remote copies, remote signals or barrier semaphores. Data moves between devices by JAX's collectives and lax.ppermute only.
A program may use at most 128 MiB of HBM per device.

```python
import jax
import jax.numpy as jnp
from jax import lax

D = 4096
DH = 128
H = 16
TILE = 128
TOK_DEV = 512
TOKENS = 1024
HD = 2048
N_CTX = 2


def strengthened(values, stream_key, source, target, parts, factor):
    owner, partner = [(jnp.arange(values.shape[position]) // (values.shape[position] // parts)).reshape([-1 if axis == position else 1 for axis in range(values.ndim)]) for position in (source, target)]
    chosen = jax.random.permutation(stream_key, parts)[partner]
    strong = (owner == chosen) | (owner == (partner + parts // 2) % parts)
    return jnp.where(strong, factor * values, values)


def shard_levels(key, dims, cuts, low, largest):
    def one(position, shards_of):
        heights = jax.random.uniform(jax.random.fold_in(jax.random.fold_in(key, 6), position), (shards_of,), jnp.float32, low / len(cuts), largest / len(cuts))
        return jnp.repeat(jnp.exp(heights), dims[position] // shards_of).reshape((-1,) + (1,) * (len(dims) - position - 1))

    loudness = one(*cuts[0])
    for cut in cuts[1:]:
        loudness = loudness * one(*cut)
    return loudness


def centred(own_key, shape, scale, reach, split=(), kind=jnp.bfloat16):
    values = scale * jax.random.normal(own_key, shape, jnp.float32)
    if split:
        values = values * shard_levels(own_key, shape, split, -0.22, 0.18)
    return jnp.clip(values, -reach, reach).astype(kind)


def bell_draw_with(key, dims, scale, bound, pieces, heavy, dtype=jnp.bfloat16):
    result = scale * jax.random.normal(key, dims, jnp.float32)
    if pieces:
        result = result * shard_levels(key, dims, pieces, -0.22, 0.18)
    return jnp.clip(strengthened(result, jax.random.fold_in(key, 3), *heavy), -bound, bound).astype(dtype)


def setup_inputs(seed: int = 0, part: int = 0) -> dict:
    splits = jax.random.split(jax.random.key(seed), 6)
    part_splits = jax.random.split(jax.random.fold_in(splits[5], part), 6)
    return {
        "queries": centred(part_splits[0], (TOKENS, HD), 1.5, 9.0, ((0, 2), (1, 4))),
        "keys": centred(part_splits[1], (TOKENS, HD), 1.5, 9.0, ((0, 2), (1, 4))),
        "values": centred(part_splits[2], (TOKENS, HD), 1.0, 6.0, ((0, 2), (1, 4))),
        "out_weight": centred(splits[3], (HD, D), HD ** -0.5, 0.125, ((0, 4), (1, 2))),
        "out_grad": bell_draw_with(part_splits[4], (TOKENS, D), 1.0, 6.0, ((0, 2),), (0, 1, 2, 2.0)),
    }


EPS = 1e-06
HIGH = lax.Precision.HIGHEST

def feature(x):
    return jax.nn.elu(x) + 1.0

def causal_normed(fq, fk, vals, heads, width, tile):
    count = fq.shape[0]
    tiles = count // tile
    fq4 = fq.reshape(tiles, tile, heads, width)
    fk4 = fk.reshape(tiles, tile, heads, width)
    v4 = vals.reshape(tiles, tile, heads, width)
    states = jnp.einsum('nshd,nshe->nhde', fk4, v4, precision=HIGH)
    prefix = jnp.cumsum(states, 0) - states
    lower = jnp.tril(jnp.ones((tile, tile), jnp.float32))
    scores = jnp.einsum('nthd,nshd->nhts', fq4, fk4, precision=HIGH) * lower
    raw = jnp.einsum('nhts,nshe->nthe', scores, v4, precision=HIGH)
    raw = raw + jnp.einsum('nthd,nhde->nthe', fq4, prefix, precision=HIGH)
    meansq = lax.optimization_barrier(jnp.mean(raw * raw, axis=-1, keepdims=True))
    normed = raw * lax.rsqrt(meansq + EPS)
    return normed.reshape(count, heads * width)

def reference(queries, keys, values, out_weight, out_grad):

    def forward(qa, ka, va):
        return causal_normed(feature(qa), feature(ka), va, H, DH, TILE)
    normed, pull = jax.vjp(forward, queries.astype(jnp.float32), keys.astype(jnp.float32), values.astype(jnp.float32))
    attn = normed.astype(jnp.bfloat16)
    layer_out = jnp.dot(attn, out_weight, preferred_element_type=jnp.float32).astype(jnp.bfloat16)
    attn_grad = jnp.dot(out_grad, out_weight.T, preferred_element_type=jnp.float32).astype(jnp.bfloat16)

    def add_block(index, total):
        begin = (index * TOK_DEV).astype(jnp.int32)
        block_attn = lax.dynamic_slice_in_dim(attn, begin, TOK_DEV, 0)
        block_grad = lax.dynamic_slice_in_dim(out_grad, begin, TOK_DEV, 0)
        term = jnp.dot(block_attn.T, block_grad, preferred_element_type=jnp.float32).astype(jnp.bfloat16)
        term = lax.optimization_barrier(term)
        return total + term.astype(jnp.float32)
    weight_grad = lax.fori_loop(0, N_CTX, add_block, jnp.zeros((HD, D), jnp.float32))
    grad_q, grad_k, grad_v = pull(attn_grad.astype(jnp.float32))
    return (layer_out, grad_q.astype(jnp.bfloat16), grad_k.astype(jnp.bfloat16), grad_v.astype(jnp.bfloat16), weight_grad)
```

```python
import functools

import jax
import jax.numpy as jnp
from jax import lax
from jax.experimental import pallas as pl
from jax.experimental.pallas import tpu as pltpu
from jax.sharding import PartitionSpec as P

DH = 128
CHUNK = 256
EPS = 1e-06
F32 = jnp.float32
BF16 = jnp.bfloat16


def feature(x):
    return jnp.where(x > 0, x + 1.0, jnp.exp(jnp.minimum(x, 0.0)))


def dot_nn(a, b):
    return lax.dot_general(a, b, (((1,), (0,)), ((), ())), preferred_element_type=F32)


def dot_nt(a, b):
    return lax.dot_general(a, b, (((1,), (1,)), ((), ())), preferred_element_type=F32)


def dot_tn(a, b):
    return lax.dot_general(a, b, (((0,), (0,)), ((), ())), preferred_element_type=F32)


def shape_of(shape, dtype):
    return jax.ShapeDtypeStruct(shape, dtype)


def params(mib):
    return pltpu.CompilerParams(vmem_limit_bytes=mib * 1024 * 1024)


def state_kernel(k_ref, v_ref, out_ref):
    for lo in range(0, k_ref.shape[1], DH):
        cols = slice(lo, lo + DH)
        fk = feature(k_ref[:, cols].astype(F32)).astype(BF16)
        out_ref[cols, :] = dot_tn(fk, v_ref[:, cols]).astype(BF16)


def local_state(keys, values):
    width = keys.shape[1]
    return pl.pallas_call(
        state_kernel, out_shape=shape_of((width, DH), BF16), compiler_params=params(32)
    )(keys, values)


def forward_kernel(q_ref, k_ref, v_ref, carried_ref, attn_ref, raw_ref, prefix_ref):
    tok, width = q_ref.shape
    chunk = min(CHUNK, tok)
    row = lax.broadcasted_iota(jnp.int32, (chunk, chunk), 0)
    col = lax.broadcasted_iota(jnp.int32, (chunk, chunk), 1)
    lower = row >= col
    for lo in range(0, width, DH):
        cols = slice(lo, lo + DH)
        prefix = carried_ref[cols, :].astype(F32)
        for i in range(tok // chunk):
            rows = slice(i * chunk, (i + 1) * chunk)
            fq = feature(q_ref[rows, cols].astype(F32)).astype(BF16)
            fk = feature(k_ref[rows, cols].astype(F32)).astype(BF16)
            v = v_ref[rows, cols]
            low_prefix = prefix.astype(BF16)
            prefix_ref[i, cols, :] = low_prefix
            scores = jnp.where(lower, dot_nt(fq, fk), 0.0).astype(BF16)
            raw = dot_nn(scores, v) + dot_nn(fq, low_prefix)
            raw_ref[rows, cols] = raw
            inv = lax.rsqrt(jnp.mean(raw * raw, axis=-1, keepdims=True) + EPS)
            attn_ref[rows, cols] = (raw * inv).astype(BF16)
            if i + 1 < tok // chunk:
                prefix = prefix + dot_tn(fk, v)


def forward(queries, keys, values, carried):
    tok, width = queries.shape
    chunks = tok // min(CHUNK, tok)
    return pl.pallas_call(
        forward_kernel,
        out_shape=(
            shape_of((tok, width), BF16),
            shape_of((tok, width), F32),
            shape_of((chunks, width, DH), BF16),
        ),
        compiler_params=params(32),
    )(queries, keys, values, carried)


def cotangent_kernel(own_blocks, s_ref, grad_ref, own_ref, rest_ref, q_ref, raw_ref,
                     draw_ref, gsum_ref, glocal_ref, acc_ref):
    step = pl.program_id(0)

    @pl.when(step == 0)
    def _():
        acc_ref[...] = dot_nt(grad_ref[...], own_ref[...])

    @pl.when((step > 0) & (step < own_blocks))
    def _():
        acc_ref[...] += dot_nt(grad_ref[...], own_ref[...])

    @pl.when(step >= own_blocks)
    def _():
        acc_ref[...] += dot_nt(grad_ref[...], rest_ref[...])

    @pl.when(step == pl.num_programs(0) - 1)
    def _():
        tok, width = q_ref.shape
        chunk = min(CHUNK, tok)
        for lo in range(0, width, DH):
            cols = slice(lo, lo + DH)
            later = jnp.zeros((DH, DH), F32)
            for i in reversed(range(tok // chunk)):
                rows = slice(i * chunk, (i + 1) * chunk)
                glocal_ref[i, cols, :] = later
                grad = acc_ref[rows, cols].astype(BF16).astype(F32)
                raw = raw_ref[rows, cols]
                inv = lax.rsqrt(jnp.mean(raw * raw, axis=-1, keepdims=True) + EPS)
                normed = raw * inv
                mean = jnp.mean(grad * normed, axis=-1, keepdims=True)
                draw = (inv * (grad - normed * mean)).astype(BF16)
                draw_ref[rows, cols] = draw
                fq = feature(q_ref[rows, cols].astype(F32)).astype(BF16)
                later = later + dot_tn(fq, draw)
            gsum_ref[cols, :] = later.astype(BF16)


def cotangent(scal, out_grad, own, rest, queries, raw):
    tok, width = queries.shape
    block = min(1024, own.shape[1])
    own_blocks = own.shape[1] // block
    blocks = out_grad.shape[1] // block
    chunks = tok // min(CHUNK, tok)
    whole = lambda *dims: pl.BlockSpec(dims, lambda j, s: (0,) * len(dims))
    return pl.pallas_call(
        functools.partial(cotangent_kernel, own_blocks),
        out_shape=(
            shape_of((tok, width), BF16),
            shape_of((width, DH), BF16),
            shape_of((chunks, width, DH), F32),
        ),
        grid_spec=pltpu.PrefetchScalarGridSpec(
            num_scalar_prefetch=1,
            grid=(blocks,),
            in_specs=[
                pl.BlockSpec((tok, block), lambda j, s: (0, lax.rem(s[0] * own_blocks + j, blocks))),
                pl.BlockSpec((width, block), lambda j, s: (0, jnp.minimum(j, own_blocks - 1))),
                pl.BlockSpec((width, block), lambda j, s: (0, jnp.maximum(j - own_blocks, 0))),
                whole(tok, width),
                whole(tok, width),
            ],
            out_specs=(whole(tok, width), whole(width, DH), whole(chunks, width, DH)),
            scratch_shapes=[pltpu.VMEM((tok, width), F32)],
        ),
        compiler_params=params(40),
    )(scal, out_grad, own, rest, queries, raw)


def term_kernel(s_ref, attn_ref, grad_ref, out_ref):
    out_ref[...] = dot_tn(attn_ref[...], grad_ref[...]).astype(BF16)


def term_for_others(scal, attn, out_grad, own_width):
    tok, width = attn.shape
    block = min(1024, own_width)
    own_blocks = own_width // block
    blocks = out_grad.shape[1] // block
    return pl.pallas_call(
        term_kernel,
        out_shape=shape_of((width, out_grad.shape[1] - own_width), BF16),
        grid_spec=pltpu.PrefetchScalarGridSpec(
            num_scalar_prefetch=1,
            grid=(blocks - own_blocks,),
            in_specs=[
                pl.BlockSpec((tok, width), lambda j, s: (0, 0)),
                pl.BlockSpec(
                    (tok, block), lambda j, s: (0, lax.rem(s[0] * own_blocks + own_blocks + j, blocks))
                ),
            ],
            out_specs=pl.BlockSpec((width, block), lambda j, s: (0, j)),
        ),
        compiler_params=params(32),
    )(scal, attn, out_grad)


def weight_grad_kernel(s_ref, attn_ref, grad_ref, others_ref, out_ref):
    term = dot_tn(attn_ref[...], grad_ref[...]).astype(BF16)
    out_ref[...] = term.astype(F32) + others_ref[...].astype(F32)


def own_weight_grad(scal, attn, out_grad, others):
    tok, width = attn.shape
    own_width = others.shape[1]
    block = min(1024, own_width)
    own_blocks = own_width // block
    return pl.pallas_call(
        weight_grad_kernel,
        out_shape=shape_of((width, own_width), F32),
        grid_spec=pltpu.PrefetchScalarGridSpec(
            num_scalar_prefetch=1,
            grid=(own_blocks,),
            in_specs=[
                pl.BlockSpec((tok, width), lambda j, s: (0, 0)),
                pl.BlockSpec((tok, block), lambda j, s: (0, s[0] * own_blocks + j)),
                pl.BlockSpec((width, block), lambda j, s: (0, j)),
            ],
            out_specs=pl.BlockSpec((width, block), lambda j, s: (0, j)),
        ),
        compiler_params=params(32),
    )(scal, attn, out_grad, others)


def backward_kernel(q_ref, k_ref, v_ref, draw_ref, prefix_ref, suffix_ref, glocal_ref,
                    dq_ref, dk_ref, dv_ref):
    tok, width = q_ref.shape
    chunk = min(CHUNK, tok)
    row = lax.broadcasted_iota(jnp.int32, (chunk, chunk), 0)
    col = lax.broadcasted_iota(jnp.int32, (chunk, chunk), 1)
    lower = row >= col
    upper = row <= col
    for lo in range(0, width, DH):
        cols = slice(lo, lo + DH)
        suffix = suffix_ref[cols, :].astype(F32)
        for i in range(tok // chunk):
            rows = slice(i * chunk, (i + 1) * chunk)
            q = q_ref[rows, cols].astype(F32)
            k = k_ref[rows, cols].astype(F32)
            q_slope = jnp.exp(jnp.minimum(q, 0.0))
            k_slope = jnp.exp(jnp.minimum(k, 0.0))
            fq = jnp.where(q > 0, q + 1.0, q_slope).astype(BF16)
            fk = jnp.where(k > 0, k + 1.0, k_slope).astype(BF16)
            v = v_ref[rows, cols]
            draw = draw_ref[rows, cols]
            later = (suffix + glocal_ref[i, cols, :]).astype(BF16)
            dscores = jnp.where(lower, dot_nt(draw, v), 0.0).astype(BF16)
            dfq = dot_nn(dscores, fk) + dot_nt(draw, prefix_ref[i, cols, :])
            dq_ref[rows, cols] = (dfq * q_slope).astype(BF16)
            dscores_t = jnp.where(upper, dot_nt(v, draw), 0.0).astype(BF16)
            dfk = dot_nn(dscores_t, fq) + dot_nt(v, later)
            dk_ref[rows, cols] = (dfk * k_slope).astype(BF16)
            scores_t = jnp.where(upper, dot_nt(fk, fq), 0.0).astype(BF16)
            dv = dot_nn(scores_t, draw) + dot_nn(fk, later)
            dv_ref[rows, cols] = dv.astype(BF16)


def backward(queries, keys, values, draw, prefix, suffix, glocal):
    out = shape_of(queries.shape, BF16)
    return pl.pallas_call(
        backward_kernel, out_shape=(out, out, out), compiler_params=params(40)
    )(queries, keys, values, draw, prefix, suffix, glocal)


def project_kernel(s_ref, a_ref, a1_ref, a2_ref, a3_ref, own_ref, rest_ref,
                   m1_ref, z1_ref, o1_ref, oz1_ref, d_ref, dz_ref, od_ref, odz_ref, out_ref, acc_ref):
    half = m1_ref.shape[0]
    first = pl.ds(pl.multiple_of(s_ref[3] * half, half), half)
    second = pl.ds(pl.multiple_of((1 - s_ref[3]) * half, half), half)

    @pl.when(s_ref[0] == s_ref[1])
    def _():
        acc_ref[...] = dot_nn(a_ref[...], own_ref[...])

    @pl.when(s_ref[0] != s_ref[1])
    def _():
        acc_ref[...] = dot_nn(a_ref[...], rest_ref[...])

    acc = acc_ref[...]
    acc += dot_nn(a1_ref[:, first], m1_ref[...])
    acc += dot_nn(a1_ref[:, second], z1_ref[...])
    acc += dot_nn(a2_ref[:, first], o1_ref[...])
    acc += dot_nn(a2_ref[:, second], oz1_ref[...])
    acc += dot_nn(a3_ref[:, first], d_ref[...] + od_ref[...])
    acc += dot_nn(a3_ref[:, second], dz_ref[...] + odz_ref[...])
    out_ref[...] = acc.astype(BF16)


def project(scal, attns, own, rest, pieces):
    tok, width = attns[0].shape
    half, out_width = pieces[0].shape
    block = 512
    blocks = out_width // block
    whole = pl.BlockSpec((tok, width), lambda j, s: (0, 0))
    local = pl.BlockSpec((width, block), lambda j, s: (0, s[2] * blocks + j))
    piece = pl.BlockSpec((half, block), lambda j, s: (0, j))
    return pl.pallas_call(
        project_kernel,
        out_shape=shape_of((tok, out_width), BF16),
        grid_spec=pltpu.PrefetchScalarGridSpec(
            num_scalar_prefetch=1,
            grid=(blocks,),
            in_specs=[whole] * 4 + [local] * 2 + [piece] * 8,
            out_specs=pl.BlockSpec((tok, block), lambda j, s: (0, j)),
            scratch_shapes=[pltpu.VMEM((tok, block), F32)],
        ),
        compiler_params=params(40),
    )(scal, *attns, own, rest, *pieces)


def shift(array, axis, count, by, wrap):
    pairs = [(i, (i + by) % count) for i in range(count) if wrap or 0 <= i + by < count]
    return lax.ppermute(array, axis, pairs)


def total(arrays):
    if len(arrays) == 1:
        return arrays[0]
    return functools.reduce(jnp.add, [a.astype(F32) for a in arrays])


def body(n_ctx, n_head, n_rep, queries, keys, values, out_weight, out_grad):
    c, h, z = lax.axis_index("ctx"), lax.axis_index("head"), lax.axis_index("rep")
    x, y, p = h % 2, h // 2, z % 2
    scal = jnp.stack([c, y, x, p]).astype(jnp.int32)
    paired = n_ctx == 2 and n_head == 4 and n_rep % 2 == 0
    own_width = out_weight.shape[1]

    if paired:
        group = ("ctx", "head")
        half, wide = out_weight.shape[0] // 2, out_weight.shape[1] // 2
        near = [(4 * (i // 2) + i, i ^ 1) for i in range(4)]
        near += [(4 * (1 - i // 2) + i, 4 + (i ^ 2)) for i in range(4)]
        far = [(4 * (1 - i // 2) + i, i ^ 3) for i in range(4)]
        start = p * half
        near_piece = lax.dynamic_slice(
            out_weight, (start, wide * jnp.where(c == y, 1 - x, x)), (half, wide)
        )
        far_piece = lax.dynamic_slice(out_weight, (start, wide * (1 - x)), (half, wide))
        near_mine = lax.ppermute(near_piece, group, near)
        far_mine = lax.ppermute(far_piece, group, far)

    rest = [shift(out_weight, "ctx", n_ctx, -k, True) for k in range(1, n_ctx)]
    rest = rest[0] if n_ctx == 2 else jnp.concatenate(rest, 1)

    state = local_state(keys, values)
    carried = total([shift(state, "ctx", n_ctx, k, False) for k in range(1, n_ctx)])
    attn, raw, prefix = forward(queries, keys, values, carried)

    if paired:
        zpair = [(i, i ^ 1) for i in range(n_rep)]
        swap = [(0, 1), (1, 0)]
        one = [(i, i ^ 1) for i in range(4)] + [(4 + i, 4 + (i ^ 2)) for i in range(4)]
        two = [(i, i ^ 2) for i in range(4)] + [(4 + i, 4 + (i ^ 1)) for i in range(4)]
        attn_1 = lax.ppermute(attn, group, one)
        attn_2 = lax.ppermute(attn, group, two)
        near_z = lax.ppermute(near_mine, "rep", zpair)
        far_z = lax.ppermute(far_mine, "rep", zpair)
        attn_3 = lax.ppermute(attn_1, group, two)
        near_other = lax.ppermute(near_mine, "ctx", swap)
        near_other_z = lax.ppermute(near_z, "ctx", swap)
        far_other = lax.ppermute(far_mine, "ctx", swap)
        far_other_z = lax.ppermute(far_z, "ctx", swap)

    draw, gsum, glocal = cotangent(scal, out_grad, out_weight, rest, queries, raw)
    suffix = total([shift(gsum, "ctx", n_ctx, -k, False) for k in range(1, n_ctx)])

    terms = term_for_others(scal, attn, out_grad, own_width)
    others = []
    for k in range(1, n_ctx):
        term = terms[:, (k - 1) * own_width : k * own_width] if n_ctx > 2 else terms
        others.append(shift(term, "ctx", n_ctx, k, True))
    query_grad, key_grad, value_grad = backward(queries, keys, values, draw, prefix, suffix, glocal)
    weight_grad = own_weight_grad(scal, attn, out_grad, total(others))

    if paired:
        layer_out = project(
            scal, (attn, attn_1, attn_2, attn_3), out_weight, rest,
            (near_mine, near_z, near_other, near_other_z, far_mine, far_z, far_other, far_other_z),
        )
    else:
        full = lax.all_gather(out_weight, "ctx", axis=1, tiled=True)
        partial_out = jnp.dot(attn, full, preferred_element_type=F32).astype(BF16)
        layer_out = lax.psum_scatter(partial_out, "head", scatter_dimension=1, tiled=True)
    return layer_out, query_grad, key_grad, value_grad, weight_grad


def solution(mesh):
    tokens = P(("rep", "ctx"), "head")
    sizes = mesh.shape["ctx"], mesh.shape["head"], mesh.shape["rep"]
    return jax.shard_map(
        functools.partial(body, *sizes),
        mesh=mesh,
        in_specs=(tokens, tokens, tokens, P("head", "ctx"), P(("rep", "ctx"), None)),
        out_specs=(tokens, tokens, tokens, tokens, P(("rep", "head"), "ctx")),
        check_vma=False,
    )
```

```python
import functools

import jax
import jax.numpy as jnp
from jax import lax
from jax.experimental import pallas as pl
from jax.experimental.pallas import tpu as pltpu
from jax.sharding import PartitionSpec as P

DH = 128
CHUNK = 256
EPS = 1e-06
F32 = jnp.float32
BF16 = jnp.bfloat16


def feature(x):
    return jnp.where(x > 0, x + 1.0, jnp.exp(jnp.minimum(x, 0.0)))


def dot_nn(a, b):
    return lax.dot_general(a, b, (((1,), (0,)), ((), ())), preferred_element_type=F32)


def dot_nt(a, b):
    return lax.dot_general(a, b, (((1,), (1,)), ((), ())), preferred_element_type=F32)


def dot_tn(a, b):
    return lax.dot_general(a, b, (((0,), (0,)), ((), ())), preferred_element_type=F32)


def shape_of(shape, dtype):
    return jax.ShapeDtypeStruct(shape, dtype)


def params(mib):
    return pltpu.CompilerParams(vmem_limit_bytes=mib * 1024 * 1024)


def cost(flops, moved):
    return pl.CostEstimate(flops=flops, transcendentals=0, bytes_accessed=moved)


def state_kernel(k_ref, v_ref, out_ref):
    for lo in range(0, k_ref.shape[1], DH):
        cols = slice(lo, lo + DH)
        fk = feature(k_ref[:, cols].astype(F32)).astype(BF16)
        out_ref[cols, :] = dot_tn(fk, v_ref[:, cols]).astype(BF16)


def local_state(keys, values):
    width = keys.shape[1]
    return pl.pallas_call(
        state_kernel,
        out_shape=shape_of((width, DH), BF16),
        compiler_params=params(32),
        cost_estimate=cost(2 * keys.size * DH, 4 * keys.size),
    )(keys, values)


def opening_kernel(s_ref, k_hbm, v_hbm, weight_hbm, grad_hbm, state_ref, near_ref, far_ref, turn_ref,
                   k_buf, v_buf, sems, slice_sems):
    half, wide = near_ref.shape
    rows = pl.ds(pl.multiple_of(s_ref[3] * half, half), half)
    far_column = 1 - s_ref[2]
    near_column = jnp.where(s_ref[0] == s_ref[1], far_column, s_ref[2])
    slices = []
    for i, (column, ref) in enumerate([(near_column, near_ref), (far_column, far_ref)]):
        cols = pl.ds(pl.multiple_of(column * wide, wide), wide)
        slices.append(pltpu.make_async_copy(weight_hbm.at[rows, cols], ref, slice_sems.at[i]))
    own = turn_ref.shape[1]
    cols = pl.ds(pl.multiple_of((1 - s_ref[0]) * own, own), own)
    slices.append(pltpu.make_async_copy(grad_hbm.at[:, cols], turn_ref, slice_sems.at[2]))
    slices[0].start()
    loads = []
    for i, lo in enumerate(range(0, k_hbm.shape[1], DH)):
        cols = pl.ds(lo, DH)
        loads.append([
            pltpu.make_async_copy(k_hbm.at[:, cols], k_buf.at[:, cols], sems.at[0, i]),
            pltpu.make_async_copy(v_hbm.at[:, cols], v_buf.at[:, cols], sems.at[1, i]),
        ])
        loads[-1][0].start()
        loads[-1][1].start()
    slices[1].start()
    slices[2].start()
    for i, lo in enumerate(range(0, k_hbm.shape[1], DH)):
        cols = slice(lo, lo + DH)
        loads[i][0].wait()
        loads[i][1].wait()
        fk = feature(k_buf[:, cols].astype(F32)).astype(BF16)
        state_ref[cols, :] = dot_tn(fk, v_buf[:, cols]).astype(BF16)
    for piece in slices:
        piece.wait()


def opening(scal, keys, values, weight, out_grad):
    tok, width = keys.shape
    piece = shape_of((weight.shape[0] // 2, weight.shape[1] // 2), BF16)
    hbm = pl.BlockSpec(memory_space=pltpu.HBM)
    return pl.pallas_call(
        opening_kernel,
        out_shape=(shape_of((width, DH), BF16), piece, piece, shape_of((tok, weight.shape[1]), BF16)),
        grid_spec=pltpu.PrefetchScalarGridSpec(
            num_scalar_prefetch=1,
            grid=(1,),
            in_specs=[hbm] * 4,
            out_specs=(
                pl.BlockSpec((width, DH), lambda j, s: (0, 0)),
                pl.BlockSpec(memory_space=pl.ANY),
                pl.BlockSpec(memory_space=pl.ANY),
                pl.BlockSpec(memory_space=pl.ANY),
            ),
            scratch_shapes=[
                pltpu.VMEM((tok, width), BF16),
                pltpu.VMEM((tok, width), BF16),
                pltpu.SemaphoreType.DMA((2, width // DH)),
                pltpu.SemaphoreType.DMA((3,)),
            ],
        ),
        compiler_params=params(32),
        cost_estimate=cost(2 * keys.size * DH, 4 * keys.size),
    )(scal, keys, values, weight, out_grad)


def forward_kernel(q_ref, k_ref, v_ref, carried_ref, attn_ref, raw_ref, prefix_ref):
    tok, width = q_ref.shape
    chunk = min(CHUNK, tok)
    row = lax.broadcasted_iota(jnp.int32, (chunk, chunk), 0)
    col = lax.broadcasted_iota(jnp.int32, (chunk, chunk), 1)
    lower = row >= col
    for lo in range(0, width, DH):
        cols = slice(lo, lo + DH)
        prefix = carried_ref[cols, :].astype(F32)
        for i in range(tok // chunk):
            rows = slice(i * chunk, (i + 1) * chunk)
            fq = feature(q_ref[rows, cols].astype(F32)).astype(BF16)
            fk = feature(k_ref[rows, cols].astype(F32)).astype(BF16)
            v = v_ref[rows, cols]
            low_prefix = prefix.astype(BF16)
            prefix_ref[i, cols, :] = low_prefix
            scores = jnp.where(lower, dot_nt(fq, fk), 0.0).astype(BF16)
            raw = dot_nn(scores, v) + dot_nn(fq, low_prefix)
            raw_ref[rows, cols] = raw
            inv = lax.rsqrt(jnp.mean(raw * raw, axis=-1, keepdims=True) + EPS)
            attn_ref[rows, cols] = (raw * inv).astype(BF16)
            if i + 1 < tok // chunk:
                prefix = prefix + dot_tn(fk, v)


def forward(queries, keys, values, carried):
    tok, width = queries.shape
    chunks = tok // min(CHUNK, tok)
    return pl.pallas_call(
        forward_kernel,
        out_shape=(
            shape_of((tok, width), BF16),
            shape_of((tok, width), F32),
            shape_of((chunks, width, DH), BF16),
        ),
        compiler_params=params(32),
        cost_estimate=cost(16 * queries.size * DH, 12 * queries.size),
    )(queries, keys, values, carried)


def cotangent_kernel(own_blocks, s_ref, grad_ref, own_ref, rest_ref, q_ref, raw_ref,
                     draw_ref, gsum_ref, glocal_ref, acc_ref):
    step = pl.program_id(0)

    @pl.when(step == 0)
    def _():
        acc_ref[...] = dot_nt(grad_ref[...], own_ref[...])

    @pl.when((step > 0) & (step < own_blocks))
    def _():
        acc_ref[...] += dot_nt(grad_ref[...], own_ref[...])

    @pl.when(step >= own_blocks)
    def _():
        acc_ref[...] += dot_nt(grad_ref[...], rest_ref[...])

    @pl.when(step == pl.num_programs(0) - 1)
    def _():
        tok, width = q_ref.shape
        chunk = min(CHUNK, tok)
        for lo in range(0, width, DH):
            cols = slice(lo, lo + DH)
            later = jnp.zeros((DH, DH), F32)
            for i in reversed(range(tok // chunk)):
                rows = slice(i * chunk, (i + 1) * chunk)
                glocal_ref[i, cols, :] = later
                grad = acc_ref[rows, cols].astype(BF16).astype(F32)
                raw = raw_ref[rows, cols]
                inv = lax.rsqrt(jnp.mean(raw * raw, axis=-1, keepdims=True) + EPS)
                normed = raw * inv
                mean = jnp.mean(grad * normed, axis=-1, keepdims=True)
                draw = (inv * (grad - normed * mean)).astype(BF16)
                draw_ref[rows, cols] = draw
                fq = feature(q_ref[rows, cols].astype(F32)).astype(BF16)
                later = later + dot_tn(fq, draw)
            gsum_ref[cols, :] = later.astype(BF16)


def cotangent(scal, out_grad, own, rest, queries, raw):
    tok, width = queries.shape
    block = min(1024, own.shape[1])
    own_blocks = own.shape[1] // block
    blocks = out_grad.shape[1] // block
    chunks = tok // min(CHUNK, tok)
    whole = lambda *dims: pl.BlockSpec(dims, lambda j, s: (0,) * len(dims))
    return pl.pallas_call(
        functools.partial(cotangent_kernel, own_blocks),
        out_shape=(
            shape_of((tok, width), BF16),
            shape_of((width, DH), BF16),
            shape_of((chunks, width, DH), F32),
        ),
        grid_spec=pltpu.PrefetchScalarGridSpec(
            num_scalar_prefetch=1,
            grid=(blocks,),
            in_specs=[
                pl.BlockSpec((tok, block), lambda j, s: (0, lax.rem(s[0] * own_blocks + j, blocks))),
                pl.BlockSpec((width, block), lambda j, s: (0, jnp.minimum(j, own_blocks - 1))),
                pl.BlockSpec((width, block), lambda j, s: (0, jnp.maximum(j - own_blocks, 0))),
                whole(tok, width),
                whole(tok, width),
            ],
            out_specs=(whole(tok, width), whole(width, DH), whole(chunks, width, DH)),
            scratch_shapes=[pltpu.VMEM((tok, width), F32)],
        ),
        compiler_params=params(40),
        cost_estimate=cost(4 * out_grad.size * width, 4 * out_grad.size),
    )(scal, out_grad, own, rest, queries, raw)


def weight_grad_kernel(s_ref, attn_ref, grad_ref, other_attn_ref, other_grad_ref, out_ref):
    tok = attn_ref.shape[0]
    acc = dot_tn(attn_ref[...], grad_ref[...]).astype(BF16).astype(F32)
    for lo in range(0, other_attn_ref.shape[0], tok):
        rows = slice(lo, lo + tok)
        acc += dot_tn(other_attn_ref[rows, :], other_grad_ref[rows, :]).astype(BF16).astype(F32)
    out_ref[...] = acc


def own_weight_grad(scal, attn, out_grad, other_attn, other_grad):
    tok, width = attn.shape
    other_tok, own_width = other_grad.shape
    block = min(512, own_width)
    own_blocks = own_width // block
    return pl.pallas_call(
        weight_grad_kernel,
        out_shape=shape_of((width, own_width), F32),
        grid_spec=pltpu.PrefetchScalarGridSpec(
            num_scalar_prefetch=1,
            grid=(own_blocks,),
            in_specs=[
                pl.BlockSpec((tok, width), lambda j, s: (0, 0)),
                pl.BlockSpec((tok, block), lambda j, s: (0, s[0] * own_blocks + j)),
                pl.BlockSpec((other_tok, width), lambda j, s: (0, 0)),
                pl.BlockSpec((other_tok, block), lambda j, s: (0, j)),
            ],
            out_specs=pl.BlockSpec((width, block), lambda j, s: (0, j)),
        ),
        compiler_params=params(40),
        cost_estimate=cost(4 * out_grad.size * width, 4 * out_grad.size),
    )(scal, attn, out_grad, other_attn, other_grad)


def backward_kernel(q_ref, k_ref, v_ref, draw_ref, prefix_ref, suffix_ref, glocal_ref,
                    dq_ref, dk_ref, dv_ref):
    tok, width = q_ref.shape
    chunk = min(CHUNK, tok)
    row = lax.broadcasted_iota(jnp.int32, (chunk, chunk), 0)
    col = lax.broadcasted_iota(jnp.int32, (chunk, chunk), 1)
    lower = row >= col
    upper = row <= col
    for lo in range(0, width, DH):
        cols = slice(lo, lo + DH)
        suffix = suffix_ref[cols, :].astype(F32)
        for i in range(tok // chunk):
            rows = slice(i * chunk, (i + 1) * chunk)
            q = q_ref[rows, cols].astype(F32)
            k = k_ref[rows, cols].astype(F32)
            q_slope = jnp.exp(jnp.minimum(q, 0.0))
            k_slope = jnp.exp(jnp.minimum(k, 0.0))
            fq = jnp.where(q > 0, q + 1.0, q_slope).astype(BF16)
            fk = jnp.where(k > 0, k + 1.0, k_slope).astype(BF16)
            v = v_ref[rows, cols]
            draw = draw_ref[rows, cols]
            later = (suffix + glocal_ref[i, cols, :]).astype(BF16)
            dscores = jnp.where(lower, dot_nt(draw, v), 0.0).astype(BF16)
            dfq = dot_nn(dscores, fk) + dot_nt(draw, prefix_ref[i, cols, :])
            dq_ref[rows, cols] = (dfq * q_slope).astype(BF16)
            dscores_t = jnp.where(upper, dot_nt(v, draw), 0.0).astype(BF16)
            dfk = dot_nn(dscores_t, fq) + dot_nt(v, later)
            dk_ref[rows, cols] = (dfk * k_slope).astype(BF16)
            scores_t = jnp.where(upper, dot_nt(fk, fq), 0.0).astype(BF16)
            dv = dot_nn(scores_t, draw) + dot_nn(fk, later)
            dv_ref[rows, cols] = dv.astype(BF16)


def backward(queries, keys, values, draw, prefix, suffix, glocal):
    out = shape_of(queries.shape, BF16)
    return pl.pallas_call(
        backward_kernel, out_shape=(out, out, out), compiler_params=params(40),
        cost_estimate=cost(32 * queries.size * DH, 16 * queries.size),
    )(queries, keys, values, draw, prefix, suffix, glocal)


def halves(s_ref, half):
    first = pl.ds(pl.multiple_of(s_ref[3] * half, half), half)
    second = pl.ds(pl.multiple_of((1 - s_ref[3]) * half, half), half)
    return first, second


def project_near_kernel(s_ref, a_ref, a1_ref, a2_ref, own_ref, rest_ref,
                        m1_ref, z1_ref, o1_ref, oz1_ref, out_ref):
    first, second = halves(s_ref, m1_ref.shape[0])

    @pl.when(s_ref[0] == s_ref[1])
    def _():
        out_ref[...] = dot_nn(a_ref[...], own_ref[...])

    @pl.when(s_ref[0] != s_ref[1])
    def _():
        out_ref[...] = dot_nn(a_ref[...], rest_ref[...])

    acc = dot_nn(a1_ref[:, first], m1_ref[...])
    acc += dot_nn(a1_ref[:, second], z1_ref[...])
    acc += dot_nn(a2_ref[:, first], o1_ref[...])
    acc += dot_nn(a2_ref[:, second], oz1_ref[...])
    out_ref[...] += acc


def project_near(scal, attns, own, rest, pieces):
    tok, width = attns[0].shape
    half, out_width = pieces[0].shape
    block = 512
    blocks = out_width // block
    whole = pl.BlockSpec((tok, width), lambda j, s: (0, 0))
    local = pl.BlockSpec((width, block), lambda j, s: (0, s[2] * blocks + j))
    piece = pl.BlockSpec((half, block), lambda j, s: (0, j))
    return pl.pallas_call(
        project_near_kernel,
        out_shape=shape_of((tok, out_width), F32),
        grid_spec=pltpu.PrefetchScalarGridSpec(
            num_scalar_prefetch=1,
            grid=(blocks,),
            in_specs=[whole] * 3 + [local] * 2 + [piece] * 4,
            out_specs=pl.BlockSpec((tok, block), lambda j, s: (0, j)),
        ),
        compiler_params=params(40),
        cost_estimate=cost(6 * tok * width * out_width, 8 * width * out_width),
    )(scal, *attns, own, rest, *pieces)


def project_far_kernel(s_ref, near_ref, a_ref, d_ref, od_ref, dz_ref, odz_ref, out_ref):
    first, second = halves(s_ref, d_ref.shape[0])
    acc = near_ref[...] + dot_nn(a_ref[:, first], d_ref[...] + od_ref[...])
    out_ref[...] = (acc + dot_nn(a_ref[:, second], dz_ref[...] + odz_ref[...])).astype(BF16)


def project_far(scal, near, attn, pieces):
    tok, width = attn.shape
    half, out_width = pieces[0].shape
    block = 512
    piece = pl.BlockSpec((half, block), lambda j, s: (0, j))
    out = pl.BlockSpec((tok, block), lambda j, s: (0, j))
    return pl.pallas_call(
        project_far_kernel,
        out_shape=shape_of((tok, out_width), BF16),
        grid_spec=pltpu.PrefetchScalarGridSpec(
            num_scalar_prefetch=1,
            grid=(out_width // block,),
            in_specs=[out, pl.BlockSpec((tok, width), lambda j, s: (0, 0))] + [piece] * 4,
            out_specs=out,
        ),
        compiler_params=params(40),
        cost_estimate=cost(2 * tok * width * out_width, 8 * width * out_width),
    )(scal, near, attn, *pieces)


def in_hbm(array):
    return pltpu.with_memory_space_constraint(array, pltpu.HBM)


def after(array, *needed):
    return lax.optimization_barrier((array, *needed))[0]


def shift(array, axis, count, by, wrap):
    pairs = [(i, (i + by) % count) for i in range(count) if wrap or 0 <= i + by < count]
    return lax.ppermute(array, axis, pairs)


def total(arrays):
    if len(arrays) == 1:
        return arrays[0]
    return functools.reduce(jnp.add, [a.astype(F32) for a in arrays])


def body(n_ctx, n_head, n_rep, queries, keys, values, out_weight, out_grad):
    c, h, z = lax.axis_index("ctx"), lax.axis_index("head"), lax.axis_index("rep")
    x, y, p = h & 1, h >> 1, z & 1
    scal = jnp.stack([c, y, x, p]).astype(jnp.int32)
    paired = n_ctx == 2 and n_head == 4 and n_rep % 2 == 0
    own_width = out_weight.shape[1]
    weight_hbm, grad_hbm = in_hbm(out_weight), in_hbm(out_grad)

    if paired:
        group = ("ctx", "head")
        near = [(4 * (i // 2) + i, i ^ 1) for i in range(4)]
        near += [(4 * (1 - i // 2) + i, 4 + (i ^ 2)) for i in range(4)]
        far = [(4 * (1 - i // 2) + i, i ^ 3) for i in range(4)]
        one = [(i, i ^ 1) for i in range(4)] + [(4 + i, 4 + (i ^ 2)) for i in range(4)]
        two = [(i, i ^ 2) for i in range(4)] + [(4 + i, 4 + (i ^ 1)) for i in range(4)]
        zpair = [(i, i ^ 1) for i in range(n_rep)]
        swap = [(0, 1), (1, 0)]
        state, near_piece, far_piece, turn = opening(
            scal, in_hbm(keys), in_hbm(values), weight_hbm, grad_hbm
        )
        near_mine = lax.ppermute(near_piece, group, near)
        far_mine = lax.ppermute(far_piece, group, far)
        other_grad = in_hbm(lax.ppermute(turn, "ctx", swap))
    else:
        state = local_state(keys, values)
        other_grad = []
        for k in range(1, n_ctx):
            start = lax.rem(c + k, n_ctx) * own_width
            turn = lax.dynamic_slice_in_dim(out_grad, start, own_width, 1)
            other_grad.append(shift(turn, "ctx", n_ctx, k, True))
        other_grad = jnp.concatenate(other_grad, 0)

    carried = total([shift(state, "ctx", n_ctx, k, False) for k in range(1, n_ctx)])
    rest = [shift(out_weight, "ctx", n_ctx, -k, True) for k in range(1, n_ctx)]
    rest = in_hbm(rest[0] if n_ctx == 2 else jnp.concatenate(rest, 1))
    attn, raw, prefix = forward(queries, keys, values, carried)

    if paired:
        attn_1 = lax.ppermute(attn, group, one)
        attn_2 = lax.ppermute(attn, group, two)
        near_z = lax.ppermute(near_mine, "rep", zpair)
        near_other = lax.ppermute(near_mine, "ctx", swap)
        raw = after(raw, near_mine, other_grad)

    draw, gsum, glocal = cotangent(scal, grad_hbm, weight_hbm, rest, queries, raw)
    suffix = total([shift(gsum, "ctx", n_ctx, -k, False) for k in range(1, n_ctx)])

    turn = after(attn, gsum)
    other_attn = [shift(turn, "ctx", n_ctx, k, True) for k in range(1, n_ctx)]
    other_attn = other_attn[0] if n_ctx == 2 else jnp.concatenate(other_attn, 0)

    if paired:
        far_z = lax.ppermute(after(far_mine, gsum), "rep", zpair)
        attn_3 = lax.ppermute(attn_1, group, two)
        suffix = after(suffix, far_mine, attn_1, near_other)

    query_grad, key_grad, value_grad = backward(queries, keys, values, draw, prefix, suffix, glocal)

    if paired:
        near_other_z = lax.ppermute(near_z, "ctx", swap)
        far_other = lax.ppermute(after(far_mine, query_grad), "ctx", swap)
        other_attn = after(other_attn, attn_2, near_z, query_grad)

    weight_grad = own_weight_grad(scal, attn, grad_hbm, other_attn, other_grad)

    if paired:
        far_other_z = lax.ppermute(far_z, "ctx", swap)

    if paired:
        near_out = project_near(
            scal, (after(attn, weight_grad, near_other_z, far_other), attn_1, attn_2), weight_hbm, rest,
            (near_mine, near_z, near_other, near_other_z),
        )
        layer_out = project_far(scal, near_out, attn_3, (far_mine, far_other, far_z, far_other_z))
    else:
        full = lax.all_gather(out_weight, "ctx", axis=1, tiled=True)
        partial_out = jnp.dot(attn, full, preferred_element_type=F32).astype(BF16)
        layer_out = lax.psum_scatter(partial_out, "head", scatter_dimension=1, tiled=True)
    return layer_out, query_grad, key_grad, value_grad, weight_grad


def solution(mesh):
    tokens = P(("rep", "ctx"), "head")
    sizes = mesh.shape["ctx"], mesh.shape["head"], mesh.shape["rep"]
    return jax.shard_map(
        functools.partial(body, *sizes),
        mesh=mesh,
        in_specs=(tokens, tokens, tokens, P("head", "ctx"), P(("rep", "ctx"), None)),
        out_specs=(tokens, tokens, tokens, tokens, P(("rep", "head"), "ctx")),
        check_vma=False,
    )
```

```python
import functools

import jax
import jax.numpy as jnp
from jax import lax
from jax.experimental import pallas as pl
from jax.experimental.pallas import tpu as pltpu
from jax.sharding import PartitionSpec as P

DH = 128
CHUNK = 256
EPS = 1e-06
F32 = jnp.float32
BF16 = jnp.bfloat16


def feature(x):
    return jnp.where(x > 0, x + 1.0, jnp.exp(jnp.minimum(x, 0.0)))


def dot_nn(a, b):
    return lax.dot_general(a, b, (((1,), (0,)), ((), ())), preferred_element_type=F32)


def dot_nt(a, b):
    return lax.dot_general(a, b, (((1,), (1,)), ((), ())), preferred_element_type=F32)


def dot_tn(a, b):
    return lax.dot_general(a, b, (((0,), (0,)), ((), ())), preferred_element_type=F32)


def shape_of(shape, dtype):
    return jax.ShapeDtypeStruct(shape, dtype)


def params(mib):
    return pltpu.CompilerParams(vmem_limit_bytes=mib * 1024 * 1024)


def cost(flops, moved):
    return pl.CostEstimate(flops=flops, transcendentals=0, bytes_accessed=moved)


def state_kernel(k_ref, v_ref, out_ref):
    for lo in range(0, k_ref.shape[1], DH):
        cols = slice(lo, lo + DH)
        fk = feature(k_ref[:, cols].astype(F32)).astype(BF16)
        out_ref[cols, :] = dot_tn(fk, v_ref[:, cols]).astype(BF16)


def local_state(keys, values):
    width = keys.shape[1]
    return pl.pallas_call(
        state_kernel,
        out_shape=shape_of((width, DH), BF16),
        compiler_params=params(16),
        cost_estimate=cost(2 * keys.size * DH, 4 * keys.size),
    )(keys, values)


def opening_kernel(s_ref, q_hbm, k_hbm, v_hbm, weight_hbm, grad_hbm,
                   state_ref, near_ref, far_ref, turn_ref, q_ref, k_ref, v_ref, sems, slice_sems):
    half, wide = near_ref.shape
    rows = pl.ds(pl.multiple_of(s_ref[3] * half, half), half)
    far_column = 1 - s_ref[2]
    near_column = jnp.where(s_ref[0] == s_ref[1], far_column, s_ref[2])
    loads = []
    for i, lo in enumerate(range(0, k_hbm.shape[1], DH)):
        cols = pl.ds(lo, DH)
        loads.append([
            pltpu.make_async_copy(k_hbm.at[:, cols], k_ref.at[:, cols], sems.at[0, i]),
            pltpu.make_async_copy(v_hbm.at[:, cols], v_ref.at[:, cols], sems.at[1, i]),
        ])
        loads[-1][0].start()
        loads[-1][1].start()
    moves = []
    for i, (column, ref) in enumerate([(near_column, near_ref), (far_column, far_ref)]):
        cols = pl.ds(pl.multiple_of(column * wide, wide), wide)
        moves.append(pltpu.make_async_copy(weight_hbm.at[rows, cols], ref, slice_sems.at[i]))
        moves[-1].start()
    moves.append(pltpu.make_async_copy(q_hbm, q_ref, slice_sems.at[2]))
    moves[-1].start()
    own = turn_ref.shape[1]
    cols = pl.ds(pl.multiple_of((1 - s_ref[0]) * own, own), own)
    moves.append(pltpu.make_async_copy(grad_hbm.at[:, cols], turn_ref, slice_sems.at[3]))
    moves[-1].start()
    for i, lo in enumerate(range(0, k_hbm.shape[1], DH)):
        cols = slice(lo, lo + DH)
        loads[i][0].wait()
        loads[i][1].wait()
        fk = feature(k_ref[:, cols].astype(F32)).astype(BF16)
        state_ref[cols, :] = dot_tn(fk, v_ref[:, cols]).astype(BF16)
    for move in moves:
        move.wait()


def opening(scal, queries, keys, values, weight, out_grad):
    tok, width = keys.shape
    piece = shape_of((weight.shape[0] // 2, weight.shape[1] // 2), BF16)
    hbm = pl.BlockSpec(memory_space=pltpu.HBM)
    vmem = pl.BlockSpec(memory_space=pltpu.VMEM)
    return pl.pallas_call(
        opening_kernel,
        out_shape=(shape_of((width, DH), BF16), piece, piece, shape_of((tok, weight.shape[1]), BF16))
        + (shape_of(keys.shape, BF16),) * 3,
        in_specs=[pl.BlockSpec(memory_space=pltpu.SMEM)] + [hbm] * 5,
        out_specs=(vmem,) * 7,
        scratch_shapes=[
            pltpu.SemaphoreType.DMA((2, width // DH)),
            pltpu.SemaphoreType.DMA((4,)),
        ],
        compiler_params=params(16),
        cost_estimate=cost(2 * keys.size * DH, 4 * keys.size),
    )(scal, queries, keys, values, weight, out_grad)


def forward_kernel(q_ref, k_ref, v_ref, carried_ref, attn_ref, raw_ref, prefix_ref):
    tok, width = q_ref.shape
    chunk = min(CHUNK, tok)
    row = lax.broadcasted_iota(jnp.int32, (chunk, chunk), 0)
    col = lax.broadcasted_iota(jnp.int32, (chunk, chunk), 1)
    lower = row >= col
    for lo in range(0, width, DH):
        cols = slice(lo, lo + DH)
        prefix = carried_ref[cols, :].astype(F32)
        for i in range(tok // chunk):
            rows = slice(i * chunk, (i + 1) * chunk)
            fq = feature(q_ref[rows, cols].astype(F32)).astype(BF16)
            fk = feature(k_ref[rows, cols].astype(F32)).astype(BF16)
            v = v_ref[rows, cols]
            low_prefix = prefix.astype(BF16)
            prefix_ref[i, cols, :] = low_prefix
            scores = jnp.where(lower, dot_nt(fq, fk), 0.0).astype(BF16)
            raw = dot_nn(scores, v) + dot_nn(fq, low_prefix)
            raw_ref[rows, cols] = raw
            inv = lax.rsqrt(jnp.mean(raw * raw, axis=-1, keepdims=True) + EPS)
            attn_ref[rows, cols] = (raw * inv).astype(BF16)
            if i + 1 < tok // chunk:
                prefix = prefix + dot_tn(fk, v)


def forward(queries, keys, values, carried):
    tok, width = queries.shape
    chunks = tok // min(CHUNK, tok)
    return pl.pallas_call(
        forward_kernel,
        out_shape=(
            shape_of((tok, width), BF16),
            shape_of((tok, width), F32),
            shape_of((chunks, width, DH), BF16),
        ),
        compiler_params=params(16),
        cost_estimate=cost(16 * queries.size * DH, 12 * queries.size),
    )(queries, keys, values, carried)


def cotangent_kernel(s_ref, grad_ref, own_ref, rest_ref, q_ref, raw_ref,
                     draw_ref, gsum_ref, glocal_ref, acc_ref):
    own_width, rest_width = own_ref.shape[1], rest_ref.shape[1]
    if own_width == rest_width:
        own = pl.ds(pl.multiple_of(s_ref[0] * own_width, own_width), own_width)
        rest = pl.ds(pl.multiple_of((1 - s_ref[0]) * own_width, own_width), own_width)
        acc_ref[...] = dot_nt(grad_ref[:, own], own_ref[...])
        acc_ref[...] += dot_nt(grad_ref[:, rest], rest_ref[...])
    else:
        count = (own_width + rest_width) // own_width
        acc_ref[...] = jnp.zeros_like(acc_ref)
        for k in range(count):
            place = lax.rem(s_ref[0] + k, count) * own_width
            part = grad_ref[:, pl.ds(pl.multiple_of(place, own_width), own_width)]
            weight = own_ref[...] if k == 0 else rest_ref[:, (k - 1) * own_width : k * own_width]
            acc_ref[...] += dot_nt(part, weight)
    tok, width = q_ref.shape
    chunk = min(CHUNK, tok)
    for lo in range(0, width, DH):
        cols = slice(lo, lo + DH)
        later = jnp.zeros((DH, DH), F32)
        for i in reversed(range(tok // chunk)):
            rows = slice(i * chunk, (i + 1) * chunk)
            glocal_ref[i, cols, :] = later
            grad = acc_ref[rows, cols].astype(BF16).astype(F32)
            raw = raw_ref[rows, cols]
            inv = lax.rsqrt(jnp.mean(raw * raw, axis=-1, keepdims=True) + EPS)
            normed = raw * inv
            mean = jnp.mean(grad * normed, axis=-1, keepdims=True)
            draw = (inv * (grad - normed * mean)).astype(BF16)
            draw_ref[rows, cols] = draw
            fq = feature(q_ref[rows, cols].astype(F32)).astype(BF16)
            later = later + dot_tn(fq, draw)
        gsum_ref[cols, :] = later.astype(BF16)


def smem_then_vmem(count):
    return [pl.BlockSpec(memory_space=pltpu.SMEM)] + [pl.BlockSpec(memory_space=pltpu.VMEM)] * count


def cotangent(scal, out_grad, own, rest, queries, raw):
    tok, width = queries.shape
    chunks = tok // min(CHUNK, tok)
    return pl.pallas_call(
        cotangent_kernel,
        out_shape=(
            shape_of((tok, width), BF16),
            shape_of((width, DH), BF16),
            shape_of((chunks, width, DH), F32),
        ),
        in_specs=smem_then_vmem(5),
        scratch_shapes=[pltpu.VMEM((tok, width), F32)],
        compiler_params=params(16),
        cost_estimate=cost(2 * out_grad.size * width, 4 * out_grad.size),
    )(scal, out_grad, own, rest, queries, raw)


def weight_grad_kernel(s_ref, attn_ref, grad_ref, other_attn_ref, other_grad_ref, out_ref):
    tok = attn_ref.shape[0]
    block = out_ref.shape[1]
    step = pl.program_id(0)
    place = s_ref[0] * other_grad_ref.shape[1] + step * block
    part = grad_ref[:, pl.ds(pl.multiple_of(place, block), block)]
    acc = dot_tn(attn_ref[...], part).astype(BF16).astype(F32)
    here = pl.ds(pl.multiple_of(step * block, block), block)
    for lo in range(0, other_attn_ref.shape[0], tok):
        rows = slice(lo, lo + tok)
        acc += dot_tn(other_attn_ref[rows, :], other_grad_ref[rows, here]).astype(BF16).astype(F32)
    out_ref[...] = acc


def own_weight_grad(scal, attn, out_grad, other_attn, other_grad):
    width = attn.shape[1]
    own_width = other_grad.shape[1]
    block = min(512, own_width)
    return pl.pallas_call(
        weight_grad_kernel,
        out_shape=shape_of((width, own_width), F32),
        grid=(own_width // block,),
        in_specs=smem_then_vmem(4),
        out_specs=pl.BlockSpec((width, block), lambda j: (0, j)),
        compiler_params=params(24),
        cost_estimate=cost(2 * out_grad.size * width, 4 * out_grad.size),
    )(scal, attn, out_grad, other_attn, other_grad)


def backward_kernel(q_ref, k_ref, v_ref, draw_ref, prefix_ref, suffix_ref, glocal_ref,
                    dq_ref, dk_ref, dv_ref):
    tok, width = q_ref.shape
    chunk = min(CHUNK, tok)
    row = lax.broadcasted_iota(jnp.int32, (chunk, chunk), 0)
    col = lax.broadcasted_iota(jnp.int32, (chunk, chunk), 1)
    lower = row >= col
    upper = row <= col
    for lo in range(0, width, DH):
        cols = slice(lo, lo + DH)
        suffix = suffix_ref[cols, :].astype(F32)
        for i in range(tok // chunk):
            rows = slice(i * chunk, (i + 1) * chunk)
            q = q_ref[rows, cols].astype(F32)
            k = k_ref[rows, cols].astype(F32)
            q_slope = jnp.exp(jnp.minimum(q, 0.0))
            k_slope = jnp.exp(jnp.minimum(k, 0.0))
            fq = jnp.where(q > 0, q + 1.0, q_slope).astype(BF16)
            fk = jnp.where(k > 0, k + 1.0, k_slope).astype(BF16)
            v = v_ref[rows, cols]
            draw = draw_ref[rows, cols]
            later = (suffix + glocal_ref[i, cols, :]).astype(BF16)
            dscores = jnp.where(lower, dot_nt(draw, v), 0.0).astype(BF16)
            dfq = dot_nn(dscores, fk) + dot_nt(draw, prefix_ref[i, cols, :])
            dq_ref[rows, cols] = (dfq * q_slope).astype(BF16)
            dscores_t = jnp.where(upper, dot_nt(v, draw), 0.0).astype(BF16)
            dfk = dot_nn(dscores_t, fq) + dot_nt(v, later)
            dk_ref[rows, cols] = (dfk * k_slope).astype(BF16)
            scores_t = jnp.where(upper, dot_nt(fk, fq), 0.0).astype(BF16)
            dv = dot_nn(scores_t, draw) + dot_nn(fk, later)
            dv_ref[rows, cols] = dv.astype(BF16)


def backward(queries, keys, values, draw, prefix, suffix, glocal):
    out = shape_of(queries.shape, BF16)
    return pl.pallas_call(
        backward_kernel, out_shape=(out, out, out), compiler_params=params(16),
        cost_estimate=cost(32 * queries.size * DH, 16 * queries.size),
    )(queries, keys, values, draw, prefix, suffix, glocal)


def halves(s_ref, half):
    first = pl.ds(pl.multiple_of(s_ref[3] * half, half), half)
    second = pl.ds(pl.multiple_of((1 - s_ref[3]) * half, half), half)
    return first, second


def project_near_kernel(s_ref, a_ref, a1_ref, a2_ref, own_ref, rest_ref,
                        m1_ref, z1_ref, o1_ref, oz1_ref, out_ref):
    first, second = halves(s_ref, m1_ref.shape[0])
    wide = out_ref.shape[1]
    local = pl.ds(pl.multiple_of(s_ref[2] * wide, wide), wide)
    mine = s_ref[0] == s_ref[1]

    @pl.when(mine)
    def _():
        out_ref[...] = dot_nn(a_ref[...], own_ref[:, local])

    @pl.when(jnp.logical_not(mine))
    def _():
        out_ref[...] = dot_nn(a_ref[...], rest_ref[:, local])

    acc = dot_nn(a1_ref[:, first], m1_ref[...])
    acc += dot_nn(a1_ref[:, second], z1_ref[...])
    acc += dot_nn(a2_ref[:, first], o1_ref[...])
    acc += dot_nn(a2_ref[:, second], oz1_ref[...])
    out_ref[...] += acc


def project_near(scal, attns, own, rest, pieces):
    tok, width = attns[0].shape
    out_width = pieces[0].shape[1]
    return pl.pallas_call(
        project_near_kernel,
        out_shape=shape_of((tok, out_width), F32),
        in_specs=smem_then_vmem(9),
        compiler_params=params(16),
        cost_estimate=cost(6 * tok * width * out_width, 8 * width * out_width),
    )(scal, *attns, own, rest, *pieces)


def project_far_kernel(s_ref, near_ref, a_ref, d_ref, od_ref, dz_ref, odz_ref, out_ref):
    first, second = halves(s_ref, d_ref.shape[0])
    block = out_ref.shape[1]
    here = pl.ds(pl.multiple_of(pl.program_id(0) * block, block), block)
    acc = near_ref[:, here] + dot_nn(a_ref[:, first], d_ref[:, here] + od_ref[:, here])
    acc += dot_nn(a_ref[:, second], dz_ref[:, here] + odz_ref[:, here])
    out_ref[...] = acc.astype(BF16)


def project_far(scal, near, attn, pieces):
    tok, width = attn.shape
    out_width = pieces[0].shape[1]
    block = 512
    return pl.pallas_call(
        project_far_kernel,
        out_shape=shape_of((tok, out_width), BF16),
        grid=(out_width // block,),
        in_specs=smem_then_vmem(6),
        out_specs=pl.BlockSpec((tok, block), lambda j: (0, j)),
        compiler_params=params(16),
        cost_estimate=cost(2 * tok * width * out_width, 8 * width * out_width),
    )(scal, near, attn, *pieces)


def in_hbm(array):
    return pltpu.with_memory_space_constraint(array, pltpu.HBM)


def after(array, *needed):
    return lax.optimization_barrier((array, *needed))[0]


def shift(array, axis, count, by, wrap):
    pairs = [(i, (i + by) % count) for i in range(count) if wrap or 0 <= i + by < count]
    return lax.ppermute(array, axis, pairs)


def total(arrays):
    if len(arrays) == 1:
        return arrays[0]
    return functools.reduce(jnp.add, [a.astype(F32) for a in arrays])


def body(n_ctx, n_head, n_rep, queries, keys, values, out_weight, out_grad):
    c, h, z = lax.axis_index("ctx"), lax.axis_index("head"), lax.axis_index("rep")
    x, y, p = h & 1, h >> 1, z & 1
    scal = jnp.stack([c, y, x, p]).astype(jnp.int32)
    paired = n_ctx == 2 and n_head == 4 and n_rep % 2 == 0
    own_width = out_weight.shape[1]
    weight_hbm, grad_hbm = in_hbm(out_weight), in_hbm(out_grad)

    if paired:
        group = ("ctx", "head")
        near = [(4 * (i // 2) + i, i ^ 1) for i in range(4)]
        near += [(4 * (1 - i // 2) + i, 4 + (i ^ 2)) for i in range(4)]
        far = [(4 * (1 - i // 2) + i, i ^ 3) for i in range(4)]
        one = [(i, i ^ 1) for i in range(4)] + [(4 + i, 4 + (i ^ 2)) for i in range(4)]
        two = [(i, i ^ 2) for i in range(4)] + [(4 + i, 4 + (i ^ 1)) for i in range(4)]
        zpair = [(i, i ^ 1) for i in range(n_rep)]
        swap = [(0, 1), (1, 0)]
        state, near_piece, far_piece, turn, queries, keys, values = opening(
            scal, in_hbm(queries), in_hbm(keys), in_hbm(values), weight_hbm, grad_hbm
        )
        near_mine = lax.ppermute(near_piece, group, near)
        far_mine = lax.ppermute(far_piece, group, far)
        other_grad = lax.ppermute(turn, "ctx", swap)
    else:
        state = local_state(keys, values)
        other_grad = []
        for k in range(1, n_ctx):
            start = lax.rem(c + k, n_ctx) * own_width
            turn = lax.dynamic_slice_in_dim(out_grad, start, own_width, 1)
            other_grad.append(shift(turn, "ctx", n_ctx, k, True))
        other_grad = jnp.concatenate(other_grad, 0)

    carried = total([shift(state, "ctx", n_ctx, k, False) for k in range(1, n_ctx)])
    rest = [shift(out_weight, "ctx", n_ctx, -k, True) for k in range(1, n_ctx)]
    rest = rest[0] if n_ctx == 2 else jnp.concatenate(rest, 1)
    attn, raw, prefix = forward(queries, keys, values, carried)

    other_attn = [shift(attn, "ctx", n_ctx, k, True) for k in range(1, n_ctx)]
    other_attn = other_attn[0] if n_ctx == 2 else jnp.concatenate(other_attn, 0)
    if paired:
        attn_1 = lax.ppermute(attn, group, one)
        attn_2 = lax.ppermute(attn, group, two)
        near_z = lax.ppermute(near_mine, "rep", zpair)
        raw = after(raw, near_mine, rest, other_grad)

    draw, gsum, glocal = cotangent(scal, out_grad, out_weight, rest, queries, raw)
    suffix = total([shift(gsum, "ctx", n_ctx, -k, False) for k in range(1, n_ctx)])

    if paired:
        far_z = lax.ppermute(after(far_mine, gsum), "rep", zpair)
        other_attn = after(other_attn, gsum, far_mine)

    weight_grad = own_weight_grad(scal, attn, out_grad, other_attn, other_grad)

    if paired:
        near_other = lax.ppermute(after(near_mine, weight_grad), "ctx", swap)
        suffix = after(suffix, weight_grad)

    query_grad, key_grad, value_grad = backward(queries, keys, values, draw, prefix, suffix, glocal)

    if paired:
        attn_3 = lax.ppermute(after(attn_1, query_grad), group, two)
        near_other_z = lax.ppermute(after(near_z, weight_grad), "ctx", swap)
        far_other = lax.ppermute(after(far_mine, weight_grad), "ctx", swap)
        far_other_z = lax.ppermute(after(far_z, query_grad), "ctx", swap)

    if paired:
        near_out = project_near(
            scal, (after(attn, query_grad), attn_1, attn_2), out_weight, rest,
            (near_mine, near_z, near_other, near_other_z),
        )
        layer_out = project_far(scal, near_out, attn_3, (far_mine, far_other, far_z, far_other_z))
    else:
        full = lax.all_gather(out_weight, "ctx", axis=1, tiled=True)
        partial_out = jnp.dot(attn, full, preferred_element_type=F32).astype(BF16)
        layer_out = lax.psum_scatter(partial_out, "head", scatter_dimension=1, tiled=True)
    return layer_out, query_grad, key_grad, value_grad, weight_grad


def solution(mesh):
    tokens = P(("rep", "ctx"), "head")
    sizes = mesh.shape["ctx"], mesh.shape["head"], mesh.shape["rep"]
    return jax.shard_map(
        functools.partial(body, *sizes),
        mesh=mesh,
        in_specs=(tokens, tokens, tokens, P("head", "ctx"), P(("rep", "ctx"), None)),
        out_specs=(tokens, tokens, tokens, tokens, P(("rep", "head"), "ctx")),
        check_vma=False,
    )
```

```python
import functools

import jax
import jax.numpy as jnp
from jax import lax
from jax.experimental import pallas as pl
from jax.experimental.pallas import tpu as pltpu
from jax.sharding import PartitionSpec as P

DH = 128
CHUNK = 256
EPS = 1e-06
F32 = jnp.float32
BF16 = jnp.bfloat16


def feature(x):
    return jnp.where(x > 0, x + 1.0, jnp.exp(jnp.minimum(x, 0.0)))


def dot_nn(a, b):
    return lax.dot_general(a, b, (((1,), (0,)), ((), ())), preferred_element_type=F32)


def dot_nt(a, b):
    return lax.dot_general(a, b, (((1,), (1,)), ((), ())), preferred_element_type=F32)


def dot_tn(a, b):
    return lax.dot_general(a, b, (((0,), (0,)), ((), ())), preferred_element_type=F32)


def shape_of(shape, dtype):
    return jax.ShapeDtypeStruct(shape, dtype)


def params(mib):
    return pltpu.CompilerParams(vmem_limit_bytes=mib * 1024 * 1024)


def cost(flops, moved):
    return pl.CostEstimate(flops=flops, transcendentals=0, bytes_accessed=moved)


def state_kernel(k_ref, v_ref, out_ref):
    for lo in range(0, k_ref.shape[1], DH):
        cols = slice(lo, lo + DH)
        fk = feature(k_ref[:, cols].astype(F32)).astype(BF16)
        out_ref[cols, :] = dot_tn(fk, v_ref[:, cols]).astype(BF16)


def local_state(keys, values):
    width = keys.shape[1]
    return pl.pallas_call(
        state_kernel,
        out_shape=shape_of((width, DH), BF16),
        compiler_params=params(16),
        cost_estimate=cost(2 * keys.size * DH, 4 * keys.size),
    )(keys, values)


def opening_kernel(s_ref, q_hbm, k_hbm, v_hbm, weight_hbm, grad_hbm,
                   state_ref, near_ref, far_ref, turn_ref, q_ref, k_ref, v_ref, sems, slice_sems):
    half, wide = near_ref.shape
    rows = pl.ds(pl.multiple_of(s_ref[3] * half, half), half)
    far_column = 1 - s_ref[2]
    near_column = jnp.where(s_ref[0] == s_ref[1], far_column, s_ref[2])
    loads = []
    for i, lo in enumerate(range(0, k_hbm.shape[1], DH)):
        cols = pl.ds(lo, DH)
        loads.append([
            pltpu.make_async_copy(k_hbm.at[:, cols], k_ref.at[:, cols], sems.at[0, i]),
            pltpu.make_async_copy(v_hbm.at[:, cols], v_ref.at[:, cols], sems.at[1, i]),
        ])
        loads[-1][0].start()
        loads[-1][1].start()
    moves = []
    for i, (column, ref) in enumerate([(near_column, near_ref), (far_column, far_ref)]):
        cols = pl.ds(pl.multiple_of(column * wide, wide), wide)
        moves.append(pltpu.make_async_copy(weight_hbm.at[rows, cols], ref, slice_sems.at[i]))
        moves[-1].start()
    moves.append(pltpu.make_async_copy(q_hbm, q_ref, slice_sems.at[2]))
    moves[-1].start()
    own = turn_ref.shape[1]
    cols = pl.ds(pl.multiple_of((1 - s_ref[0]) * own, own), own)
    moves.append(pltpu.make_async_copy(grad_hbm.at[:, cols], turn_ref, slice_sems.at[3]))
    moves[-1].start()
    for i, lo in enumerate(range(0, k_hbm.shape[1], DH)):
        cols = slice(lo, lo + DH)
        loads[i][0].wait()
        loads[i][1].wait()
        fk = feature(k_ref[:, cols].astype(F32)).astype(BF16)
        state_ref[cols, :] = dot_tn(fk, v_ref[:, cols]).astype(BF16)
    for move in moves:
        move.wait()


def opening(scal, queries, keys, values, weight, out_grad):
    tok, width = keys.shape
    piece = shape_of((weight.shape[0] // 2, weight.shape[1] // 2), BF16)
    hbm = pl.BlockSpec(memory_space=pltpu.HBM)
    vmem = pl.BlockSpec(memory_space=pltpu.VMEM)
    return pl.pallas_call(
        opening_kernel,
        out_shape=(shape_of((width, DH), BF16), piece, piece, shape_of((tok, weight.shape[1]), BF16))
        + (shape_of(keys.shape, BF16),) * 3,
        in_specs=[pl.BlockSpec(memory_space=pltpu.SMEM)] + [hbm] * 5,
        out_specs=(vmem,) * 7,
        scratch_shapes=[
            pltpu.SemaphoreType.DMA((2, width // DH)),
            pltpu.SemaphoreType.DMA((4,)),
        ],
        compiler_params=params(16),
        cost_estimate=cost(2 * keys.size * DH, 4 * keys.size),
    )(scal, queries, keys, values, weight, out_grad)


def forward_kernel(q_ref, k_ref, v_ref, carried_ref, attn_ref, raw_ref, prefix_ref):
    tok, width = q_ref.shape
    chunk = min(CHUNK, tok)
    row = lax.broadcasted_iota(jnp.int32, (chunk, chunk), 0)
    col = lax.broadcasted_iota(jnp.int32, (chunk, chunk), 1)
    lower = row >= col
    for lo in range(0, width, DH):
        cols = slice(lo, lo + DH)
        prefix = carried_ref[cols, :].astype(F32)
        for i in range(tok // chunk):
            rows = slice(i * chunk, (i + 1) * chunk)
            fq = feature(q_ref[rows, cols].astype(F32)).astype(BF16)
            fk = feature(k_ref[rows, cols].astype(F32)).astype(BF16)
            v = v_ref[rows, cols]
            low_prefix = prefix.astype(BF16)
            prefix_ref[i, cols, :] = low_prefix
            scores = jnp.where(lower, dot_nt(fq, fk), 0.0).astype(BF16)
            raw = dot_nn(scores, v) + dot_nn(fq, low_prefix)
            raw_ref[rows, cols] = raw
            inv = lax.rsqrt(jnp.mean(raw * raw, axis=-1, keepdims=True) + EPS)
            attn_ref[rows, cols] = (raw * inv).astype(BF16)
            if i + 1 < tok // chunk:
                prefix = prefix + dot_tn(fk, v)


def forward(queries, keys, values, carried):
    tok, width = queries.shape
    chunks = tok // min(CHUNK, tok)
    return pl.pallas_call(
        forward_kernel,
        out_shape=(
            shape_of((tok, width), BF16),
            shape_of((tok, width), F32),
            shape_of((chunks, width, DH), BF16),
        ),
        compiler_params=params(16),
        cost_estimate=cost(16 * queries.size * DH, 12 * queries.size),
    )(queries, keys, values, carried)


def cotangent_kernel(s_ref, grad_ref, own_ref, rest_ref, q_ref, raw_ref, draw_ref, gsum_ref, glocal_ref):
    own_width, rest_width = own_ref.shape[1], rest_ref.shape[1]
    count = (own_width + rest_width) // own_width
    tok, width = q_ref.shape
    chunk = min(CHUNK, tok)
    for top in range(0, width, 2 * DH):
        pair = slice(top, top + 2 * DH)
        total_grad = None
        for k in range(count):
            place = lax.rem(s_ref[0] + k, count) * own_width
            part = grad_ref[:, pl.ds(pl.multiple_of(place, own_width), own_width)]
            if k == 0:
                weight = own_ref[pair, :]
            else:
                weight = rest_ref[pair, (k - 1) * own_width : k * own_width]
            product = dot_nt(part, weight)
            total_grad = product if total_grad is None else total_grad + product
        for lo in (top, top + DH):
            cols = slice(lo, lo + DH)
            later = jnp.zeros((DH, DH), F32)
            for i in reversed(range(tok // chunk)):
                rows = slice(i * chunk, (i + 1) * chunk)
                glocal_ref[i, cols, :] = later
                grad = total_grad[rows, lo - top : lo - top + DH].astype(BF16).astype(F32)
                raw = raw_ref[rows, cols]
                inv = lax.rsqrt(jnp.mean(raw * raw, axis=-1, keepdims=True) + EPS)
                normed = raw * inv
                mean = jnp.mean(grad * normed, axis=-1, keepdims=True)
                draw = (inv * (grad - normed * mean)).astype(BF16)
                draw_ref[rows, cols] = draw
                fq = feature(q_ref[rows, cols].astype(F32)).astype(BF16)
                later = later + dot_tn(fq, draw)
            gsum_ref[cols, :] = later.astype(BF16)


def smem_then_vmem(count):
    return [pl.BlockSpec(memory_space=pltpu.SMEM)] + [pl.BlockSpec(memory_space=pltpu.VMEM)] * count


def cotangent(scal, out_grad, own, rest, queries, raw):
    tok, width = queries.shape
    chunks = tok // min(CHUNK, tok)
    return pl.pallas_call(
        cotangent_kernel,
        out_shape=(
            shape_of((tok, width), BF16),
            shape_of((width, DH), BF16),
            shape_of((chunks, width, DH), F32),
        ),
        in_specs=smem_then_vmem(5),
        compiler_params=params(16),
        cost_estimate=cost(2 * out_grad.size * width, 4 * out_grad.size),
    )(scal, out_grad, own, rest, queries, raw)


def weight_grad_kernel(s_ref, attn_ref, grad_ref, other_ref, other_grad_ref, out_hbm, out_buf, sems):
    tok, width = attn_ref.shape
    blocks, _, block = out_buf.shape
    attn_t = attn_ref[...].T
    others_t = [other_ref[lo : lo + tok, :].T for lo in range(0, other_ref.shape[0], tok)]
    moves = []
    for j in range(blocks):
        here = slice(j * block, (j + 1) * block)
        place = s_ref[0] * (blocks * block) + j * block
        part = grad_ref[:, pl.ds(pl.multiple_of(place, block), block)]
        acc = dot_nn(attn_t, part).astype(BF16).astype(F32)
        for k, other_t in enumerate(others_t):
            part = other_grad_ref[k * tok : (k + 1) * tok, here]
            acc += dot_nn(other_t, part).astype(BF16).astype(F32)
        out_buf[j] = acc
        moves.append(pltpu.make_async_copy(out_buf.at[j], out_hbm.at[:, here], sems.at[j]))
        moves[-1].start()
    for move in moves:
        move.wait()


def own_weight_grad(scal, attn, out_grad, other, other_grad):
    width = attn.shape[1]
    own_width = other_grad.shape[1]
    block = min(256, own_width)
    return pl.pallas_call(
        weight_grad_kernel,
        out_shape=shape_of((width, own_width), F32),
        in_specs=smem_then_vmem(4),
        out_specs=pl.BlockSpec(memory_space=pl.ANY),
        scratch_shapes=[
            pltpu.VMEM((own_width // block, width, block), F32),
            pltpu.SemaphoreType.DMA((own_width // block,)),
        ],
        compiler_params=params(16),
        cost_estimate=cost(2 * out_grad.size * width, 4 * out_grad.size),
    )(scal, attn, out_grad, other, other_grad)


def backward_kernel(q_ref, k_ref, v_ref, draw_ref, prefix_ref, suffix_ref, glocal_ref,
                    dq_ref, dk_ref, dv_ref):
    tok, width = q_ref.shape
    chunk = min(CHUNK, tok)
    row = lax.broadcasted_iota(jnp.int32, (chunk, chunk), 0)
    col = lax.broadcasted_iota(jnp.int32, (chunk, chunk), 1)
    lower = row >= col
    upper = row <= col
    for lo in range(0, width, DH):
        cols = slice(lo, lo + DH)
        suffix = suffix_ref[cols, :].astype(F32)
        for i in range(tok // chunk):
            rows = slice(i * chunk, (i + 1) * chunk)
            q = q_ref[rows, cols].astype(F32)
            k = k_ref[rows, cols].astype(F32)
            q_slope = jnp.exp(jnp.minimum(q, 0.0))
            k_slope = jnp.exp(jnp.minimum(k, 0.0))
            fq = jnp.where(q > 0, q + 1.0, q_slope).astype(BF16)
            fk = jnp.where(k > 0, k + 1.0, k_slope).astype(BF16)
            v = v_ref[rows, cols]
            draw = draw_ref[rows, cols]
            later = (suffix + glocal_ref[i, cols, :]).astype(BF16)
            dscores = jnp.where(lower, dot_nt(draw, v), 0.0).astype(BF16)
            dfq = dot_nn(dscores, fk) + dot_nt(draw, prefix_ref[i, cols, :])
            dq_ref[rows, cols] = (dfq * q_slope).astype(BF16)
            dscores_t = jnp.where(upper, dot_nt(v, draw), 0.0).astype(BF16)
            dfk = dot_nn(dscores_t, fq) + dot_nt(v, later)
            dk_ref[rows, cols] = (dfk * k_slope).astype(BF16)
            scores_t = jnp.where(upper, dot_nt(fk, fq), 0.0).astype(BF16)
            dv = dot_nn(scores_t, draw) + dot_nn(fk, later)
            dv_ref[rows, cols] = dv.astype(BF16)


def backward(queries, keys, values, draw, prefix, suffix, glocal):
    out = shape_of(queries.shape, BF16)
    return pl.pallas_call(
        backward_kernel,
        out_shape=(out, out, out),
        compiler_params=params(16),
        cost_estimate=cost(32 * queries.size * DH, 16 * queries.size),
    )(queries, keys, values, draw, prefix, suffix, glocal)


def halves(s_ref, half):
    first = pl.ds(pl.multiple_of(s_ref[3] * half, half), half)
    second = pl.ds(pl.multiple_of((1 - s_ref[3]) * half, half), half)
    return first, second


def project_own_kernel(s_ref, a_ref, own_ref, rest_ref, out_ref):
    wide = out_ref.shape[1]
    local = pl.ds(pl.multiple_of(s_ref[2] * wide, wide), wide)
    mine = s_ref[0] == s_ref[1]

    @pl.when(mine)
    def _():
        out_ref[...] = dot_nn(a_ref[...], own_ref[:, local])

    @pl.when(jnp.logical_not(mine))
    def _():
        out_ref[...] = dot_nn(a_ref[...], rest_ref[:, local])


def project_own(scal, attn, own, rest, out_width):
    tok, width = attn.shape
    return pl.pallas_call(
        project_own_kernel,
        out_shape=shape_of((tok, out_width), F32),
        in_specs=smem_then_vmem(3),
        compiler_params=params(16),
        cost_estimate=cost(2 * tok * width * out_width, 8 * width * out_width),
    )(scal, attn, own, rest)


def project_near_kernel(s_ref, out_so_far_ref, a1_ref, a2_ref, m1_ref, z1_ref, o1_ref, oz1_ref, out_ref):
    first, second = halves(s_ref, m1_ref.shape[0])
    acc = out_so_far_ref[...] + dot_nn(a1_ref[:, first], m1_ref[...])
    acc += dot_nn(a1_ref[:, second], z1_ref[...])
    acc += dot_nn(a2_ref[:, first], o1_ref[...])
    acc += dot_nn(a2_ref[:, second], oz1_ref[...])
    out_ref[...] = acc


def project_near(scal, out_so_far, attns, pieces):
    tok, width = attns[0].shape
    out_width = pieces[0].shape[1]
    return pl.pallas_call(
        project_near_kernel,
        out_shape=shape_of((tok, out_width), F32),
        in_specs=smem_then_vmem(7),
        compiler_params=params(16),
        cost_estimate=cost(4 * tok * width * out_width, 8 * width * out_width),
    )(scal, out_so_far, *attns, *pieces)


def project_far_kernel(s_ref, near_ref, a_ref, d_ref, od_ref, dz_ref, odz_ref, out_hbm, out_buf, sems):
    first, second = halves(s_ref, d_ref.shape[0])
    blocks, _, block = out_buf.shape
    moves = []
    for j in range(blocks):
        here = slice(j * block, (j + 1) * block)
        acc = near_ref[:, here] + dot_nn(a_ref[:, first], d_ref[:, here] + od_ref[:, here])
        acc += dot_nn(a_ref[:, second], dz_ref[:, here] + odz_ref[:, here])
        out_buf[j] = acc.astype(BF16)
        moves.append(pltpu.make_async_copy(out_buf.at[j], out_hbm.at[:, here], sems.at[j]))
        moves[-1].start()
    for move in moves:
        move.wait()


def project_far(scal, near, attn, pieces):
    tok, width = attn.shape
    out_width = pieces[0].shape[1]
    block = 256
    return pl.pallas_call(
        project_far_kernel,
        out_shape=shape_of((tok, out_width), BF16),
        in_specs=smem_then_vmem(6),
        out_specs=pl.BlockSpec(memory_space=pl.ANY),
        scratch_shapes=[
            pltpu.VMEM((out_width // block, tok, block), BF16),
            pltpu.SemaphoreType.DMA((out_width // block,)),
        ],
        compiler_params=params(16),
        cost_estimate=cost(2 * tok * width * out_width, 8 * width * out_width),
    )(scal, near, attn, *pieces)


def in_hbm(array):
    return pltpu.with_memory_space_constraint(array, pltpu.HBM)


def after(array, *needed):
    return lax.optimization_barrier((array, *needed))[0]


def shift(array, axis, count, by, wrap):
    pairs = [(i, (i + by) % count) for i in range(count) if wrap or 0 <= i + by < count]
    return lax.ppermute(array, axis, pairs)


def total(arrays):
    if len(arrays) == 1:
        return arrays[0]
    return functools.reduce(jnp.add, [a.astype(F32) for a in arrays])


def body(n_ctx, n_head, n_rep, queries, keys, values, out_weight, out_grad):
    c, h, z = lax.axis_index("ctx"), lax.axis_index("head"), lax.axis_index("rep")
    x, y, p = h & 1, h >> 1, z & 1
    scal = jnp.stack([c, y, x, p]).astype(jnp.int32)
    paired = n_ctx == 2 and n_head == 4 and n_rep % 2 == 0
    own_width = out_weight.shape[1]
    weight_hbm, grad_hbm = in_hbm(out_weight), in_hbm(out_grad)

    if paired:
        group = ("ctx", "head")
        near = [(4 * (i // 2) + i, i ^ 1) for i in range(4)]
        near += [(4 * (1 - i // 2) + i, 4 + (i ^ 2)) for i in range(4)]
        far = [(4 * (1 - i // 2) + i, i ^ 3) for i in range(4)]
        one = [(i, i ^ 1) for i in range(4)] + [(4 + i, 4 + (i ^ 2)) for i in range(4)]
        two = [(i, i ^ 2) for i in range(4)] + [(4 + i, 4 + (i ^ 1)) for i in range(4)]
        zpair = [(i, i ^ 1) for i in range(n_rep)]
        swap = [(0, 1), (1, 0)]
        state, near_piece, far_piece, turn, queries, keys, values = opening(
            scal, in_hbm(queries), in_hbm(keys), in_hbm(values), weight_hbm, grad_hbm
        )
        near_mine = lax.ppermute(near_piece, group, near)
        far_mine = lax.ppermute(far_piece, group, far)
        other_grad = lax.ppermute(turn, "ctx", swap)
    else:
        state = local_state(keys, values)
        other_grad = []
        for k in range(1, n_ctx):
            start = lax.rem(c + k, n_ctx) * own_width
            turn = lax.dynamic_slice_in_dim(out_grad, start, own_width, 1)
            other_grad.append(shift(turn, "ctx", n_ctx, k, True))
        other_grad = jnp.concatenate(other_grad, 0)

    carried = total([shift(state, "ctx", n_ctx, k, False) for k in range(1, n_ctx)])
    rest = [shift(out_weight, "ctx", n_ctx, -k, True) for k in range(1, n_ctx)]
    rest = rest[0] if n_ctx == 2 else jnp.concatenate(rest, 1)
    attn, raw, prefix = forward(queries, keys, values, carried)

    other_attn = [shift(attn, "ctx", n_ctx, k, True) for k in range(1, n_ctx)]
    other_attn = other_attn[0] if n_ctx == 2 else jnp.concatenate(other_attn, 0)
    if paired:
        attn_1 = lax.ppermute(attn, group, one)
        attn_2 = lax.ppermute(attn, group, two)
        near_z = lax.ppermute(near_mine, "rep", zpair)
        raw = after(raw, near_mine, rest, other_grad)

    draw, gsum, glocal = cotangent(scal, out_grad, out_weight, rest, queries, raw)
    suffix = total([shift(gsum, "ctx", n_ctx, -k, False) for k in range(1, n_ctx)])

    if paired:
        far_z = lax.ppermute(after(far_mine, gsum), "rep", zpair)
        own_out = project_own(scal, after(attn, gsum), out_weight, rest, out_weight.shape[1] // 2)
        other_attn = after(other_attn, own_out, far_mine)

    weight_grad = own_weight_grad(scal, attn, out_grad, other_attn, other_grad)

    if paired:
        near_other = lax.ppermute(after(near_mine, weight_grad), "ctx", swap)
        attn_3 = lax.ppermute(after(attn_1, weight_grad), group, two)
        near_other_z = lax.ppermute(after(near_z, weight_grad), "ctx", swap)
        suffix = after(suffix, weight_grad, attn_1, attn_2)

    query_grad, key_grad, value_grad = backward(queries, keys, values, draw, prefix, suffix, glocal)

    if paired:
        far_other = lax.ppermute(after(far_mine, weight_grad), "ctx", swap)
        near_out = project_near(
            scal, after(own_out, query_grad), (attn_1, attn_2),
            (near_mine, near_z, near_other, near_other_z),
        )
        far_other_z = lax.ppermute(after(far_z, near_out), "ctx", swap)
        layer_out = project_far(scal, near_out, attn_3, (far_mine, far_other, far_z, far_other_z))
    else:
        full = lax.all_gather(out_weight, "ctx", axis=1, tiled=True)
        partial_out = jnp.dot(attn, full, preferred_element_type=F32).astype(BF16)
        layer_out = lax.psum_scatter(partial_out, "head", scatter_dimension=1, tiled=True)
    return layer_out, query_grad, key_grad, value_grad, weight_grad


def solution(mesh):
    tokens = P(("rep", "ctx"), "head")
    sizes = mesh.shape["ctx"], mesh.shape["head"], mesh.shape["rep"]
    return jax.shard_map(
        functools.partial(body, *sizes),
        mesh=mesh,
        in_specs=(tokens, tokens, tokens, P("head", "ctx"), P(("rep", "ctx"), None)),
        out_specs=(tokens, tokens, tokens, tokens, P(("rep", "head"), "ctx")),
        check_vma=False,
    )
```

```python
import functools

import jax
import jax.numpy as jnp
from jax import lax
from jax.experimental import pallas as pl
from jax.experimental.pallas import tpu as pltpu
from jax.sharding import PartitionSpec as P

DH = 128
CHUNK = 256
EPS = 1e-06
F32 = jnp.float32
BF16 = jnp.bfloat16


def feature(x):
    return jnp.where(x > 0, x + 1.0, jnp.exp(jnp.minimum(x, 0.0)))


def dot_nn(a, b):
    return lax.dot_general(a, b, (((1,), (0,)), ((), ())), preferred_element_type=F32)


def dot_nt(a, b):
    return lax.dot_general(a, b, (((1,), (1,)), ((), ())), preferred_element_type=F32)


def dot_tn(a, b):
    return lax.dot_general(a, b, (((0,), (0,)), ((), ())), preferred_element_type=F32)


def shape_of(shape, dtype):
    return jax.ShapeDtypeStruct(shape, dtype)


def params(mib):
    return pltpu.CompilerParams(vmem_limit_bytes=mib * 1024 * 1024)


def cost(flops, moved):
    return pl.CostEstimate(flops=flops, transcendentals=0, bytes_accessed=moved)


def state_kernel(k_ref, v_ref, out_ref):
    for lo in range(0, k_ref.shape[1], DH):
        cols = slice(lo, lo + DH)
        fk = feature(k_ref[:, cols].astype(F32)).astype(BF16)
        out_ref[cols, :] = dot_tn(fk, v_ref[:, cols]).astype(BF16)


def local_state(keys, values):
    width = keys.shape[1]
    return pl.pallas_call(
        state_kernel,
        out_shape=shape_of((width, DH), BF16),
        compiler_params=params(16),
        cost_estimate=cost(2 * keys.size * DH, 4 * keys.size),
    )(keys, values)


def opening_kernel(s_ref, q_hbm, k_hbm, v_hbm, weight_hbm, grad_hbm,
                   state_ref, near_ref, far_ref, turn_ref, q_ref, k_ref, v_ref, sems, slice_sems):
    half, wide = near_ref.shape
    rows = pl.ds(pl.multiple_of(s_ref[3] * half, half), half)
    far_column = 1 - s_ref[2]
    near_column = jnp.where(s_ref[0] == s_ref[1], far_column, s_ref[2])
    loads = []
    for i, lo in enumerate(range(0, k_hbm.shape[1], DH)):
        cols = pl.ds(lo, DH)
        loads.append([
            pltpu.make_async_copy(k_hbm.at[:, cols], k_ref.at[:, cols], sems.at[0, i]),
            pltpu.make_async_copy(v_hbm.at[:, cols], v_ref.at[:, cols], sems.at[1, i]),
        ])
        loads[-1][0].start()
        loads[-1][1].start()
    moves = []
    for i, (column, ref) in enumerate([(near_column, near_ref), (far_column, far_ref)]):
        cols = pl.ds(pl.multiple_of(column * wide, wide), wide)
        moves.append(pltpu.make_async_copy(weight_hbm.at[rows, cols], ref, slice_sems.at[i]))
        moves[-1].start()
    moves.append(pltpu.make_async_copy(q_hbm, q_ref, slice_sems.at[2]))
    moves[-1].start()
    own = turn_ref.shape[1]
    cols = pl.ds(pl.multiple_of((1 - s_ref[0]) * own, own), own)
    moves.append(pltpu.make_async_copy(grad_hbm.at[:, cols], turn_ref, slice_sems.at[3]))
    moves[-1].start()
    for i, lo in enumerate(range(0, k_hbm.shape[1], DH)):
        cols = slice(lo, lo + DH)
        loads[i][0].wait()
        loads[i][1].wait()
        fk = feature(k_ref[:, cols].astype(F32)).astype(BF16)
        state_ref[cols, :] = dot_tn(fk, v_ref[:, cols]).astype(BF16)
    for move in moves:
        move.wait()


def opening(scal, queries, keys, values, weight, out_grad):
    tok, width = keys.shape
    piece = shape_of((weight.shape[0] // 2, weight.shape[1] // 2), BF16)
    hbm = pl.BlockSpec(memory_space=pltpu.HBM)
    vmem = pl.BlockSpec(memory_space=pltpu.VMEM)
    return pl.pallas_call(
        opening_kernel,
        out_shape=(shape_of((width, DH), BF16), piece, piece, shape_of((tok, weight.shape[1]), BF16))
        + (shape_of(keys.shape, BF16),) * 3,
        in_specs=[pl.BlockSpec(memory_space=pltpu.SMEM)] + [hbm] * 5,
        out_specs=(vmem,) * 7,
        scratch_shapes=[
            pltpu.SemaphoreType.DMA((2, width // DH)),
            pltpu.SemaphoreType.DMA((4,)),
        ],
        compiler_params=params(16),
        cost_estimate=cost(2 * keys.size * DH, 4 * keys.size),
    )(scal, queries, keys, values, weight, out_grad)


def forward_kernel(q_ref, k_ref, v_ref, carried_ref, grad_hbm, attn_ref, raw_ref, prefix_ref, grad_ref, sem):
    load = pltpu.make_async_copy(grad_hbm, grad_ref, sem)
    load.start()
    tok, width = q_ref.shape
    chunk = min(CHUNK, tok)
    row = lax.broadcasted_iota(jnp.int32, (chunk, chunk), 0)
    col = lax.broadcasted_iota(jnp.int32, (chunk, chunk), 1)
    lower = row >= col
    for lo in range(0, width, DH):
        cols = slice(lo, lo + DH)
        prefix = carried_ref[cols, :].astype(F32)
        for i in range(tok // chunk):
            rows = slice(i * chunk, (i + 1) * chunk)
            fq = feature(q_ref[rows, cols].astype(F32)).astype(BF16)
            fk = feature(k_ref[rows, cols].astype(F32)).astype(BF16)
            v = v_ref[rows, cols]
            low_prefix = prefix.astype(BF16)
            prefix_ref[i, cols, :] = low_prefix
            scores = jnp.where(lower, dot_nt(fq, fk), 0.0).astype(BF16)
            raw = dot_nn(scores, v) + dot_nn(fq, low_prefix)
            raw_ref[rows, cols] = raw
            inv = lax.rsqrt(jnp.mean(raw * raw, axis=-1, keepdims=True) + EPS)
            attn_ref[rows, cols] = (raw * inv).astype(BF16)
            if i + 1 < tok // chunk:
                prefix = prefix + dot_tn(fk, v)
    load.wait()


def forward(queries, keys, values, carried, out_grad):
    tok, width = queries.shape
    vmem = pl.BlockSpec(memory_space=pltpu.VMEM)
    chunks = tok // min(CHUNK, tok)
    return pl.pallas_call(
        forward_kernel,
        out_shape=(
            shape_of((tok, width), BF16),
            shape_of((tok, width), F32),
            shape_of((chunks, width, DH), BF16),
            shape_of(out_grad.shape, BF16),
        ),
        in_specs=[vmem] * 4 + [pl.BlockSpec(memory_space=pltpu.HBM)],
        out_specs=(vmem,) * 4,
        scratch_shapes=[pltpu.SemaphoreType.DMA],
        compiler_params=params(16),
        cost_estimate=cost(16 * queries.size * DH, 12 * queries.size),
    )(queries, keys, values, carried, out_grad)


def cotangent_kernel(s_ref, own_ref, grad_ref, rest_ref, q_ref, raw_ref, attn_ref,
                     draw_ref, gsum_ref, glocal_ref, out_ref, acc_ref):
    own_width, rest_width = own_ref.shape[1], rest_ref.shape[1]
    count = (own_width + rest_width) // own_width
    tok, width = q_ref.shape
    chunk = min(CHUNK, tok)

    def part(k):
        place = lax.rem(s_ref[0] + k, count) * own_width
        return grad_ref[:, pl.ds(pl.multiple_of(place, own_width), own_width)]

    acc_ref[...] = dot_nt(part(0), own_ref[...])
    for k in range(1, count):
        acc_ref[...] += dot_nt(part(k), rest_ref[:, (k - 1) * own_width : k * own_width])
    for lo in range(0, width, DH):
        cols = slice(lo, lo + DH)
        later = jnp.zeros((DH, DH), F32)
        for i in reversed(range(tok // chunk)):
            rows = slice(i * chunk, (i + 1) * chunk)
            glocal_ref[i, cols, :] = later
            grad = acc_ref[rows, cols].astype(BF16).astype(F32)
            raw = raw_ref[rows, cols]
            inv = lax.rsqrt(jnp.mean(raw * raw, axis=-1, keepdims=True) + EPS)
            normed = raw * inv
            mean = jnp.mean(grad * normed, axis=-1, keepdims=True)
            draw = (inv * (grad - normed * mean)).astype(BF16)
            draw_ref[rows, cols] = draw
            fq = feature(q_ref[rows, cols].astype(F32)).astype(BF16)
            later = later + dot_tn(fq, draw)
        gsum_ref[cols, :] = later.astype(BF16)
    wide = out_ref.shape[1]
    if wide < own_width:
        local = pl.ds(pl.multiple_of(s_ref[2] * wide, wide), wide)
        weight = jnp.where(s_ref[0] == s_ref[1], own_ref[:, local], rest_ref[:, local])
        out_ref[...] = dot_nn(attn_ref[...], weight)


def smem_then_vmem(count):
    return [pl.BlockSpec(memory_space=pltpu.SMEM)] + [pl.BlockSpec(memory_space=pltpu.VMEM)] * count


def cotangent(scal, weight, out_grad, rest, queries, raw, attn, out_width):
    tok, width = queries.shape
    chunks = tok // min(CHUNK, tok)
    return pl.pallas_call(
        cotangent_kernel,
        out_shape=(
            shape_of((tok, width), BF16),
            shape_of((width, DH), BF16),
            shape_of((chunks, width, DH), F32),
            shape_of((tok, out_width), F32),
        ),
        in_specs=smem_then_vmem(6),
        scratch_shapes=[pltpu.VMEM((tok, width), F32)],
        compiler_params=params(16),
        cost_estimate=cost(2 * out_grad.size * width, 4 * out_grad.size),
    )(scal, weight, out_grad, rest, queries, raw, attn)


def weight_grad_kernel(s_ref, attn_ref, grad_ref, other_ref, other_grad_ref, out_hbm, out_buf, sems):
    tok, width = attn_ref.shape
    blocks, _, block = out_buf.shape
    attn_t = attn_ref[...].T
    others_t = [other_ref[lo : lo + tok, :].T for lo in range(0, other_ref.shape[0], tok)]
    moves = []
    for j in range(blocks):
        here = slice(j * block, (j + 1) * block)
        place = s_ref[0] * (blocks * block) + j * block
        part = grad_ref[:, pl.ds(pl.multiple_of(place, block), block)]
        acc = dot_nn(attn_t, part).astype(BF16).astype(F32)
        for k, other_t in enumerate(others_t):
            part = other_grad_ref[k * tok : (k + 1) * tok, here]
            acc += dot_nn(other_t, part).astype(BF16).astype(F32)
        out_buf[j] = acc
        moves.append(pltpu.make_async_copy(out_buf.at[j], out_hbm.at[:, here], sems.at[j]))
        moves[-1].start()
    for move in moves:
        move.wait()


def own_weight_grad(scal, attn, out_grad, other, other_grad):
    width = attn.shape[1]
    own_width = other_grad.shape[1]
    block = min(256, own_width)
    return pl.pallas_call(
        weight_grad_kernel,
        out_shape=shape_of((width, own_width), F32),
        in_specs=smem_then_vmem(4),
        out_specs=pl.BlockSpec(memory_space=pl.ANY),
        scratch_shapes=[
            pltpu.VMEM((own_width // block, width, block), F32),
            pltpu.SemaphoreType.DMA((own_width // block,)),
        ],
        compiler_params=params(16),
        cost_estimate=cost(2 * out_grad.size * width, 4 * out_grad.size),
    )(scal, attn, out_grad, other, other_grad)


def backward_kernel(q_ref, k_ref, v_ref, draw_ref, prefix_ref, suffix_ref, glocal_ref,
                    dq_ref, dk_ref, dv_ref):
    tok, width = q_ref.shape
    chunk = min(CHUNK, tok)
    row = lax.broadcasted_iota(jnp.int32, (chunk, chunk), 0)
    col = lax.broadcasted_iota(jnp.int32, (chunk, chunk), 1)
    lower = row >= col
    upper = row <= col
    for lo in range(0, width, DH):
        cols = slice(lo, lo + DH)
        suffix = suffix_ref[cols, :].astype(F32)
        for i in range(tok // chunk):
            rows = slice(i * chunk, (i + 1) * chunk)
            q = q_ref[rows, cols].astype(F32)
            k = k_ref[rows, cols].astype(F32)
            q_slope = jnp.exp(jnp.minimum(q, 0.0))
            k_slope = jnp.exp(jnp.minimum(k, 0.0))
            fq = jnp.where(q > 0, q + 1.0, q_slope).astype(BF16)
            fk = jnp.where(k > 0, k + 1.0, k_slope).astype(BF16)
            v = v_ref[rows, cols]
            draw = draw_ref[rows, cols]
            later = (suffix + glocal_ref[i, cols, :]).astype(BF16)
            dscores = jnp.where(lower, dot_nt(draw, v), 0.0).astype(BF16)
            dfq = dot_nn(dscores, fk) + dot_nt(draw, prefix_ref[i, cols, :])
            dq_ref[rows, cols] = (dfq * q_slope).astype(BF16)
            dscores_t = jnp.where(upper, dot_nt(v, draw), 0.0).astype(BF16)
            dfk = dot_nn(dscores_t, fq) + dot_nt(v, later)
            dk_ref[rows, cols] = (dfk * k_slope).astype(BF16)
            scores_t = jnp.where(upper, dot_nt(fk, fq), 0.0).astype(BF16)
            dv = dot_nn(scores_t, draw) + dot_nn(fk, later)
            dv_ref[rows, cols] = dv.astype(BF16)


def backward(queries, keys, values, draw, prefix, suffix, glocal):
    out = shape_of(queries.shape, BF16)
    return pl.pallas_call(
        backward_kernel,
        out_shape=(out, out, out),
        compiler_params=params(16),
        cost_estimate=cost(32 * queries.size * DH, 16 * queries.size),
    )(queries, keys, values, draw, prefix, suffix, glocal)


def halves(s_ref, half):
    first = pl.ds(pl.multiple_of(s_ref[3] * half, half), half)
    second = pl.ds(pl.multiple_of((1 - s_ref[3]) * half, half), half)
    return first, second


def project_near_kernel(s_ref, out_so_far_ref, a1_ref, a2_ref, m1_ref, z1_ref, o1_ref, oz1_ref, out_ref):
    first, second = halves(s_ref, m1_ref.shape[0])
    acc = out_so_far_ref[...] + dot_nn(a1_ref[:, first], m1_ref[...])
    acc += dot_nn(a1_ref[:, second], z1_ref[...])
    acc += dot_nn(a2_ref[:, first], o1_ref[...])
    acc += dot_nn(a2_ref[:, second], oz1_ref[...])
    out_ref[...] = acc


def project_near(scal, out_so_far, attns, pieces):
    tok, width = attns[0].shape
    out_width = pieces[0].shape[1]
    return pl.pallas_call(
        project_near_kernel,
        out_shape=shape_of((tok, out_width), F32),
        in_specs=smem_then_vmem(7),
        compiler_params=params(16),
        cost_estimate=cost(4 * tok * width * out_width, 8 * width * out_width),
    )(scal, out_so_far, *attns, *pieces)


def project_far_kernel(s_ref, near_ref, a_ref, d_ref, od_ref, dz_ref, odz_ref, out_hbm, out_buf, sems):
    first, second = halves(s_ref, d_ref.shape[0])
    blocks, _, block = out_buf.shape
    moves = []
    for j in range(blocks):
        here = slice(j * block, (j + 1) * block)
        acc = near_ref[:, here] + dot_nn(a_ref[:, first], d_ref[:, here] + od_ref[:, here])
        acc += dot_nn(a_ref[:, second], dz_ref[:, here] + odz_ref[:, here])
        out_buf[j] = acc.astype(BF16)
        moves.append(pltpu.make_async_copy(out_buf.at[j], out_hbm.at[:, here], sems.at[j]))
        moves[-1].start()
    for move in moves:
        move.wait()


def project_far(scal, near, attn, pieces):
    tok, width = attn.shape
    out_width = pieces[0].shape[1]
    block = 256
    return pl.pallas_call(
        project_far_kernel,
        out_shape=shape_of((tok, out_width), BF16),
        in_specs=smem_then_vmem(6),
        out_specs=pl.BlockSpec(memory_space=pl.ANY),
        scratch_shapes=[
            pltpu.VMEM((out_width // block, tok, block), BF16),
            pltpu.SemaphoreType.DMA((out_width // block,)),
        ],
        compiler_params=params(16),
        cost_estimate=cost(2 * tok * width * out_width, 8 * width * out_width),
    )(scal, near, attn, *pieces)


def in_hbm(array):
    return pltpu.with_memory_space_constraint(array, pltpu.HBM)


def after(array, *needed):
    return lax.optimization_barrier((array, *needed))[0]


def shift(array, axis, count, by, wrap):
    pairs = [(i, (i + by) % count) for i in range(count) if wrap or 0 <= i + by < count]
    return lax.ppermute(array, axis, pairs)


def total(arrays):
    if len(arrays) == 1:
        return arrays[0]
    return functools.reduce(jnp.add, [a.astype(F32) for a in arrays])


def body(n_ctx, n_head, n_rep, queries, keys, values, out_weight, out_grad):
    c, h, z = lax.axis_index("ctx"), lax.axis_index("head"), lax.axis_index("rep")
    x, y, p = h & 1, h >> 1, z & 1
    scal = jnp.stack([c, y, x, p]).astype(jnp.int32)
    paired = n_ctx == 2 and n_head == 4 and n_rep % 2 == 0
    own_width = out_weight.shape[1]
    weight_hbm, grad_hbm = in_hbm(out_weight), in_hbm(out_grad)

    if paired:
        group = ("ctx", "head")
        near = [(4 * (i // 2) + i, i ^ 1) for i in range(4)]
        near += [(4 * (1 - i // 2) + i, 4 + (i ^ 2)) for i in range(4)]
        far = [(4 * (1 - i // 2) + i, i ^ 3) for i in range(4)]
        one = [(i, i ^ 1) for i in range(4)] + [(4 + i, 4 + (i ^ 2)) for i in range(4)]
        two = [(i, i ^ 2) for i in range(4)] + [(4 + i, 4 + (i ^ 1)) for i in range(4)]
        zpair = [(i, i ^ 1) for i in range(n_rep)]
        swap = [(0, 1), (1, 0)]
        state, near_piece, far_piece, turn, queries, keys, values = opening(
            scal, in_hbm(queries), in_hbm(keys), in_hbm(values), weight_hbm, grad_hbm
        )
        near_mine = lax.ppermute(near_piece, group, near)
        far_mine = lax.ppermute(far_piece, group, far)
        other_grad = lax.ppermute(turn, "ctx", swap)
    else:
        state = local_state(keys, values)
        other_grad = []
        for k in range(1, n_ctx):
            start = lax.rem(c + k, n_ctx) * own_width
            turn = lax.dynamic_slice_in_dim(out_grad, start, own_width, 1)
            other_grad.append(shift(turn, "ctx", n_ctx, k, True))
        other_grad = jnp.concatenate(other_grad, 0)

    carried = total([shift(state, "ctx", n_ctx, k, False) for k in range(1, n_ctx)])
    rest = [shift(out_weight, "ctx", n_ctx, -k, True) for k in range(1, n_ctx)]
    rest = rest[0] if n_ctx == 2 else jnp.concatenate(rest, 1)
    if paired:
        carried = after(carried, rest)
    attn, raw, prefix, grad_vmem = forward(queries, keys, values, carried, grad_hbm)

    if paired:
        attn_1 = lax.ppermute(attn, group, one)
        attn_2 = lax.ppermute(attn, group, two)
        near_z = lax.ppermute(near_mine, "rep", zpair)
        raw = after(raw, near_mine, rest, other_grad)
    other_attn = [shift(attn, "ctx", n_ctx, k, True) for k in range(1, n_ctx)]
    other_attn = other_attn[0] if n_ctx == 2 else jnp.concatenate(other_attn, 0)

    draw, gsum, glocal, own_out = cotangent(
        scal, out_weight, grad_vmem, rest, queries, raw, attn, own_width // 2 if paired else own_width
    )
    suffix = total([shift(gsum, "ctx", n_ctx, -k, False) for k in range(1, n_ctx)])

    if paired:
        far_z = lax.ppermute(after(far_mine, gsum), ("ctx", "rep"), zpair)
        other_attn = after(other_attn, gsum, far_mine)

    weight_grad = own_weight_grad(scal, attn, grad_vmem, other_attn, other_grad)

    if paired:
        near_other = lax.ppermute(after(near_mine, weight_grad), "ctx", swap)
        attn_3 = lax.ppermute(after(attn_1, weight_grad), group, two)
        near_other_z = lax.ppermute(after(near_z, weight_grad), "ctx", swap)
        suffix = after(suffix, weight_grad, attn_1, attn_2)

    query_grad, key_grad, value_grad = backward(queries, keys, values, draw, prefix, suffix, glocal)

    if paired:
        far_other = lax.ppermute(after(far_mine, weight_grad), "ctx", [(0, 1)])
        near_out = project_near(
            scal, after(own_out, query_grad), (attn_1, attn_2),
            (near_mine, near_z, near_other, near_other_z),
        )
        far_other_z = lax.ppermute(after(far_z, near_out), "ctx", [(0, 1)])
        layer_out = project_far(scal, near_out, attn_3, (far_mine, far_other, far_z, far_other_z))
    else:
        full = lax.all_gather(out_weight, "ctx", axis=1, tiled=True)
        partial_out = jnp.dot(attn, full, preferred_element_type=F32).astype(BF16)
        layer_out = lax.psum_scatter(partial_out, "head", scatter_dimension=1, tiled=True)
    return layer_out, query_grad, key_grad, value_grad, weight_grad


def solution(mesh):
    tokens = P(("rep", "ctx"), "head")
    sizes = mesh.shape["ctx"], mesh.shape["head"], mesh.shape["rep"]
    return jax.shard_map(
        functools.partial(body, *sizes),
        mesh=mesh,
        in_specs=(tokens, tokens, tokens, P("head", "ctx"), P(("rep", "ctx"), None)),
        out_specs=(tokens, tokens, tokens, tokens, P(("rep", "head"), "ctx")),
        check_vma=False,
    )
```

```python
import functools

import jax
import jax.numpy as jnp
from jax import lax
from jax.experimental import pallas as pl
from jax.experimental.pallas import tpu as pltpu
from jax.sharding import PartitionSpec as P

DH = 128
CHUNK = 256
EPS = 1e-06
F32 = jnp.float32
BF16 = jnp.bfloat16


def feature(x):
    return jnp.where(x > 0, x + 1.0, jnp.exp(jnp.minimum(x, 0.0)))


def dot_nn(a, b):
    return lax.dot_general(a, b, (((1,), (0,)), ((), ())), preferred_element_type=F32)


def dot_nt(a, b):
    return lax.dot_general(a, b, (((1,), (1,)), ((), ())), preferred_element_type=F32)


def dot_tn(a, b):
    return lax.dot_general(a, b, (((0,), (0,)), ((), ())), preferred_element_type=F32)


def shape_of(shape, dtype):
    return jax.ShapeDtypeStruct(shape, dtype)


def params(mib):
    return pltpu.CompilerParams(vmem_limit_bytes=mib * 1024 * 1024)


def cost(flops, moved):
    return pl.CostEstimate(flops=flops, transcendentals=0, bytes_accessed=moved)


def state_kernel(k_ref, v_ref, out_ref):
    for lo in range(0, k_ref.shape[1], DH):
        cols = slice(lo, lo + DH)
        fk = feature(k_ref[:, cols].astype(F32)).astype(BF16)
        out_ref[cols, :] = dot_tn(fk, v_ref[:, cols]).astype(BF16)


def local_state(keys, values):
    width = keys.shape[1]
    return pl.pallas_call(
        state_kernel,
        out_shape=shape_of((width, DH), BF16),
        compiler_params=params(16),
        cost_estimate=cost(2 * keys.size * DH, 4 * keys.size),
    )(keys, values)


def opening_kernel(s_ref, q_hbm, k_hbm, v_hbm, weight_hbm, grad_hbm,
                   state_ref, near_ref, far_ref, turn_ref, q_ref, k_ref, v_ref, sems, slice_sems):
    half, wide = near_ref.shape
    rows = pl.ds(pl.multiple_of(s_ref[3] * half, half), half)
    far_column = 1 - s_ref[2]
    near_column = jnp.where(s_ref[0] == s_ref[1], far_column, s_ref[2])
    loads = []
    for i, lo in enumerate(range(0, k_hbm.shape[1], DH)):
        cols = pl.ds(lo, DH)
        loads.append([
            pltpu.make_async_copy(k_hbm.at[:, cols], k_ref.at[:, cols], sems.at[0, i]),
            pltpu.make_async_copy(v_hbm.at[:, cols], v_ref.at[:, cols], sems.at[1, i]),
        ])
        loads[-1][0].start()
        loads[-1][1].start()
    moves = []
    for i, (column, ref) in enumerate([(near_column, near_ref), (far_column, far_ref)]):
        cols = pl.ds(pl.multiple_of(column * wide, wide), wide)
        moves.append(pltpu.make_async_copy(weight_hbm.at[rows, cols], ref, slice_sems.at[i]))
        moves[-1].start()
    moves.append(pltpu.make_async_copy(q_hbm, q_ref, slice_sems.at[2]))
    moves[-1].start()
    own = turn_ref.shape[1]
    cols = pl.ds(pl.multiple_of((1 - s_ref[0]) * own, own), own)
    moves.append(pltpu.make_async_copy(grad_hbm.at[:, cols], turn_ref, slice_sems.at[3]))
    moves[-1].start()
    for i, lo in enumerate(range(0, k_hbm.shape[1], DH)):
        cols = slice(lo, lo + DH)
        loads[i][0].wait()
        loads[i][1].wait()
        fk = feature(k_ref[:, cols].astype(F32)).astype(BF16)
        state_ref[cols, :] = dot_tn(fk, v_ref[:, cols]).astype(BF16)
    for move in moves:
        move.wait()


def opening(scal, queries, keys, values, weight, out_grad):
    tok, width = keys.shape
    piece = shape_of((weight.shape[0] // 2, weight.shape[1] // 2), BF16)
    hbm = pl.BlockSpec(memory_space=pltpu.HBM)
    vmem = pl.BlockSpec(memory_space=pltpu.VMEM)
    return pl.pallas_call(
        opening_kernel,
        out_shape=(shape_of((width, DH), BF16), piece, piece, shape_of((tok, weight.shape[1]), BF16))
        + (shape_of(keys.shape, BF16),) * 3,
        in_specs=[pl.BlockSpec(memory_space=pltpu.SMEM)] + [hbm] * 5,
        out_specs=(vmem,) * 7,
        scratch_shapes=[
            pltpu.SemaphoreType.DMA((2, width // DH)),
            pltpu.SemaphoreType.DMA((4,)),
        ],
        compiler_params=params(16),
        cost_estimate=cost(2 * keys.size * DH, 4 * keys.size),
    )(scal, queries, keys, values, weight, out_grad)


def forward_kernel(q_ref, k_ref, v_ref, carried_ref, attn_ref, raw_ref, prefix_ref):
    tok, width = q_ref.shape
    chunk = min(CHUNK, tok)
    row = lax.broadcasted_iota(jnp.int32, (chunk, chunk), 0)
    col = lax.broadcasted_iota(jnp.int32, (chunk, chunk), 1)
    lower = row >= col
    for lo in range(0, width, DH):
        cols = slice(lo, lo + DH)
        prefix = carried_ref[cols, :].astype(F32)
        for i in range(tok // chunk):
            rows = slice(i * chunk, (i + 1) * chunk)
            fq = feature(q_ref[rows, cols].astype(F32)).astype(BF16)
            fk = feature(k_ref[rows, cols].astype(F32)).astype(BF16)
            v = v_ref[rows, cols]
            low_prefix = prefix.astype(BF16)
            prefix_ref[i, cols, :] = low_prefix
            scores = jnp.where(lower, dot_nt(fq, fk), 0.0).astype(BF16)
            raw = dot_nn(scores, v) + dot_nn(fq, low_prefix)
            raw_ref[rows, cols] = raw
            inv = lax.rsqrt(jnp.mean(raw * raw, axis=-1, keepdims=True) + EPS)
            attn_ref[rows, cols] = (raw * inv).astype(BF16)
            if i + 1 < tok // chunk:
                prefix = prefix + dot_tn(fk, v)


def forward(queries, keys, values, carried):
    tok, width = queries.shape
    chunks = tok // min(CHUNK, tok)
    return pl.pallas_call(
        forward_kernel,
        out_shape=(
            shape_of((tok, width), BF16),
            shape_of((tok, width), F32),
            shape_of((chunks, width, DH), BF16),
        ),
        compiler_params=params(16),
        cost_estimate=cost(16 * queries.size * DH, 12 * queries.size),
    )(queries, keys, values, carried)


def smem_then_vmem(count):
    return [pl.BlockSpec(memory_space=pltpu.SMEM)] + [pl.BlockSpec(memory_space=pltpu.VMEM)] * count


def attn_grad_kernel(s_ref, own_ref, grad_ref, rest_ref, out_ref, acc_ref):
    own_width, rest_width = own_ref.shape[1], rest_ref.shape[1]
    count = (own_width + rest_width) // own_width

    def part(k):
        place = lax.rem(s_ref[0] + k, count) * own_width
        return grad_ref[:, pl.ds(pl.multiple_of(place, own_width), own_width)]

    acc_ref[...] = dot_nt(part(0), own_ref[...])
    for k in range(1, count):
        acc_ref[...] += dot_nt(part(k), rest_ref[:, (k - 1) * own_width : k * own_width])
    out_ref[...] = acc_ref[...].astype(BF16)


def attn_gradient(scal, weight, out_grad, rest):
    tok, width = out_grad.shape[0], weight.shape[0]
    return pl.pallas_call(
        attn_grad_kernel,
        out_shape=shape_of((tok, width), BF16),
        in_specs=smem_then_vmem(3),
        scratch_shapes=[pltpu.VMEM((tok, width), F32)],
        compiler_params=params(16),
        cost_estimate=cost(2 * out_grad.size * width, 4 * out_grad.size),
    )(scal, weight, out_grad, rest)


def cotangent_kernel(s_ref, attn_grad_ref, q_ref, raw_ref, attn_ref, own_ref, rest_ref,
                     draw_ref, gsum_ref, glocal_ref, out_ref):
    tok, width = q_ref.shape
    chunk = min(CHUNK, tok)
    for lo in range(0, width, DH):
        cols = slice(lo, lo + DH)
        later = jnp.zeros((DH, DH), F32)
        for i in reversed(range(tok // chunk)):
            rows = slice(i * chunk, (i + 1) * chunk)
            glocal_ref[i, cols, :] = later
            grad = attn_grad_ref[rows, cols].astype(F32)
            raw = raw_ref[rows, cols]
            inv = lax.rsqrt(jnp.mean(raw * raw, axis=-1, keepdims=True) + EPS)
            normed = raw * inv
            mean = jnp.mean(grad * normed, axis=-1, keepdims=True)
            draw = (inv * (grad - normed * mean)).astype(BF16)
            draw_ref[rows, cols] = draw
            fq = feature(q_ref[rows, cols].astype(F32)).astype(BF16)
            later = later + dot_tn(fq, draw)
        gsum_ref[cols, :] = later.astype(BF16)
    wide = out_ref.shape[1]
    if wide < own_ref.shape[1]:
        local = pl.ds(pl.multiple_of(s_ref[2] * wide, wide), wide)
        weight = jnp.where(s_ref[0] == s_ref[1], own_ref[:, local], rest_ref[:, local])
        out_ref[...] = dot_nn(attn_ref[...], weight)


def cotangent(scal, attn_grad, queries, raw, attn, own, rest, out_width):
    tok, width = queries.shape
    chunks = tok // min(CHUNK, tok)
    return pl.pallas_call(
        cotangent_kernel,
        out_shape=(
            shape_of((tok, width), BF16),
            shape_of((width, DH), BF16),
            shape_of((chunks, width, DH), F32),
            shape_of((tok, out_width), F32),
        ),
        in_specs=smem_then_vmem(6),
        compiler_params=params(16),
        cost_estimate=cost(2 * tok * width * out_width, 16 * queries.size),
    )(scal, attn_grad, queries, raw, attn, own, rest)


def weight_grad_kernel(s_ref, attn_ref, grad_ref, other_ref, other_grad_ref, out_hbm, out_buf, sems):
    tok, width = attn_ref.shape
    blocks, _, block = out_buf.shape
    attn_t = attn_ref[...].T
    others_t = [other_ref[lo : lo + tok, :].T for lo in range(0, other_ref.shape[0], tok)]
    moves = []
    for j in range(blocks):
        here = slice(j * block, (j + 1) * block)
        place = s_ref[0] * (blocks * block) + j * block
        part = grad_ref[:, pl.ds(pl.multiple_of(place, block), block)]
        acc = dot_nn(attn_t, part).astype(BF16).astype(F32)
        for k, other_t in enumerate(others_t):
            part = other_grad_ref[k * tok : (k + 1) * tok, here]
            acc += dot_nn(other_t, part).astype(BF16).astype(F32)
        out_buf[j] = acc
        moves.append(pltpu.make_async_copy(out_buf.at[j], out_hbm.at[:, here], sems.at[j]))
        moves[-1].start()
    for move in moves:
        move.wait()


def own_weight_grad(scal, attn, out_grad, other, other_grad):
    width = attn.shape[1]
    own_width = other_grad.shape[1]
    block = min(256, own_width)
    return pl.pallas_call(
        weight_grad_kernel,
        out_shape=shape_of((width, own_width), F32),
        in_specs=smem_then_vmem(4),
        out_specs=pl.BlockSpec(memory_space=pl.ANY),
        scratch_shapes=[
            pltpu.VMEM((own_width // block, width, block), F32),
            pltpu.SemaphoreType.DMA((own_width // block,)),
        ],
        compiler_params=params(16),
        cost_estimate=cost(2 * out_grad.size * width, 4 * out_grad.size),
    )(scal, attn, out_grad, other, other_grad)


def backward_kernel(q_ref, k_ref, v_ref, draw_ref, prefix_ref, suffix_ref, glocal_ref,
                    dq_ref, dk_ref, dv_ref):
    tok, width = q_ref.shape
    chunk = min(CHUNK, tok)
    row = lax.broadcasted_iota(jnp.int32, (chunk, chunk), 0)
    col = lax.broadcasted_iota(jnp.int32, (chunk, chunk), 1)
    lower = row >= col
    upper = row <= col
    for lo in range(0, width, DH):
        cols = slice(lo, lo + DH)
        suffix = suffix_ref[cols, :].astype(F32)
        for i in range(tok // chunk):
            rows = slice(i * chunk, (i + 1) * chunk)
            q = q_ref[rows, cols].astype(F32)
            k = k_ref[rows, cols].astype(F32)
            q_slope = jnp.exp(jnp.minimum(q, 0.0))
            k_slope = jnp.exp(jnp.minimum(k, 0.0))
            fq = jnp.where(q > 0, q + 1.0, q_slope).astype(BF16)
            fk = jnp.where(k > 0, k + 1.0, k_slope).astype(BF16)
            v = v_ref[rows, cols]
            draw = draw_ref[rows, cols]
            later = (suffix + glocal_ref[i, cols, :]).astype(BF16)
            dscores = jnp.where(lower, dot_nt(draw, v), 0.0).astype(BF16)
            dfq = dot_nn(dscores, fk) + dot_nt(draw, prefix_ref[i, cols, :])
            dq_ref[rows, cols] = (dfq * q_slope).astype(BF16)
            dscores_t = jnp.where(upper, dot_nt(v, draw), 0.0).astype(BF16)
            dfk = dot_nn(dscores_t, fq) + dot_nt(v, later)
            dk_ref[rows, cols] = (dfk * k_slope).astype(BF16)
            scores_t = jnp.where(upper, dot_nt(fk, fq), 0.0).astype(BF16)
            dv = dot_nn(scores_t, draw) + dot_nn(fk, later)
            dv_ref[rows, cols] = dv.astype(BF16)


def backward(queries, keys, values, draw, prefix, suffix, glocal):
    out = shape_of(queries.shape, BF16)
    return pl.pallas_call(
        backward_kernel,
        out_shape=(out, out, out),
        compiler_params=params(16),
        cost_estimate=cost(32 * queries.size * DH, 16 * queries.size),
    )(queries, keys, values, draw, prefix, suffix, glocal)


def halves(s_ref, half):
    first = pl.ds(pl.multiple_of(s_ref[3] * half, half), half)
    second = pl.ds(pl.multiple_of((1 - s_ref[3]) * half, half), half)
    return first, second


def project_kernel(s_ref, own_out_ref, a1_ref, a2_ref, a3_ref, m1_ref, z1_ref, o1_ref, oz1_ref,
                   d_ref, od_ref, dz_ref, odz_ref, out_hbm, out_buf, sems):
    first, second = halves(s_ref, d_ref.shape[0])
    blocks, _, block = out_buf.shape
    moves = []
    for j in range(blocks):
        here = slice(j * block, (j + 1) * block)
        acc = own_out_ref[:, here] + dot_nn(a1_ref[:, first], m1_ref[:, here])
        acc += dot_nn(a1_ref[:, second], z1_ref[:, here])
        acc += dot_nn(a2_ref[:, first], o1_ref[:, here])
        acc += dot_nn(a2_ref[:, second], oz1_ref[:, here])
        acc += dot_nn(a3_ref[:, first], d_ref[:, here] + od_ref[:, here])
        acc += dot_nn(a3_ref[:, second], dz_ref[:, here] + odz_ref[:, here])
        out_buf[j] = acc.astype(BF16)
        moves.append(pltpu.make_async_copy(out_buf.at[j], out_hbm.at[:, here], sems.at[j]))
        moves[-1].start()
    for move in moves:
        move.wait()


def project(scal, own_out, attns, pieces):
    tok, width = attns[0].shape
    out_width = own_out.shape[1]
    block = 256
    return pl.pallas_call(
        project_kernel,
        out_shape=shape_of((tok, out_width), BF16),
        in_specs=smem_then_vmem(12),
        out_specs=pl.BlockSpec(memory_space=pl.ANY),
        scratch_shapes=[
            pltpu.VMEM((out_width // block, tok, block), BF16),
            pltpu.SemaphoreType.DMA((out_width // block,)),
        ],
        compiler_params=params(16),
        cost_estimate=cost(6 * tok * width * out_width, 8 * width * out_width),
    )(scal, own_out, *attns, *pieces)


def in_hbm(array):
    return pltpu.with_memory_space_constraint(array, pltpu.HBM)


def after(array, *needed):
    return lax.optimization_barrier((array, *needed))[0]


def shift(array, axis, count, by, wrap):
    pairs = [(i, (i + by) % count) for i in range(count) if wrap or 0 <= i + by < count]
    return lax.ppermute(array, axis, pairs)


def total(arrays):
    if len(arrays) == 1:
        return arrays[0]
    return functools.reduce(jnp.add, [a.astype(F32) for a in arrays])


def body(n_ctx, n_head, n_rep, queries, keys, values, out_weight, out_grad):
    c, h, z = lax.axis_index("ctx"), lax.axis_index("head"), lax.axis_index("rep")
    x, y, p = h & 1, h >> 1, z & 1
    scal = jnp.stack([c, y, x, p]).astype(jnp.int32)
    paired = n_ctx == 2 and n_head == 4 and n_rep % 2 == 0
    own_width = out_weight.shape[1]
    weight_hbm, grad_hbm = in_hbm(out_weight), in_hbm(out_grad)

    if paired:
        group = ("ctx", "head")
        near = [(4 * (i // 2) + i, i ^ 1) for i in range(4)]
        near += [(4 * (1 - i // 2) + i, 4 + (i ^ 2)) for i in range(4)]
        far = [(4 * (1 - i // 2) + i, i ^ 3) for i in range(4)]
        one = [(i, i ^ 1) for i in range(4)] + [(4 + i, 4 + (i ^ 2)) for i in range(4)]
        two = [(i, i ^ 2) for i in range(4)] + [(4 + i, 4 + (i ^ 1)) for i in range(4)]
        zpair = [(i, i ^ 1) for i in range(n_rep)]
        swap = [(0, 1), (1, 0)]
        state, near_piece, far_piece, turn, queries, keys, values = opening(
            scal, in_hbm(queries), in_hbm(keys), in_hbm(values), weight_hbm, grad_hbm
        )
        near_mine = lax.ppermute(near_piece, group, near)
        far_mine = lax.ppermute(far_piece, group, far)
        other_grad = lax.ppermute(turn, "ctx", swap)
    else:
        state = local_state(keys, values)
        other_grad = []
        for k in range(1, n_ctx):
            start = lax.rem(c + k, n_ctx) * own_width
            turn = lax.dynamic_slice_in_dim(out_grad, start, own_width, 1)
            other_grad.append(shift(turn, "ctx", n_ctx, k, True))
        other_grad = jnp.concatenate(other_grad, 0)

    carried = total([shift(state, "ctx", n_ctx, k, False) for k in range(1, n_ctx)])
    rest = [shift(out_weight, "ctx", n_ctx, -k, True) for k in range(1, n_ctx)]
    rest = rest[0] if n_ctx == 2 else jnp.concatenate(rest, 1)
    attn_grad = attn_gradient(scal, out_weight, out_grad, after(rest, state))
    carried = after(carried, attn_grad)
    attn, raw, prefix = forward(queries, keys, values, carried)

    if paired:
        attn_1 = lax.ppermute(attn, group, one)
        attn_2 = lax.ppermute(attn, group, two)
        near_z = lax.ppermute(near_mine, "rep", zpair)
        raw = after(raw, near_mine, other_grad)
    other_attn = [shift(attn, "ctx", n_ctx, k, True) for k in range(1, n_ctx)]
    other_attn = other_attn[0] if n_ctx == 2 else jnp.concatenate(other_attn, 0)

    draw, gsum, glocal, own_out = cotangent(
        scal, attn_grad, queries, raw, attn, out_weight, rest, own_width // 2 if paired else own_width
    )
    suffix = total([shift(gsum, "ctx", n_ctx, -k, False) for k in range(1, n_ctx)])

    if paired:
        far_z = lax.ppermute(after(far_mine, gsum), ("ctx", "rep"), zpair)
        other_attn = after(other_attn, gsum, far_mine)

    weight_grad = own_weight_grad(scal, attn, out_grad, other_attn, other_grad)

    if paired:
        near_other = lax.ppermute(after(near_mine, weight_grad), "ctx", swap)
        attn_3 = lax.ppermute(after(attn_1, weight_grad), group, two)
        near_other_z = lax.ppermute(after(near_z, weight_grad), "ctx", swap)
        suffix = after(suffix, weight_grad, attn_1, attn_2, near_z)

    query_grad, key_grad, value_grad = backward(queries, keys, values, draw, prefix, suffix, glocal)

    if paired:
        far_other = lax.ppermute(after(far_mine, weight_grad), "ctx", [(0, 1)])
        last = after(far_z, query_grad, attn_3, near_other_z, near_other, far_other)
        far_other_z = lax.ppermute(last, "ctx", [(0, 1)])
        layer_out = project(
            scal, after(own_out, query_grad), (attn_1, attn_2, attn_3),
            (near_mine, near_z, near_other, near_other_z, far_mine, far_other, far_z, far_other_z),
        )
    else:
        full = lax.all_gather(out_weight, "ctx", axis=1, tiled=True)
        partial_out = jnp.dot(attn, full, preferred_element_type=F32).astype(BF16)
        layer_out = lax.psum_scatter(partial_out, "head", scatter_dimension=1, tiled=True)
    return layer_out, query_grad, key_grad, value_grad, weight_grad


def solution(mesh):
    tokens = P(("rep", "ctx"), "head")
    sizes = mesh.shape["ctx"], mesh.shape["head"], mesh.shape["rep"]
    return jax.shard_map(
        functools.partial(body, *sizes),
        mesh=mesh,
        in_specs=(tokens, tokens, tokens, P("head", "ctx"), P(("rep", "ctx"), None)),
        out_specs=(tokens, tokens, tokens, tokens, P(("rep", "head"), "ctx")),
        check_vma=False,
    )
```

```python
import functools

import jax
import jax.numpy as jnp
from jax import lax
from jax.experimental import pallas as pl
from jax.experimental.pallas import tpu as pltpu
from jax.sharding import PartitionSpec as P

DH = 128
CHUNK = 256
EPS = 1e-06
F32 = jnp.float32
BF16 = jnp.bfloat16


def feature(x):
    return jnp.where(x > 0, x + 1.0, jnp.exp(jnp.minimum(x, 0.0)))


def dot_nn(a, b):
    return lax.dot_general(a, b, (((1,), (0,)), ((), ())), preferred_element_type=F32)


def dot_nt(a, b):
    return lax.dot_general(a, b, (((1,), (1,)), ((), ())), preferred_element_type=F32)


def dot_tn(a, b):
    return lax.dot_general(a, b, (((0,), (0,)), ((), ())), preferred_element_type=F32)


def shape_of(shape, dtype):
    return jax.ShapeDtypeStruct(shape, dtype)


def params(mib):
    return pltpu.CompilerParams(vmem_limit_bytes=mib * 1024 * 1024)


def cost(flops, moved):
    return pl.CostEstimate(flops=flops, transcendentals=0, bytes_accessed=moved)


def state_kernel(k_ref, v_ref, out_ref):
    for lo in range(0, k_ref.shape[1], DH):
        cols = slice(lo, lo + DH)
        fk = feature(k_ref[:, cols].astype(F32)).astype(BF16)
        out_ref[cols, :] = dot_tn(fk, v_ref[:, cols]).astype(BF16)


def local_state(keys, values):
    width = keys.shape[1]
    return pl.pallas_call(
        state_kernel,
        out_shape=shape_of((width, DH), BF16),
        compiler_params=params(16),
        cost_estimate=cost(2 * keys.size * DH, 4 * keys.size),
    )(keys, values)


def opening_kernel(s_ref, q_hbm, k_hbm, v_hbm, weight_hbm, grad_hbm,
                   state_ref, near_ref, far_ref, turn_ref, q_ref, k_ref, v_ref, sems, slice_sems):
    half, wide = near_ref.shape
    rows = pl.ds(pl.multiple_of(s_ref[3] * half, half), half)
    far_column = 1 - s_ref[2]
    near_column = jnp.where(s_ref[0] == s_ref[1], far_column, s_ref[2])
    loads = []
    for i, lo in enumerate(range(0, k_hbm.shape[1], DH)):
        cols = pl.ds(lo, DH)
        loads.append([
            pltpu.make_async_copy(k_hbm.at[:, cols], k_ref.at[:, cols], sems.at[0, i]),
            pltpu.make_async_copy(v_hbm.at[:, cols], v_ref.at[:, cols], sems.at[1, i]),
        ])
        loads[-1][0].start()
        loads[-1][1].start()
    moves = []
    for i, (column, ref) in enumerate([(near_column, near_ref), (far_column, far_ref)]):
        cols = pl.ds(pl.multiple_of(column * wide, wide), wide)
        moves.append(pltpu.make_async_copy(weight_hbm.at[rows, cols], ref, slice_sems.at[i]))
        moves[-1].start()
    moves.append(pltpu.make_async_copy(q_hbm, q_ref, slice_sems.at[2]))
    moves[-1].start()
    own = turn_ref.shape[1]
    cols = pl.ds(pl.multiple_of((1 - s_ref[0]) * own, own), own)
    moves.append(pltpu.make_async_copy(grad_hbm.at[:, cols], turn_ref, slice_sems.at[3]))
    moves[-1].start()
    for i, lo in enumerate(range(0, k_hbm.shape[1], DH)):
        cols = slice(lo, lo + DH)
        loads[i][0].wait()
        loads[i][1].wait()
        fk = feature(k_ref[:, cols].astype(F32)).astype(BF16)
        state_ref[cols, :] = dot_tn(fk, v_ref[:, cols]).astype(BF16)
    for move in moves:
        move.wait()


def opening(scal, queries, keys, values, weight, out_grad):
    tok, width = keys.shape
    piece = shape_of((weight.shape[0] // 2, weight.shape[1] // 2), BF16)
    hbm = pl.BlockSpec(memory_space=pltpu.HBM)
    vmem = pl.BlockSpec(memory_space=pltpu.VMEM)
    return pl.pallas_call(
        opening_kernel,
        out_shape=(shape_of((width, DH), BF16), piece, piece, shape_of((tok, weight.shape[1]), BF16))
        + (shape_of(keys.shape, BF16),) * 3,
        in_specs=[pl.BlockSpec(memory_space=pltpu.SMEM)] + [hbm] * 5,
        out_specs=(vmem,) * 7,
        scratch_shapes=[
            pltpu.SemaphoreType.DMA((2, width // DH)),
            pltpu.SemaphoreType.DMA((4,)),
        ],
        compiler_params=params(16),
        cost_estimate=cost(2 * keys.size * DH, 4 * keys.size),
    )(scal, queries, keys, values, weight, out_grad)


def forward_kernel(q_ref, k_ref, v_ref, carried_ref, attn_ref, raw_ref, prefix_ref):
    tok, width = q_ref.shape
    chunk = min(CHUNK, tok)
    row = lax.broadcasted_iota(jnp.int32, (chunk, chunk), 0)
    col = lax.broadcasted_iota(jnp.int32, (chunk, chunk), 1)
    lower = row >= col
    for lo in range(0, width, DH):
        cols = slice(lo, lo + DH)
        prefix = carried_ref[cols, :].astype(F32)
        for i in range(tok // chunk):
            rows = slice(i * chunk, (i + 1) * chunk)
            fq = feature(q_ref[rows, cols].astype(F32)).astype(BF16)
            fk = feature(k_ref[rows, cols].astype(F32)).astype(BF16)
            v = v_ref[rows, cols]
            low_prefix = prefix.astype(BF16)
            prefix_ref[i, cols, :] = low_prefix
            scores = jnp.where(lower, dot_nt(fq, fk), 0.0).astype(BF16)
            raw = dot_nn(scores, v) + dot_nn(fq, low_prefix)
            raw_ref[rows, cols] = raw
            inv = lax.rsqrt(jnp.mean(raw * raw, axis=-1, keepdims=True) + EPS)
            attn_ref[rows, cols] = (raw * inv).astype(BF16)
            if i + 1 < tok // chunk:
                prefix = prefix + dot_tn(fk, v)


def forward(queries, keys, values, carried):
    tok, width = queries.shape
    chunks = tok // min(CHUNK, tok)
    return pl.pallas_call(
        forward_kernel,
        out_shape=(
            shape_of((tok, width), BF16),
            shape_of((tok, width), F32),
            shape_of((chunks, width, DH), BF16),
        ),
        compiler_params=params(16),
        cost_estimate=cost(16 * queries.size * DH, 12 * queries.size),
    )(queries, keys, values, carried)


def smem_then_vmem(count):
    return [pl.BlockSpec(memory_space=pltpu.SMEM)] + [pl.BlockSpec(memory_space=pltpu.VMEM)] * count


def attn_grad_kernel(s_ref, own_ref, grad_ref, rest_ref, out_ref, acc_ref):
    own_width, rest_width = own_ref.shape[1], rest_ref.shape[1]
    count = (own_width + rest_width) // own_width

    def part(k):
        place = lax.rem(s_ref[0] + k, count) * own_width
        return grad_ref[:, pl.ds(pl.multiple_of(place, own_width), own_width)]

    acc_ref[...] = dot_nt(part(0), own_ref[...])
    for k in range(1, count):
        acc_ref[...] += dot_nt(part(k), rest_ref[:, (k - 1) * own_width : k * own_width])
    out_ref[...] = acc_ref[...].astype(BF16)


def attn_gradient(scal, weight, out_grad, rest):
    tok, width = out_grad.shape[0], weight.shape[0]
    return pl.pallas_call(
        attn_grad_kernel,
        out_shape=shape_of((tok, width), BF16),
        in_specs=smem_then_vmem(3),
        scratch_shapes=[pltpu.VMEM((tok, width), F32)],
        compiler_params=params(16),
        cost_estimate=cost(2 * out_grad.size * width, 4 * out_grad.size),
    )(scal, weight, out_grad, rest)


def cotangent_kernel(s_ref, attn_grad_ref, q_ref, raw_ref, attn_ref, own_ref, rest_ref,
                     draw_ref, gsum_ref, glocal_ref, out_ref):
    tok, width = q_ref.shape
    chunk = min(CHUNK, tok)
    for lo in range(0, width, DH):
        cols = slice(lo, lo + DH)
        later = jnp.zeros((DH, DH), F32)
        for i in reversed(range(tok // chunk)):
            rows = slice(i * chunk, (i + 1) * chunk)
            glocal_ref[i, cols, :] = later
            grad = attn_grad_ref[rows, cols].astype(F32)
            raw = raw_ref[rows, cols]
            inv = lax.rsqrt(jnp.mean(raw * raw, axis=-1, keepdims=True) + EPS)
            normed = raw * inv
            mean = jnp.mean(grad * normed, axis=-1, keepdims=True)
            draw = (inv * (grad - normed * mean)).astype(BF16)
            draw_ref[rows, cols] = draw
            fq = feature(q_ref[rows, cols].astype(F32)).astype(BF16)
            later = later + dot_tn(fq, draw)
        gsum_ref[cols, :] = later.astype(BF16)
    wide = out_ref.shape[1]
    if wide < own_ref.shape[1]:
        local = pl.ds(pl.multiple_of(s_ref[2] * wide, wide), wide)
        weight = jnp.where(s_ref[0] == s_ref[1], own_ref[:, local], rest_ref[:, local])
        out_ref[...] = dot_nn(attn_ref[...], weight)


def cotangent(scal, attn_grad, queries, raw, attn, own, rest, out_width):
    tok, width = queries.shape
    chunks = tok // min(CHUNK, tok)
    return pl.pallas_call(
        cotangent_kernel,
        out_shape=(
            shape_of((tok, width), BF16),
            shape_of((width, DH), BF16),
            shape_of((chunks, width, DH), F32),
            shape_of((tok, out_width), F32),
        ),
        in_specs=smem_then_vmem(6),
        compiler_params=params(16),
        cost_estimate=cost(2 * tok * width * out_width, 16 * queries.size),
    )(scal, attn_grad, queries, raw, attn, own, rest)


def weight_grad_kernel(s_ref, attn_ref, grad_ref, other_ref, other_grad_ref, out_hbm, out_buf, sems):
    tok, width = attn_ref.shape
    blocks, _, block = out_buf.shape
    attn_t = attn_ref[...].T
    others_t = [other_ref[lo : lo + tok, :].T for lo in range(0, other_ref.shape[0], tok)]
    moves = []
    for j in range(blocks):
        here = slice(j * block, (j + 1) * block)
        place = s_ref[0] * (blocks * block) + j * block
        part = grad_ref[:, pl.ds(pl.multiple_of(place, block), block)]
        acc = dot_nn(attn_t, part).astype(BF16).astype(F32)
        for k, other_t in enumerate(others_t):
            part = other_grad_ref[k * tok : (k + 1) * tok, here]
            acc += dot_nn(other_t, part).astype(BF16).astype(F32)
        out_buf[j] = acc
        moves.append(pltpu.make_async_copy(out_buf.at[j], out_hbm.at[:, here], sems.at[j]))
        moves[-1].start()
    for move in moves:
        move.wait()


def own_weight_grad(scal, attn, out_grad, other, other_grad):
    width = attn.shape[1]
    own_width = other_grad.shape[1]
    block = min(256, own_width)
    return pl.pallas_call(
        weight_grad_kernel,
        out_shape=shape_of((width, own_width), F32),
        in_specs=smem_then_vmem(4),
        out_specs=pl.BlockSpec(memory_space=pl.ANY),
        scratch_shapes=[
            pltpu.VMEM((own_width // block, width, block), F32),
            pltpu.SemaphoreType.DMA((own_width // block,)),
        ],
        compiler_params=params(16),
        cost_estimate=cost(2 * out_grad.size * width, 4 * out_grad.size),
    )(scal, attn, out_grad, other, other_grad)


def backward_kernel(q_ref, k_ref, v_ref, draw_ref, prefix_ref, suffix_ref, glocal_ref,
                    dq_ref, dk_ref, dv_ref):
    tok, width = q_ref.shape
    chunk = min(CHUNK, tok)
    row = lax.broadcasted_iota(jnp.int32, (chunk, chunk), 0)
    col = lax.broadcasted_iota(jnp.int32, (chunk, chunk), 1)
    lower = row >= col
    upper = row <= col
    for lo in range(0, width, DH):
        cols = slice(lo, lo + DH)
        suffix = suffix_ref[cols, :].astype(F32)
        for i in range(tok // chunk):
            rows = slice(i * chunk, (i + 1) * chunk)
            q = q_ref[rows, cols].astype(F32)
            k = k_ref[rows, cols].astype(F32)
            q_slope = jnp.exp(jnp.minimum(q, 0.0))
            k_slope = jnp.exp(jnp.minimum(k, 0.0))
            fq = jnp.where(q > 0, q + 1.0, q_slope).astype(BF16)
            fk = jnp.where(k > 0, k + 1.0, k_slope).astype(BF16)
            v = v_ref[rows, cols]
            draw = draw_ref[rows, cols]
            later = (suffix + glocal_ref[i, cols, :]).astype(BF16)
            dscores = jnp.where(lower, dot_nt(draw, v), 0.0).astype(BF16)
            dfq = dot_nn(dscores, fk) + dot_nt(draw, prefix_ref[i, cols, :])
            dq_ref[rows, cols] = (dfq * q_slope).astype(BF16)
            dscores_t = jnp.where(upper, dot_nt(v, draw), 0.0).astype(BF16)
            dfk = dot_nn(dscores_t, fq) + dot_nt(v, later)
            dk_ref[rows, cols] = (dfk * k_slope).astype(BF16)
            scores_t = jnp.where(upper, dot_nt(fk, fq), 0.0).astype(BF16)
            dv = dot_nn(scores_t, draw) + dot_nn(fk, later)
            dv_ref[rows, cols] = dv.astype(BF16)


def backward(queries, keys, values, draw, prefix, suffix, glocal):
    out = shape_of(queries.shape, BF16)
    return pl.pallas_call(
        backward_kernel,
        out_shape=(out, out, out),
        compiler_params=params(16),
        cost_estimate=cost(32 * queries.size * DH, 16 * queries.size),
    )(queries, keys, values, draw, prefix, suffix, glocal)


def halves(s_ref, half):
    first = pl.ds(pl.multiple_of(s_ref[3] * half, half), half)
    second = pl.ds(pl.multiple_of((1 - s_ref[3]) * half, half), half)
    return first, second


def project_near_kernel(s_ref, so_far_ref, a1_ref, a2_ref, m1_ref, z1_ref, o1_ref, oz1_ref, out_ref):
    first, second = halves(s_ref, m1_ref.shape[0])
    acc = so_far_ref[...] + dot_nn(a1_ref[:, first], m1_ref[...])
    acc += dot_nn(a1_ref[:, second], z1_ref[...])
    acc += dot_nn(a2_ref[:, first], o1_ref[...])
    acc += dot_nn(a2_ref[:, second], oz1_ref[...])
    out_ref[...] = acc


def project_near(scal, so_far, attns, pieces):
    return pl.pallas_call(
        project_near_kernel,
        out_shape=shape_of(so_far.shape, F32),
        in_specs=smem_then_vmem(7),
        compiler_params=params(16),
        cost_estimate=cost(1000, 1000),
    )(scal, so_far, *attns, *pieces)


def project_far_kernel(s_ref, near_ref, a_ref, d_ref, od_ref, dz_ref, odz_ref, out_hbm, out_buf, sems):
    first, second = halves(s_ref, d_ref.shape[0])
    blocks, _, block = out_buf.shape
    moves = []
    for j in range(blocks):
        here = slice(j * block, (j + 1) * block)
        acc = near_ref[:, here] + dot_nn(a_ref[:, first], d_ref[:, here] + od_ref[:, here])
        acc += dot_nn(a_ref[:, second], dz_ref[:, here] + odz_ref[:, here])
        out_buf[j] = acc.astype(BF16)
        moves.append(pltpu.make_async_copy(out_buf.at[j], out_hbm.at[:, here], sems.at[j]))
        moves[-1].start()
    for move in moves:
        move.wait()


def project_far(scal, near, attn, pieces):
    tok, out_width = near.shape
    block = 256
    return pl.pallas_call(
        project_far_kernel,
        out_shape=shape_of((tok, out_width), BF16),
        in_specs=smem_then_vmem(6),
        out_specs=pl.BlockSpec(memory_space=pl.ANY),
        scratch_shapes=[
            pltpu.VMEM((out_width // block, tok, block), BF16),
            pltpu.SemaphoreType.DMA((out_width // block,)),
        ],
        compiler_params=params(16),
        cost_estimate=cost(1000, 1000),
    )(scal, near, attn, *pieces)


def in_hbm(array):
    return pltpu.with_memory_space_constraint(array, pltpu.HBM)


def after(array, *needed):
    return lax.optimization_barrier((array, *needed))[0]


def shift(array, axis, count, by, wrap):
    pairs = [(i, (i + by) % count) for i in range(count) if wrap or 0 <= i + by < count]
    return lax.ppermute(array, axis, pairs)


def total(arrays):
    if len(arrays) == 1:
        return arrays[0]
    return functools.reduce(jnp.add, [a.astype(F32) for a in arrays])


def body(n_ctx, n_head, n_rep, queries, keys, values, out_weight, out_grad):
    c, h, z = lax.axis_index("ctx"), lax.axis_index("head"), lax.axis_index("rep")
    x, y, p = h & 1, h >> 1, z & 1
    scal = jnp.stack([c, y, x, p]).astype(jnp.int32)
    paired = n_ctx == 2 and n_head == 4 and n_rep % 2 == 0
    own_width = out_weight.shape[1]
    weight_hbm, grad_hbm = in_hbm(out_weight), in_hbm(out_grad)

    if paired:
        group = ("ctx", "head")
        near = [(4 * (i // 2) + i, i ^ 1) for i in range(4)]
        near += [(4 * (1 - i // 2) + i, 4 + (i ^ 2)) for i in range(4)]
        far = [(4 * (1 - i // 2) + i, i ^ 3) for i in range(4)]
        one = [(i, i ^ 1) for i in range(4)] + [(4 + i, 4 + (i ^ 2)) for i in range(4)]
        two = [(i, i ^ 2) for i in range(4)] + [(4 + i, 4 + (i ^ 1)) for i in range(4)]
        zpair = [(i, i ^ 1) for i in range(n_rep)]
        swap = [(0, 1), (1, 0)]
        state, near_piece, far_piece, turn, queries, keys, values = opening(
            scal, in_hbm(queries), in_hbm(keys), in_hbm(values), weight_hbm, grad_hbm
        )
        near_mine = lax.ppermute(near_piece, group, near)
        other_grad = lax.ppermute(turn, "ctx", swap)
    else:
        state = local_state(keys, values)
        other_grad = []
        for k in range(1, n_ctx):
            start = lax.rem(c + k, n_ctx) * own_width
            turn = lax.dynamic_slice_in_dim(out_grad, start, own_width, 1)
            other_grad.append(shift(turn, "ctx", n_ctx, k, True))
        other_grad = jnp.concatenate(other_grad, 0)

    carried = total([shift(state, "ctx", n_ctx, k, False) for k in range(1, n_ctx)])
    rest = [shift(out_weight, "ctx", n_ctx, -k, True) for k in range(1, n_ctx)]
    rest = rest[0] if n_ctx == 2 else jnp.concatenate(rest, 1)
    attn_grad = attn_gradient(scal, out_weight, out_grad, after(rest, state))
    carried = after(carried, attn_grad)
    attn, raw, prefix = forward(queries, keys, values, carried)

    if paired:
        far_mine = lax.ppermute(after(far_piece, attn), group, far)
        attn_1 = lax.ppermute(attn, group, one)
        attn_2 = lax.ppermute(attn, group, two)
        near_z = lax.ppermute(near_mine, "rep", zpair)
        raw = after(raw, near_mine, other_grad)
    other_attn = [shift(attn, "ctx", n_ctx, k, True) for k in range(1, n_ctx)]
    other_attn = other_attn[0] if n_ctx == 2 else jnp.concatenate(other_attn, 0)

    draw, gsum, glocal, own_out = cotangent(
        scal, attn_grad, queries, raw, attn, out_weight, rest, own_width // 2 if paired else own_width
    )
    suffix = total([shift(gsum, "ctx", n_ctx, -k, False) for k in range(1, n_ctx)])

    if paired:
        other_attn = after(other_attn, gsum)

    weight_grad = own_weight_grad(scal, attn, out_grad, other_attn, other_grad)

    if paired:
        far_z = lax.ppermute(after(far_mine, weight_grad), ("ctx", "rep"), zpair)
        near_other = lax.ppermute(after(near_mine, weight_grad), "ctx", swap)
        attn_3 = lax.ppermute(after(attn_1, weight_grad), group, two)
        near_other_z = lax.ppermute(after(near_z, weight_grad), "ctx", swap)
        suffix = after(suffix, weight_grad, attn_1, attn_2, near_z)

    query_grad, key_grad, value_grad = backward(queries, keys, values, draw, prefix, suffix, glocal)

    if paired:
        far_other = lax.ppermute(after(far_mine, weight_grad), "ctx", [(0, 1)])
        near_out = project_near(
            scal, after(own_out, query_grad), (attn_1, attn_2),
            (near_mine, near_z, near_other, near_other_z),
        )
        last = after(far_z, near_out, attn_3, far_other)
        far_other_z = lax.ppermute(last, "ctx", [(0, 1)])
        layer_out = project_far(scal, near_out, attn_3, (far_mine, far_other, far_z, far_other_z))
    else:
        full = lax.all_gather(out_weight, "ctx", axis=1, tiled=True)
        partial_out = jnp.dot(attn, full, preferred_element_type=F32).astype(BF16)
        layer_out = lax.psum_scatter(partial_out, "head", scatter_dimension=1, tiled=True)
    return layer_out, query_grad, key_grad, value_grad, weight_grad


def solution(mesh):
    tokens = P(("rep", "ctx"), "head")
    sizes = mesh.shape["ctx"], mesh.shape["head"], mesh.shape["rep"]
    return jax.shard_map(
        functools.partial(body, *sizes),
        mesh=mesh,
        in_specs=(tokens, tokens, tokens, P("head", "ctx"), P(("rep", "ctx"), None)),
        out_specs=(tokens, tokens, tokens, tokens, P(("rep", "head"), "ctx")),
        check_vma=False,
    )
```

```python
import functools

import jax
import jax.numpy as jnp
from jax import lax
from jax.experimental import pallas as pl
from jax.experimental.pallas import tpu as pltpu
from jax.sharding import PartitionSpec as P

DH = 128
CHUNK = 256
EPS = 1e-06
F32 = jnp.float32
BF16 = jnp.bfloat16


def feature(x):
    return jnp.where(x > 0, x + 1.0, jnp.exp(jnp.minimum(x, 0.0)))


def dot_nn(a, b):
    return lax.dot_general(a, b, (((1,), (0,)), ((), ())), preferred_element_type=F32)


def dot_nt(a, b):
    return lax.dot_general(a, b, (((1,), (1,)), ((), ())), preferred_element_type=F32)


def dot_tn(a, b):
    return lax.dot_general(a, b, (((0,), (0,)), ((), ())), preferred_element_type=F32)


def shape_of(shape, dtype):
    return jax.ShapeDtypeStruct(shape, dtype)


def params(mib):
    return pltpu.CompilerParams(vmem_limit_bytes=mib * 1024 * 1024)


def cost(flops, moved):
    return pl.CostEstimate(flops=flops, transcendentals=0, bytes_accessed=moved)


def state_kernel(k_ref, v_ref, out_ref):
    for lo in range(0, k_ref.shape[1], DH):
        cols = slice(lo, lo + DH)
        fk = feature(k_ref[:, cols].astype(F32)).astype(BF16)
        out_ref[cols, :] = dot_tn(fk, v_ref[:, cols]).astype(BF16)


def local_state(keys, values):
    width = keys.shape[1]
    return pl.pallas_call(
        state_kernel,
        out_shape=shape_of((width, DH), BF16),
        compiler_params=params(16),
        cost_estimate=cost(2 * keys.size * DH, 4 * keys.size),
    )(keys, values)


def first_slices_kernel(s_ref, weight_hbm, grad_hbm, near_ref, turn_ref, sems):
    half, wide = near_ref.shape
    rows = pl.ds(pl.multiple_of(s_ref[3] * half, half), half)
    column = jnp.where(s_ref[0] == s_ref[1], 1 - s_ref[2], s_ref[2])
    cols = pl.ds(pl.multiple_of(column * wide, wide), wide)
    near_move = pltpu.make_async_copy(weight_hbm.at[rows, cols], near_ref, sems.at[0])
    near_move.start()
    own = turn_ref.shape[1]
    cols = pl.ds(pl.multiple_of((1 - s_ref[0]) * own, own), own)
    turn_move = pltpu.make_async_copy(grad_hbm.at[:, cols], turn_ref, sems.at[1])
    turn_move.start()
    near_move.wait()
    turn_move.wait()


def first_slices(scal, weight, out_grad):
    hbm = pl.BlockSpec(memory_space=pltpu.HBM)
    vmem = pl.BlockSpec(memory_space=pltpu.VMEM)
    return pl.pallas_call(
        first_slices_kernel,
        out_shape=(
            shape_of((weight.shape[0] // 2, weight.shape[1] // 2), BF16),
            shape_of((out_grad.shape[0], weight.shape[1]), BF16),
        ),
        in_specs=[pl.BlockSpec(memory_space=pltpu.SMEM), hbm, hbm],
        out_specs=(vmem, vmem),
        scratch_shapes=[pltpu.SemaphoreType.DMA((2,))],
        compiler_params=params(16),
        cost_estimate=cost(1000, 1000),
    )(scal, weight, out_grad)


def opening_kernel(s_ref, q_hbm, k_hbm, v_hbm, weight_hbm,
                   state_ref, far_ref, q_ref, k_ref, v_ref, sems, slice_sems):
    half, wide = far_ref.shape
    rows = pl.ds(pl.multiple_of(s_ref[3] * half, half), half)
    loads = []
    for i, lo in enumerate(range(0, k_hbm.shape[1], DH)):
        cols = pl.ds(lo, DH)
        loads.append([
            pltpu.make_async_copy(k_hbm.at[:, cols], k_ref.at[:, cols], sems.at[0, i]),
            pltpu.make_async_copy(v_hbm.at[:, cols], v_ref.at[:, cols], sems.at[1, i]),
        ])
        loads[-1][0].start()
        loads[-1][1].start()
    cols = pl.ds(pl.multiple_of((1 - s_ref[2]) * wide, wide), wide)
    moves = [pltpu.make_async_copy(weight_hbm.at[rows, cols], far_ref, slice_sems.at[0])]
    moves[-1].start()
    moves.append(pltpu.make_async_copy(q_hbm, q_ref, slice_sems.at[1]))
    moves[-1].start()
    for i, lo in enumerate(range(0, k_hbm.shape[1], DH)):
        cols = slice(lo, lo + DH)
        loads[i][0].wait()
        loads[i][1].wait()
        fk = feature(k_ref[:, cols].astype(F32)).astype(BF16)
        state_ref[cols, :] = dot_tn(fk, v_ref[:, cols]).astype(BF16)
    for move in moves:
        move.wait()


def opening(scal, queries, keys, values, weight):
    width = keys.shape[1]
    piece = shape_of((weight.shape[0] // 2, weight.shape[1] // 2), BF16)
    hbm = pl.BlockSpec(memory_space=pltpu.HBM)
    vmem = pl.BlockSpec(memory_space=pltpu.VMEM)
    return pl.pallas_call(
        opening_kernel,
        out_shape=(shape_of((width, DH), BF16), piece)
        + (shape_of(keys.shape, BF16),) * 3,
        in_specs=[pl.BlockSpec(memory_space=pltpu.SMEM)] + [hbm] * 4,
        out_specs=(vmem,) * 5,
        scratch_shapes=[
            pltpu.SemaphoreType.DMA((2, width // DH)),
            pltpu.SemaphoreType.DMA((2,)),
        ],
        compiler_params=params(16),
        cost_estimate=cost(2 * keys.size * DH, 4 * keys.size),
    )(scal, queries, keys, values, weight)


def forward_kernel(q_ref, k_ref, v_ref, carried_ref, attn_ref, attn_t_ref, raw_ref, prefix_ref):
    tok, width = q_ref.shape
    chunk = min(CHUNK, tok)
    row = lax.broadcasted_iota(jnp.int32, (chunk, chunk), 0)
    col = lax.broadcasted_iota(jnp.int32, (chunk, chunk), 1)
    lower = row >= col
    for lo in range(0, width, DH):
        cols = slice(lo, lo + DH)
        prefix = carried_ref[cols, :].astype(F32)
        for i in range(tok // chunk):
            rows = slice(i * chunk, (i + 1) * chunk)
            fq = feature(q_ref[rows, cols].astype(F32)).astype(BF16)
            fk = feature(k_ref[rows, cols].astype(F32)).astype(BF16)
            v = v_ref[rows, cols]
            low_prefix = prefix.astype(BF16)
            prefix_ref[i, cols, :] = low_prefix
            scores = jnp.where(lower, dot_nt(fq, fk), 0.0).astype(BF16)
            raw = dot_nn(scores, v) + dot_nn(fq, low_prefix)
            raw_ref[rows, cols] = raw
            inv = lax.rsqrt(jnp.mean(raw * raw, axis=-1, keepdims=True) + EPS)
            attn = (raw * inv).astype(BF16)
            attn_ref[rows, cols] = attn
            attn_t_ref[cols, rows] = attn.T
            if i + 1 < tok // chunk:
                prefix = prefix + dot_tn(fk, v)


def forward(queries, keys, values, carried):
    tok, width = queries.shape
    chunks = tok // min(CHUNK, tok)
    return pl.pallas_call(
        forward_kernel,
        out_shape=(
            shape_of((tok, width), BF16),
            shape_of((width, tok), BF16),
            shape_of((tok, width), F32),
            shape_of((chunks, width, DH), BF16),
        ),
        compiler_params=params(16),
        cost_estimate=cost(16 * queries.size * DH, 12 * queries.size),
    )(queries, keys, values, carried)


def smem_then_vmem(count):
    return [pl.BlockSpec(memory_space=pltpu.SMEM)] + [pl.BlockSpec(memory_space=pltpu.VMEM)] * count


def attn_grad_kernel(s_ref, own_ref, grad_ref, rest_ref, out_ref, acc_ref):
    own_width, rest_width = own_ref.shape[1], rest_ref.shape[1]
    count = (own_width + rest_width) // own_width

    def part(k):
        place = lax.rem(s_ref[0] + k, count) * own_width
        return grad_ref[:, pl.ds(pl.multiple_of(place, own_width), own_width)]

    acc_ref[...] = dot_nt(part(0), own_ref[...])
    for k in range(1, count):
        acc_ref[...] += dot_nt(part(k), rest_ref[:, (k - 1) * own_width : k * own_width])
    out_ref[...] = acc_ref[...].astype(BF16)


def attn_gradient(scal, weight, out_grad, rest):
    tok, width = out_grad.shape[0], weight.shape[0]
    return pl.pallas_call(
        attn_grad_kernel,
        out_shape=shape_of((tok, width), BF16),
        in_specs=smem_then_vmem(3),
        scratch_shapes=[pltpu.VMEM((tok, width), F32)],
        compiler_params=params(16),
        cost_estimate=cost(2 * out_grad.size * width, 4 * out_grad.size),
    )(scal, weight, out_grad, rest)


def cotangent_kernel(s_ref, attn_grad_ref, q_ref, raw_ref, attn_ref, own_ref, rest_ref,
                     draw_ref, gsum_ref, glocal_ref, out_ref):
    tok, width = q_ref.shape
    chunk = min(CHUNK, tok)
    for lo in range(0, width, DH):
        cols = slice(lo, lo + DH)
        later = jnp.zeros((DH, DH), F32)
        for i in reversed(range(tok // chunk)):
            rows = slice(i * chunk, (i + 1) * chunk)
            glocal_ref[i, cols, :] = later
            grad = attn_grad_ref[rows, cols].astype(F32)
            raw = raw_ref[rows, cols]
            inv = lax.rsqrt(jnp.mean(raw * raw, axis=-1, keepdims=True) + EPS)
            normed = raw * inv
            mean = jnp.mean(grad * normed, axis=-1, keepdims=True)
            draw = (inv * (grad - normed * mean)).astype(BF16)
            draw_ref[rows, cols] = draw
            fq = feature(q_ref[rows, cols].astype(F32)).astype(BF16)
            later = later + dot_tn(fq, draw)
        gsum_ref[cols, :] = later.astype(BF16)
    wide = out_ref.shape[1]
    if wide < own_ref.shape[1]:
        local = pl.ds(pl.multiple_of(s_ref[2] * wide, wide), wide)
        weight = jnp.where(s_ref[0] == s_ref[1], own_ref[:, local], rest_ref[:, local])
        out_ref[...] = dot_nn(attn_ref[...], weight)


def cotangent(scal, attn_grad, queries, raw, attn, own, rest, out_width):
    tok, width = queries.shape
    chunks = tok // min(CHUNK, tok)
    return pl.pallas_call(
        cotangent_kernel,
        out_shape=(
            shape_of((tok, width), BF16),
            shape_of((width, DH), BF16),
            shape_of((chunks, width, DH), F32),
            shape_of((tok, out_width), F32),
        ),
        in_specs=smem_then_vmem(6),
        compiler_params=params(16),
        cost_estimate=cost(2 * tok * width * out_width, 16 * queries.size),
    )(scal, attn_grad, queries, raw, attn, own, rest)


def weight_grad_kernel(s_ref, attn_t_ref, grad_ref, other_t_ref, other_grad_ref, out_hbm, out_buf, sems):
    width, tok = attn_t_ref.shape
    blocks, _, block = out_buf.shape
    moves = []
    for j in range(blocks):
        here = slice(j * block, (j + 1) * block)
        place = s_ref[0] * (blocks * block) + j * block
        part = grad_ref[:, pl.ds(pl.multiple_of(place, block), block)]
        acc = dot_nn(attn_t_ref[...], part).astype(BF16).astype(F32)
        for k in range(other_t_ref.shape[0] // width):
            other_t = other_t_ref[k * width : (k + 1) * width, :]
            part = other_grad_ref[k * tok : (k + 1) * tok, here]
            acc += dot_nn(other_t, part).astype(BF16).astype(F32)
        out_buf[j] = acc
        moves.append(pltpu.make_async_copy(out_buf.at[j], out_hbm.at[:, here], sems.at[j]))
        moves[-1].start()
    for move in moves:
        move.wait()


def own_weight_grad(scal, attn_t, out_grad, other_t, other_grad):
    width = attn_t.shape[0]
    own_width = other_grad.shape[1]
    block = min(256, own_width)
    return pl.pallas_call(
        weight_grad_kernel,
        out_shape=shape_of((width, own_width), F32),
        in_specs=smem_then_vmem(4),
        out_specs=pl.BlockSpec(memory_space=pl.ANY),
        scratch_shapes=[
            pltpu.VMEM((own_width // block, width, block), F32),
            pltpu.SemaphoreType.DMA((own_width // block,)),
        ],
        compiler_params=params(16),
        cost_estimate=cost(2 * out_grad.size * width, 4 * out_grad.size),
    )(scal, attn_t, out_grad, other_t, other_grad)


def backward_kernel(q_ref, k_ref, v_ref, draw_ref, prefix_ref, suffix_ref, glocal_ref,
                    dq_ref, dk_ref, dv_ref):
    tok, width = q_ref.shape
    chunk = min(CHUNK, tok)
    row = lax.broadcasted_iota(jnp.int32, (chunk, chunk), 0)
    col = lax.broadcasted_iota(jnp.int32, (chunk, chunk), 1)
    lower = row >= col
    upper = row <= col
    for lo in range(0, width, DH):
        cols = slice(lo, lo + DH)
        suffix = suffix_ref[cols, :].astype(F32)
        for i in range(tok // chunk):
            rows = slice(i * chunk, (i + 1) * chunk)
            q = q_ref[rows, cols].astype(F32)
            k = k_ref[rows, cols].astype(F32)
            q_slope = jnp.exp(jnp.minimum(q, 0.0))
            k_slope = jnp.exp(jnp.minimum(k, 0.0))
            fq = jnp.where(q > 0, q + 1.0, q_slope).astype(BF16)
            fk = jnp.where(k > 0, k + 1.0, k_slope).astype(BF16)
            v = v_ref[rows, cols]
            draw = draw_ref[rows, cols]
            later = (suffix + glocal_ref[i, cols, :]).astype(BF16)
            dscores = jnp.where(lower, dot_nt(draw, v), 0.0).astype(BF16)
            dfq = dot_nn(dscores, fk) + dot_nt(draw, prefix_ref[i, cols, :])
            dq_ref[rows, cols] = (dfq * q_slope).astype(BF16)
            dscores_t = jnp.where(upper, dot_nt(v, draw), 0.0).astype(BF16)
            dfk = dot_nn(dscores_t, fq) + dot_nt(v, later)
            dk_ref[rows, cols] = (dfk * k_slope).astype(BF16)
            scores_t = jnp.where(upper, dot_nt(fk, fq), 0.0).astype(BF16)
            dv = dot_nn(scores_t, draw) + dot_nn(fk, later)
            dv_ref[rows, cols] = dv.astype(BF16)


def backward(queries, keys, values, draw, prefix, suffix, glocal):
    out = shape_of(queries.shape, BF16)
    return pl.pallas_call(
        backward_kernel,
        out_shape=(out, out, out),
        compiler_params=params(16),
        cost_estimate=cost(32 * queries.size * DH, 16 * queries.size),
    )(queries, keys, values, draw, prefix, suffix, glocal)


def halves(s_ref, half):
    first = pl.ds(pl.multiple_of(s_ref[3] * half, half), half)
    second = pl.ds(pl.multiple_of((1 - s_ref[3]) * half, half), half)
    return first, second


def project_near_kernel(s_ref, so_far_ref, a1_ref, a2_ref, m1_ref, z1_ref, o1_ref, oz1_ref, out_ref):
    first, second = halves(s_ref, m1_ref.shape[0])
    acc = so_far_ref[...] + dot_nn(a1_ref[:, first], m1_ref[...])
    acc += dot_nn(a1_ref[:, second], z1_ref[...])
    acc += dot_nn(a2_ref[:, first], o1_ref[...])
    acc += dot_nn(a2_ref[:, second], oz1_ref[...])
    out_ref[...] = acc


def project_near(scal, so_far, attns, pieces):
    return pl.pallas_call(
        project_near_kernel,
        out_shape=shape_of(so_far.shape, F32),
        in_specs=smem_then_vmem(7),
        compiler_params=params(16),
        cost_estimate=cost(1000, 1000),
    )(scal, so_far, *attns, *pieces)


def project_far_kernel(s_ref, near_ref, a_ref, d_ref, od_ref, dz_ref, odz_ref, out_hbm, out_buf, sems):
    first, second = halves(s_ref, d_ref.shape[0])
    blocks, _, block = out_buf.shape
    moves = []
    for j in range(blocks):
        here = slice(j * block, (j + 1) * block)
        acc = near_ref[:, here] + dot_nn(a_ref[:, first], d_ref[:, here] + od_ref[:, here])
        acc += dot_nn(a_ref[:, second], dz_ref[:, here] + odz_ref[:, here])
        out_buf[j] = acc.astype(BF16)
        moves.append(pltpu.make_async_copy(out_buf.at[j], out_hbm.at[:, here], sems.at[j]))
        moves[-1].start()
    for move in moves:
        move.wait()


def project_far(scal, near, attn, pieces):
    tok, out_width = near.shape
    block = 256
    return pl.pallas_call(
        project_far_kernel,
        out_shape=shape_of((tok, out_width), BF16),
        in_specs=smem_then_vmem(6),
        out_specs=pl.BlockSpec(memory_space=pl.ANY),
        scratch_shapes=[
            pltpu.VMEM((out_width // block, tok, block), BF16),
            pltpu.SemaphoreType.DMA((out_width // block,)),
        ],
        compiler_params=params(16),
        cost_estimate=cost(1000, 1000),
    )(scal, near, attn, *pieces)


def in_hbm(array):
    return pltpu.with_memory_space_constraint(array, pltpu.HBM)


def after(array, *needed):
    return lax.optimization_barrier((array, *needed))[0]


def shift(array, axis, count, by, wrap):
    pairs = [(i, (i + by) % count) for i in range(count) if wrap or 0 <= i + by < count]
    return lax.ppermute(array, axis, pairs)


def total(arrays):
    if len(arrays) == 1:
        return arrays[0]
    return functools.reduce(jnp.add, [a.astype(F32) for a in arrays])


def body(n_ctx, n_head, n_rep, queries, keys, values, out_weight, out_grad):
    c, h, z = lax.axis_index("ctx"), lax.axis_index("head"), lax.axis_index("rep")
    x, y, p = h & 1, h >> 1, z & 1
    scal = jnp.stack([c, y, x, p]).astype(jnp.int32)
    paired = n_ctx == 2 and n_head == 4 and n_rep % 2 == 0
    own_width = out_weight.shape[1]
    weight_hbm, grad_hbm = in_hbm(out_weight), in_hbm(out_grad)

    if paired:
        group = ("ctx", "head")
        near = [(4 * (i // 2) + i, i ^ 1) for i in range(4)]
        near += [(4 * (1 - i // 2) + i, 4 + (i ^ 2)) for i in range(4)]
        far = [(4 * (1 - i // 2) + i, i ^ 3) for i in range(4)]
        one = [(i, i ^ 1) for i in range(4)] + [(4 + i, 4 + (i ^ 2)) for i in range(4)]
        two = [(i, i ^ 2) for i in range(4)] + [(4 + i, 4 + (i ^ 1)) for i in range(4)]
        zpair = [(i, i ^ 1) for i in range(n_rep)]
        swap = [(0, 1), (1, 0)]
        near_piece, turn = first_slices(scal, weight_hbm, grad_hbm)
        near_mine = lax.ppermute(near_piece, group, near)
        state, far_piece, queries, keys, values = opening(
            after(scal, near_piece), in_hbm(queries), in_hbm(keys), in_hbm(values), weight_hbm
        )
        other_grad = lax.ppermute(turn, "ctx", swap)
    else:
        state = local_state(keys, values)
        other_grad = []
        for k in range(1, n_ctx):
            start = lax.rem(c + k, n_ctx) * own_width
            turn = lax.dynamic_slice_in_dim(out_grad, start, own_width, 1)
            other_grad.append(shift(turn, "ctx", n_ctx, k, True))
        other_grad = jnp.concatenate(other_grad, 0)

    carried = total([shift(state, "ctx", n_ctx, k, False) for k in range(1, n_ctx)])
    rest = [shift(out_weight, "ctx", n_ctx, -k, True) for k in range(1, n_ctx)]
    rest = rest[0] if n_ctx == 2 else jnp.concatenate(rest, 1)
    attn_grad = attn_gradient(scal, out_weight, out_grad, after(rest, state))
    carried = after(carried, attn_grad)
    if paired:
        far_mine = lax.ppermute(after(far_piece, attn_grad, near_mine), group, far)
        carried = after(carried, near_mine)
    attn, attn_t, raw, prefix = forward(queries, keys, values, carried)

    if paired:
        attn_1 = lax.ppermute(attn, group, one)
        attn_2 = lax.ppermute(attn, group, two)
        near_z = lax.ppermute(near_mine, "rep", zpair)
        raw = after(raw, near_mine, other_grad)
    other_attn = [shift(attn_t, "ctx", n_ctx, k, True) for k in range(1, n_ctx)]
    other_attn = other_attn[0] if n_ctx == 2 else jnp.concatenate(other_attn, 0)

    draw, gsum, glocal, own_out = cotangent(
        scal, attn_grad, queries, raw, attn, out_weight, rest, own_width // 2 if paired else own_width
    )
    suffix = total([shift(gsum, "ctx", n_ctx, -k, False) for k in range(1, n_ctx)])

    if paired:
        far_z = lax.ppermute(after(far_mine, gsum), ("ctx", "rep"), zpair)
        other_attn = after(other_attn, gsum, far_mine)

    weight_grad = own_weight_grad(scal, attn_t, out_grad, other_attn, other_grad)

    if paired:
        near_other = lax.ppermute(after(near_mine, weight_grad), "ctx", swap)
        attn_3 = lax.ppermute(after(attn_1, weight_grad), group, two)
        near_other_z = lax.ppermute(after(near_z, weight_grad), "ctx", swap)
        suffix = after(suffix, weight_grad, attn_1, attn_2, near_z)

    query_grad, key_grad, value_grad = backward(queries, keys, values, draw, prefix, suffix, glocal)

    if paired:
        far_other = lax.ppermute(after(far_mine, weight_grad), "ctx", [(0, 1)])
        far_other_z = lax.ppermute(after(far_z, query_grad), "ctx", [(0, 1)])
        near_out = project_near(
            scal, after(own_out, query_grad, attn_3), (attn_1, attn_2),
            (near_mine, near_z, near_other, near_other_z),
        )
        layer_out = project_far(scal, near_out, attn_3, (far_mine, far_other, far_z, far_other_z))
    else:
        full = lax.all_gather(out_weight, "ctx", axis=1, tiled=True)
        partial_out = jnp.dot(attn, full, preferred_element_type=F32).astype(BF16)
        layer_out = lax.psum_scatter(partial_out, "head", scatter_dimension=1, tiled=True)
    return layer_out, query_grad, key_grad, value_grad, weight_grad


def solution(mesh):
    tokens = P(("rep", "ctx"), "head")
    sizes = mesh.shape["ctx"], mesh.shape["head"], mesh.shape["rep"]
    return jax.shard_map(
        functools.partial(body, *sizes),
        mesh=mesh,
        in_specs=(tokens, tokens, tokens, P("head", "ctx"), P(("rep", "ctx"), None)),
        out_specs=(tokens, tokens, tokens, tokens, P(("rep", "head"), "ctx")),
        check_vma=False,
    )
```

```python
import functools

import jax
import jax.numpy as jnp
from jax import lax
from jax.experimental import pallas as pl
from jax.experimental.pallas import tpu as pltpu
from jax.sharding import PartitionSpec as P

DH = 128
CHUNK = 256
EPS = 1e-06
F32 = jnp.float32
BF16 = jnp.bfloat16


def feature(x):
    return jnp.where(x > 0, x + 1.0, jnp.exp(jnp.minimum(x, 0.0)))


def dot_nn(a, b):
    return lax.dot_general(a, b, (((1,), (0,)), ((), ())), preferred_element_type=F32)


def dot_nt(a, b):
    return lax.dot_general(a, b, (((1,), (1,)), ((), ())), preferred_element_type=F32)


def dot_tn(a, b):
    return lax.dot_general(a, b, (((0,), (0,)), ((), ())), preferred_element_type=F32)


def shape_of(shape, dtype):
    return jax.ShapeDtypeStruct(shape, dtype)


def params(mib):
    return pltpu.CompilerParams(vmem_limit_bytes=mib * 1024 * 1024)


def cost(flops, moved):
    return pl.CostEstimate(flops=flops, transcendentals=0, bytes_accessed=moved)


def state_kernel(k_ref, v_ref, out_ref):
    for lo in range(0, k_ref.shape[1], DH):
        cols = slice(lo, lo + DH)
        fk = feature(k_ref[:, cols].astype(F32)).astype(BF16)
        out_ref[cols, :] = dot_tn(fk, v_ref[:, cols]).astype(BF16)


def local_state(keys, values):
    width = keys.shape[1]
    return pl.pallas_call(
        state_kernel,
        out_shape=shape_of((width, DH), BF16),
        compiler_params=params(16),
        cost_estimate=cost(2 * keys.size * DH, 4 * keys.size),
    )(keys, values)


def opening_kernel(s_ref, q_hbm, k_hbm, v_hbm, weight_hbm, grad_hbm,
                   state_ref, near_ref, far_ref, turn_ref, q_ref, k_ref, v_ref, sems, slice_sems):
    half, wide = near_ref.shape
    rows = pl.ds(pl.multiple_of(s_ref[3] * half, half), half)
    far_column = 1 - s_ref[2]
    near_column = jnp.where(s_ref[0] == s_ref[1], far_column, s_ref[2])
    loads = []
    for i, lo in enumerate(range(0, k_hbm.shape[1], DH)):
        cols = pl.ds(lo, DH)
        loads.append([
            pltpu.make_async_copy(k_hbm.at[:, cols], k_ref.at[:, cols], sems.at[0, i]),
            pltpu.make_async_copy(v_hbm.at[:, cols], v_ref.at[:, cols], sems.at[1, i]),
        ])
        loads[-1][0].start()
        loads[-1][1].start()
    moves = []
    for i, (column, ref) in enumerate([(near_column, near_ref), (far_column, far_ref)]):
        cols = pl.ds(pl.multiple_of(column * wide, wide), wide)
        moves.append(pltpu.make_async_copy(weight_hbm.at[rows, cols], ref, slice_sems.at[i]))
        moves[-1].start()
    moves.append(pltpu.make_async_copy(q_hbm, q_ref, slice_sems.at[2]))
    moves[-1].start()
    own = turn_ref.shape[1]
    cols = pl.ds(pl.multiple_of((1 - s_ref[0]) * own, own), own)
    moves.append(pltpu.make_async_copy(grad_hbm.at[:, cols], turn_ref, slice_sems.at[3]))
    moves[-1].start()
    for i, lo in enumerate(range(0, k_hbm.shape[1], DH)):
        cols = slice(lo, lo + DH)
        loads[i][0].wait()
        loads[i][1].wait()
        fk = feature(k_ref[:, cols].astype(F32)).astype(BF16)
        state_ref[cols, :] = dot_tn(fk, v_ref[:, cols]).astype(BF16)
    for move in moves:
        move.wait()


def opening(scal, queries, keys, values, weight, out_grad):
    tok, width = keys.shape
    piece = shape_of((weight.shape[0] // 2, weight.shape[1] // 2), BF16)
    hbm = pl.BlockSpec(memory_space=pltpu.HBM)
    vmem = pl.BlockSpec(memory_space=pltpu.VMEM)
    return pl.pallas_call(
        opening_kernel,
        out_shape=(shape_of((width, DH), BF16), piece, piece, shape_of((tok, weight.shape[1]), BF16))
        + (shape_of(keys.shape, BF16),) * 3,
        in_specs=[pl.BlockSpec(memory_space=pltpu.SMEM)] + [hbm] * 5,
        out_specs=(vmem,) * 7,
        scratch_shapes=[
            pltpu.SemaphoreType.DMA((2, width // DH)),
            pltpu.SemaphoreType.DMA((4,)),
        ],
        compiler_params=params(16),
        cost_estimate=cost(2 * keys.size * DH, 4 * keys.size),
    )(scal, queries, keys, values, weight, out_grad)


def forward_kernel(q_ref, k_ref, v_ref, carried_ref, attn_ref, attn_t_ref, raw_ref, prefix_ref):
    tok, width = q_ref.shape
    chunk = min(CHUNK, tok)
    row = lax.broadcasted_iota(jnp.int32, (chunk, chunk), 0)
    col = lax.broadcasted_iota(jnp.int32, (chunk, chunk), 1)
    lower = row >= col
    for lo in range(0, width, DH):
        cols = slice(lo, lo + DH)
        prefix = carried_ref[cols, :].astype(F32)
        for i in range(tok // chunk):
            rows = slice(i * chunk, (i + 1) * chunk)
            fq = feature(q_ref[rows, cols].astype(F32)).astype(BF16)
            fk = feature(k_ref[rows, cols].astype(F32)).astype(BF16)
            v = v_ref[rows, cols]
            low_prefix = prefix.astype(BF16)
            prefix_ref[i, cols, :] = low_prefix
            scores = jnp.where(lower, dot_nt(fq, fk), 0.0).astype(BF16)
            raw = dot_nn(scores, v) + dot_nn(fq, low_prefix)
            raw_ref[rows, cols] = raw
            inv = lax.rsqrt(jnp.mean(raw * raw, axis=-1, keepdims=True) + EPS)
            attn = (raw * inv).astype(BF16)
            attn_ref[rows, cols] = attn
            attn_t_ref[cols, rows] = attn.T
            if i + 1 < tok // chunk:
                prefix = prefix + dot_tn(fk, v)


def forward(queries, keys, values, carried):
    tok, width = queries.shape
    chunks = tok // min(CHUNK, tok)
    return pl.pallas_call(
        forward_kernel,
        out_shape=(
            shape_of((tok, width), BF16),
            shape_of((width, tok), BF16),
            shape_of((tok, width), F32),
            shape_of((chunks, width, DH), BF16),
        ),
        compiler_params=params(16),
        cost_estimate=cost(16 * queries.size * DH, 12 * queries.size),
    )(queries, keys, values, carried)


def smem_then_vmem(count):
    return [pl.BlockSpec(memory_space=pltpu.SMEM)] + [pl.BlockSpec(memory_space=pltpu.VMEM)] * count


def attn_grad_kernel(s_ref, own_ref, grad_ref, rest_ref, out_ref, acc_ref):
    own_width, rest_width = own_ref.shape[1], rest_ref.shape[1]
    count = (own_width + rest_width) // own_width

    def part(k):
        place = lax.rem(s_ref[0] + k, count) * own_width
        return grad_ref[:, pl.ds(pl.multiple_of(place, own_width), own_width)]

    acc_ref[...] = dot_nt(part(0), own_ref[...])
    for k in range(1, count):
        acc_ref[...] += dot_nt(part(k), rest_ref[:, (k - 1) * own_width : k * own_width])
    out_ref[...] = acc_ref[...].astype(BF16)


def attn_gradient(scal, weight, out_grad, rest):
    tok, width = out_grad.shape[0], weight.shape[0]
    return pl.pallas_call(
        attn_grad_kernel,
        out_shape=shape_of((tok, width), BF16),
        in_specs=smem_then_vmem(3),
        scratch_shapes=[pltpu.VMEM((tok, width), F32)],
        compiler_params=params(16),
        cost_estimate=cost(2 * out_grad.size * width, 4 * out_grad.size),
    )(scal, weight, out_grad, rest)


def cotangent_kernel(s_ref, attn_grad_ref, q_ref, raw_ref, attn_ref, own_ref, rest_ref,
                     draw_ref, gsum_ref, glocal_ref, out_ref):
    tok, width = q_ref.shape
    chunk = min(CHUNK, tok)
    for lo in range(0, width, DH):
        cols = slice(lo, lo + DH)
        later = jnp.zeros((DH, DH), F32)
        for i in reversed(range(tok // chunk)):
            rows = slice(i * chunk, (i + 1) * chunk)
            glocal_ref[i, cols, :] = later
            grad = attn_grad_ref[rows, cols].astype(F32)
            raw = raw_ref[rows, cols]
            inv = lax.rsqrt(jnp.mean(raw * raw, axis=-1, keepdims=True) + EPS)
            normed = raw * inv
            mean = jnp.mean(grad * normed, axis=-1, keepdims=True)
            draw = (inv * (grad - normed * mean)).astype(BF16)
            draw_ref[rows, cols] = draw
            fq = feature(q_ref[rows, cols].astype(F32)).astype(BF16)
            later = later + dot_tn(fq, draw)
        gsum_ref[cols, :] = later.astype(BF16)
    wide = out_ref.shape[1]
    if wide < own_ref.shape[1]:
        local = pl.ds(pl.multiple_of(s_ref[2] * wide, wide), wide)
        weight = jnp.where(s_ref[0] == s_ref[1], own_ref[:, local], rest_ref[:, local])
        out_ref[...] = dot_nn(attn_ref[...], weight)


def cotangent(scal, attn_grad, queries, raw, attn, own, rest, out_width):
    tok, width = queries.shape
    chunks = tok // min(CHUNK, tok)
    return pl.pallas_call(
        cotangent_kernel,
        out_shape=(
            shape_of((tok, width), BF16),
            shape_of((width, DH), BF16),
            shape_of((chunks, width, DH), F32),
            shape_of((tok, out_width), F32),
        ),
        in_specs=smem_then_vmem(6),
        compiler_params=params(16),
        cost_estimate=cost(2 * tok * width * out_width, 16 * queries.size),
    )(scal, attn_grad, queries, raw, attn, own, rest)


def weight_grad_kernel(s_ref, attn_t_ref, grad_ref, other_t_ref, other_grad_ref, out_hbm, out_buf, sems):
    width, tok = attn_t_ref.shape
    blocks, _, block = out_buf.shape
    moves = []
    for j in range(blocks):
        here = slice(j * block, (j + 1) * block)
        place = s_ref[0] * (blocks * block) + j * block
        part = grad_ref[:, pl.ds(pl.multiple_of(place, block), block)]
        acc = dot_nn(attn_t_ref[...], part).astype(BF16).astype(F32)
        for k in range(other_t_ref.shape[0] // width):
            other_t = other_t_ref[k * width : (k + 1) * width, :]
            part = other_grad_ref[k * tok : (k + 1) * tok, here]
            acc += dot_nn(other_t, part).astype(BF16).astype(F32)
        out_buf[j] = acc
        moves.append(pltpu.make_async_copy(out_buf.at[j], out_hbm.at[:, here], sems.at[j]))
        moves[-1].start()
    for move in moves:
        move.wait()


def own_weight_grad(scal, attn_t, out_grad, other_t, other_grad):
    width = attn_t.shape[0]
    own_width = other_grad.shape[1]
    block = min(512, own_width)
    return pl.pallas_call(
        weight_grad_kernel,
        out_shape=shape_of((width, own_width), F32),
        in_specs=smem_then_vmem(4),
        out_specs=pl.BlockSpec(memory_space=pl.ANY),
        scratch_shapes=[
            pltpu.VMEM((own_width // block, width, block), F32),
            pltpu.SemaphoreType.DMA((own_width // block,)),
        ],
        compiler_params=params(16),
        cost_estimate=cost(2 * out_grad.size * width, 4 * out_grad.size),
    )(scal, attn_t, out_grad, other_t, other_grad)


def backward_kernel(q_ref, k_ref, v_ref, draw_ref, prefix_ref, suffix_ref, glocal_ref,
                    dq_ref, dk_ref, dv_ref):
    tok, width = q_ref.shape
    chunk = min(CHUNK, tok)
    row = lax.broadcasted_iota(jnp.int32, (chunk, chunk), 0)
    col = lax.broadcasted_iota(jnp.int32, (chunk, chunk), 1)
    lower = row >= col
    upper = row <= col
    for lo in range(0, width, DH):
        cols = slice(lo, lo + DH)
        suffix = suffix_ref[cols, :].astype(F32)
        for i in range(tok // chunk):
            rows = slice(i * chunk, (i + 1) * chunk)
            q = q_ref[rows, cols].astype(F32)
            k = k_ref[rows, cols].astype(F32)
            q_slope = jnp.exp(jnp.minimum(q, 0.0))
            k_slope = jnp.exp(jnp.minimum(k, 0.0))
            fq = jnp.where(q > 0, q + 1.0, q_slope).astype(BF16)
            fk = jnp.where(k > 0, k + 1.0, k_slope).astype(BF16)
            v = v_ref[rows, cols]
            draw = draw_ref[rows, cols]
            later = (suffix + glocal_ref[i, cols, :]).astype(BF16)
            dscores = jnp.where(lower, dot_nt(draw, v), 0.0).astype(BF16)
            dfq = dot_nn(dscores, fk) + dot_nt(draw, prefix_ref[i, cols, :])
            dq_ref[rows, cols] = (dfq * q_slope).astype(BF16)
            dscores_t = jnp.where(upper, dot_nt(v, draw), 0.0).astype(BF16)
            dfk = dot_nn(dscores_t, fq) + dot_nt(v, later)
            dk_ref[rows, cols] = (dfk * k_slope).astype(BF16)
            scores_t = jnp.where(upper, dot_nt(fk, fq), 0.0).astype(BF16)
            dv = dot_nn(scores_t, draw) + dot_nn(fk, later)
            dv_ref[rows, cols] = dv.astype(BF16)


def backward(queries, keys, values, draw, prefix, suffix, glocal):
    out = shape_of(queries.shape, BF16)
    return pl.pallas_call(
        backward_kernel,
        out_shape=(out, out, out),
        compiler_params=params(16),
        cost_estimate=cost(32 * queries.size * DH, 16 * queries.size),
    )(queries, keys, values, draw, prefix, suffix, glocal)


def halves(s_ref, half):
    first = pl.ds(pl.multiple_of(s_ref[3] * half, half), half)
    second = pl.ds(pl.multiple_of((1 - s_ref[3]) * half, half), half)
    return first, second


def project_near_kernel(s_ref, so_far_ref, a1_ref, a2_ref, m1_ref, z1_ref, o1_ref, oz1_ref, out_ref):
    first, second = halves(s_ref, m1_ref.shape[0])
    acc = so_far_ref[...] + dot_nn(a1_ref[:, first], m1_ref[...])
    acc += dot_nn(a1_ref[:, second], z1_ref[...])
    acc += dot_nn(a2_ref[:, first], o1_ref[...])
    acc += dot_nn(a2_ref[:, second], oz1_ref[...])
    out_ref[...] = acc


def project_near(scal, so_far, attns, pieces):
    return pl.pallas_call(
        project_near_kernel,
        out_shape=shape_of(so_far.shape, F32),
        in_specs=smem_then_vmem(7),
        compiler_params=params(16),
        cost_estimate=cost(1000, 1000),
    )(scal, so_far, *attns, *pieces)


def project_far_kernel(s_ref, near_ref, a_ref, d_ref, od_ref, dz_ref, odz_ref, out_hbm, out_buf, sems):
    first, second = halves(s_ref, d_ref.shape[0])
    blocks, _, block = out_buf.shape
    moves = []
    for j in range(blocks):
        here = slice(j * block, (j + 1) * block)
        acc = near_ref[:, here] + dot_nn(a_ref[:, first], d_ref[:, here] + od_ref[:, here])
        acc += dot_nn(a_ref[:, second], dz_ref[:, here] + odz_ref[:, here])
        out_buf[j] = acc.astype(BF16)
        moves.append(pltpu.make_async_copy(out_buf.at[j], out_hbm.at[:, here], sems.at[j]))
        moves[-1].start()
    for move in moves:
        move.wait()


def project_far(scal, near, attn, pieces):
    tok, out_width = near.shape
    block = 512
    return pl.pallas_call(
        project_far_kernel,
        out_shape=shape_of((tok, out_width), BF16),
        in_specs=smem_then_vmem(6),
        out_specs=pl.BlockSpec(memory_space=pl.ANY),
        scratch_shapes=[
            pltpu.VMEM((out_width // block, tok, block), BF16),
            pltpu.SemaphoreType.DMA((out_width // block,)),
        ],
        compiler_params=params(16),
        cost_estimate=cost(1000, 1000),
    )(scal, near, attn, *pieces)


def in_hbm(array):
    return pltpu.with_memory_space_constraint(array, pltpu.HBM)


def after(array, *needed):
    return lax.optimization_barrier((array, *needed))[0]


def shift(array, axis, count, by, wrap):
    pairs = [(i, (i + by) % count) for i in range(count) if wrap or 0 <= i + by < count]
    return lax.ppermute(array, axis, pairs)


def total(arrays):
    if len(arrays) == 1:
        return arrays[0]
    return functools.reduce(jnp.add, [a.astype(F32) for a in arrays])


def body(n_ctx, n_head, n_rep, queries, keys, values, out_weight, out_grad):
    c, h, z = lax.axis_index("ctx"), lax.axis_index("head"), lax.axis_index("rep")
    x, y, p = h & 1, h >> 1, z & 1
    scal = jnp.stack([c, y, x, p]).astype(jnp.int32)
    paired = n_ctx == 2 and n_head == 4 and n_rep % 2 == 0
    own_width = out_weight.shape[1]
    weight_hbm, grad_hbm = in_hbm(out_weight), in_hbm(out_grad)

    if paired:
        group = ("ctx", "head")
        near = [(4 * (i // 2) + i, i ^ 1) for i in range(4)]
        near += [(4 * (1 - i // 2) + i, 4 + (i ^ 2)) for i in range(4)]
        far = [(4 * (1 - i // 2) + i, i ^ 3) for i in range(4)]
        one = [(i, i ^ 1) for i in range(4)] + [(4 + i, 4 + (i ^ 2)) for i in range(4)]
        two = [(i, i ^ 2) for i in range(4)] + [(4 + i, 4 + (i ^ 1)) for i in range(4)]
        zpair = [(i, i ^ 1) for i in range(n_rep)]
        swap = [(0, 1), (1, 0)]
        state, near_piece, far_piece, turn, queries, keys, values = opening(
            scal, in_hbm(queries), in_hbm(keys), in_hbm(values), weight_hbm, grad_hbm
        )
        near_mine = lax.ppermute(near_piece, group, near)
        far_mine = lax.ppermute(far_piece, group, far)
        other_grad = lax.ppermute(turn, "ctx", swap)
    else:
        state = local_state(keys, values)
        other_grad = []
        for k in range(1, n_ctx):
            start = lax.rem(c + k, n_ctx) * own_width
            turn = lax.dynamic_slice_in_dim(out_grad, start, own_width, 1)
            other_grad.append(shift(turn, "ctx", n_ctx, k, True))
        other_grad = jnp.concatenate(other_grad, 0)

    carried = total([shift(state, "ctx", n_ctx, k, False) for k in range(1, n_ctx)])
    rest = [shift(out_weight, "ctx", n_ctx, -k, True) for k in range(1, n_ctx)]
    rest = rest[0] if n_ctx == 2 else jnp.concatenate(rest, 1)
    attn_grad = attn_gradient(scal, out_weight, out_grad, after(rest, state))
    carried = after(carried, attn_grad)
    attn, attn_t, raw, prefix = forward(queries, keys, values, carried)

    if paired:
        attn_1 = lax.ppermute(attn, group, one)
        attn_2 = lax.ppermute(attn, group, two)
        near_z = lax.ppermute(near_mine, "rep", zpair)
        raw = after(raw, near_mine, other_grad)
    other_attn = [shift(attn_t, "ctx", n_ctx, k, True) for k in range(1, n_ctx)]
    other_attn = other_attn[0] if n_ctx == 2 else jnp.concatenate(other_attn, 0)

    draw, gsum, glocal, own_out = cotangent(
        scal, attn_grad, queries, raw, attn, out_weight, rest, own_width // 2 if paired else own_width
    )
    suffix = total([shift(gsum, "ctx", n_ctx, -k, False) for k in range(1, n_ctx)])

    if paired:
        far_z = lax.ppermute(after(far_mine, gsum), ("ctx", "rep"), zpair)
        other_attn = after(other_attn, gsum, far_mine)

    weight_grad = own_weight_grad(scal, attn_t, out_grad, other_attn, other_grad)

    if paired:
        near_other = lax.ppermute(after(near_mine, weight_grad), "ctx", swap)
        attn_3 = lax.ppermute(after(attn_1, weight_grad), group, two)
        near_other_z = lax.ppermute(after(near_z, weight_grad), "ctx", swap)
        suffix = after(suffix, weight_grad, attn_1, attn_2, near_z)

    query_grad, key_grad, value_grad = backward(queries, keys, values, draw, prefix, suffix, glocal)

    if paired:
        far_other = lax.ppermute(after(far_mine, weight_grad), "ctx", [(0, 1)])
        far_other_z = lax.ppermute(after(far_z, query_grad), "ctx", [(0, 1)])
        near_out = project_near(
            scal, after(own_out, query_grad, attn_3), (attn_1, attn_2),
            (near_mine, near_z, near_other, near_other_z),
        )
        layer_out = project_far(scal, near_out, attn_3, (far_mine, far_other, far_z, far_other_z))
    else:
        full = lax.all_gather(out_weight, "ctx", axis=1, tiled=True)
        partial_out = jnp.dot(attn, full, preferred_element_type=F32).astype(BF16)
        layer_out = lax.psum_scatter(partial_out, "head", scatter_dimension=1, tiled=True)
    return layer_out, query_grad, key_grad, value_grad, weight_grad


def solution(mesh):
    tokens = P(("rep", "ctx"), "head")
    sizes = mesh.shape["ctx"], mesh.shape["head"], mesh.shape["rep"]
    return jax.shard_map(
        functools.partial(body, *sizes),
        mesh=mesh,
        in_specs=(tokens, tokens, tokens, P("head", "ctx"), P(("rep", "ctx"), None)),
        out_specs=(tokens, tokens, tokens, tokens, P(("rep", "head"), "ctx")),
        check_vma=False,
    )
```

```python
import functools

import jax
import jax.numpy as jnp
from jax import lax
from jax.experimental import pallas as pl
from jax.experimental.pallas import tpu as pltpu
from jax.sharding import PartitionSpec as P

DH = 128
CHUNK = 256
EPS = 1e-06
F32 = jnp.float32
BF16 = jnp.bfloat16


def feature(x):
    return jnp.where(x > 0, x + 1.0, jnp.exp(jnp.minimum(x, 0.0)))


def dot_nn(a, b):
    return lax.dot_general(a, b, (((1,), (0,)), ((), ())), preferred_element_type=F32)


def dot_nt(a, b):
    return lax.dot_general(a, b, (((1,), (1,)), ((), ())), preferred_element_type=F32)


def dot_tn(a, b):
    return lax.dot_general(a, b, (((0,), (0,)), ((), ())), preferred_element_type=F32)


def shape_of(shape, dtype):
    return jax.ShapeDtypeStruct(shape, dtype)


def params(mib):
    return pltpu.CompilerParams(vmem_limit_bytes=mib * 1024 * 1024)


def cost(flops, moved):
    return pl.CostEstimate(flops=flops, transcendentals=0, bytes_accessed=moved)


def state_kernel(k_ref, v_ref, out_ref):
    for lo in range(0, k_ref.shape[1], DH):
        cols = slice(lo, lo + DH)
        fk = feature(k_ref[:, cols].astype(F32)).astype(BF16)
        out_ref[cols, :] = dot_tn(fk, v_ref[:, cols]).astype(BF16)


def local_state(keys, values):
    width = keys.shape[1]
    return pl.pallas_call(
        state_kernel,
        out_shape=shape_of((width, DH), BF16),
        compiler_params=params(16),
        cost_estimate=cost(2 * keys.size * DH, 4 * keys.size),
    )(keys, values)


def opening_kernel(s_ref, q_hbm, k_hbm, v_hbm, weight_hbm, grad_hbm,
                   state_ref, near_ref, far_ref, turn_ref, q_ref, k_ref, v_ref, sems, slice_sems):
    half, wide = near_ref.shape
    rows = pl.ds(pl.multiple_of(s_ref[3] * half, half), half)
    far_column = 1 - s_ref[2]
    near_column = jnp.where(s_ref[0] == s_ref[1], far_column, s_ref[2])
    loads = []
    for i, lo in enumerate(range(0, k_hbm.shape[1], DH)):
        cols = pl.ds(lo, DH)
        loads.append([
            pltpu.make_async_copy(k_hbm.at[:, cols], k_ref.at[:, cols], sems.at[0, i]),
            pltpu.make_async_copy(v_hbm.at[:, cols], v_ref.at[:, cols], sems.at[1, i]),
        ])
        loads[-1][0].start()
        loads[-1][1].start()
    moves = []
    for i, (column, ref) in enumerate([(near_column, near_ref), (far_column, far_ref)]):
        cols = pl.ds(pl.multiple_of(column * wide, wide), wide)
        moves.append(pltpu.make_async_copy(weight_hbm.at[rows, cols], ref, slice_sems.at[i]))
        moves[-1].start()
    moves.append(pltpu.make_async_copy(q_hbm, q_ref, slice_sems.at[2]))
    moves[-1].start()
    own = turn_ref.shape[1]
    cols = pl.ds(pl.multiple_of((1 - s_ref[0]) * own, own), own)
    moves.append(pltpu.make_async_copy(grad_hbm.at[:, cols], turn_ref, slice_sems.at[3]))
    moves[-1].start()
    for i, lo in enumerate(range(0, k_hbm.shape[1], DH)):
        cols = slice(lo, lo + DH)
        loads[i][0].wait()
        loads[i][1].wait()
        fk = feature(k_ref[:, cols].astype(F32)).astype(BF16)
        state_ref[cols, :] = dot_tn(fk, v_ref[:, cols]).astype(BF16)
    for move in moves:
        move.wait()


def opening(scal, queries, keys, values, weight, out_grad):
    tok, width = keys.shape
    piece = shape_of((weight.shape[0] // 2, weight.shape[1] // 2), BF16)
    hbm = pl.BlockSpec(memory_space=pltpu.HBM)
    vmem = pl.BlockSpec(memory_space=pltpu.VMEM)
    return pl.pallas_call(
        opening_kernel,
        out_shape=(shape_of((width, DH), BF16), piece, piece, shape_of((tok, weight.shape[1]), BF16))
        + (shape_of(keys.shape, BF16),) * 3,
        in_specs=[pl.BlockSpec(memory_space=pltpu.SMEM)] + [hbm] * 5,
        out_specs=(vmem,) * 7,
        scratch_shapes=[
            pltpu.SemaphoreType.DMA((2, width // DH)),
            pltpu.SemaphoreType.DMA((4,)),
        ],
        compiler_params=params(16),
        cost_estimate=cost(2 * keys.size * DH, 4 * keys.size),
    )(scal, queries, keys, values, weight, out_grad)


def forward_kernel(q_ref, k_ref, v_ref, carried_ref, attn_ref, attn_t_ref, raw_ref, prefix_ref):
    tok, width = q_ref.shape
    chunk = min(CHUNK, tok)
    row = lax.broadcasted_iota(jnp.int32, (chunk, chunk), 0)
    col = lax.broadcasted_iota(jnp.int32, (chunk, chunk), 1)
    lower = row >= col
    for lo in range(0, width, DH):
        cols = slice(lo, lo + DH)
        prefix = carried_ref[cols, :].astype(F32)
        for i in range(tok // chunk):
            rows = slice(i * chunk, (i + 1) * chunk)
            fq = feature(q_ref[rows, cols].astype(F32)).astype(BF16)
            fk = feature(k_ref[rows, cols].astype(F32)).astype(BF16)
            v = v_ref[rows, cols]
            low_prefix = prefix.astype(BF16)
            prefix_ref[i, cols, :] = low_prefix
            scores = jnp.where(lower, dot_nt(fq, fk), 0.0).astype(BF16)
            raw = dot_nn(scores, v) + dot_nn(fq, low_prefix)
            raw_ref[rows, cols] = raw
            inv = lax.rsqrt(jnp.mean(raw * raw, axis=-1, keepdims=True) + EPS)
            attn = (raw * inv).astype(BF16)
            attn_ref[rows, cols] = attn
            attn_t_ref[cols, rows] = attn.T
            if i + 1 < tok // chunk:
                prefix = prefix + dot_tn(fk, v)


def forward(queries, keys, values, carried):
    tok, width = queries.shape
    chunks = tok // min(CHUNK, tok)
    return pl.pallas_call(
        forward_kernel,
        out_shape=(
            shape_of((tok, width), BF16),
            shape_of((width, tok), BF16),
            shape_of((tok, width), F32),
            shape_of((chunks, width, DH), BF16),
        ),
        compiler_params=params(16),
        cost_estimate=cost(16 * queries.size * DH, 12 * queries.size),
    )(queries, keys, values, carried)


def smem_then_vmem(count):
    return [pl.BlockSpec(memory_space=pltpu.SMEM)] + [pl.BlockSpec(memory_space=pltpu.VMEM)] * count


def attn_grad_kernel(s_ref, own_ref, grad_ref, rest_ref, out_ref, acc_ref):
    own_width, rest_width = own_ref.shape[1], rest_ref.shape[1]
    count = (own_width + rest_width) // own_width

    def part(k):
        place = lax.rem(s_ref[0] + k, count) * own_width
        return grad_ref[:, pl.ds(pl.multiple_of(place, own_width), own_width)]

    acc_ref[...] = dot_nt(part(0), own_ref[...])
    for k in range(1, count):
        acc_ref[...] += dot_nt(part(k), rest_ref[:, (k - 1) * own_width : k * own_width])
    out_ref[...] = acc_ref[...].astype(BF16)


def attn_gradient(scal, weight, out_grad, rest):
    tok, width = out_grad.shape[0], weight.shape[0]
    return pl.pallas_call(
        attn_grad_kernel,
        out_shape=shape_of((tok, width), BF16),
        in_specs=smem_then_vmem(3),
        scratch_shapes=[pltpu.VMEM((tok, width), F32)],
        compiler_params=params(16),
        cost_estimate=cost(2 * out_grad.size * width, 4 * out_grad.size),
    )(scal, weight, out_grad, rest)


def cotangent_kernel(s_ref, attn_grad_ref, q_ref, raw_ref, attn_ref, own_ref, rest_ref,
                     draw_ref, gsum_ref, glocal_ref, out_ref):
    tok, width = q_ref.shape
    chunk = min(CHUNK, tok)
    for lo in range(0, width, DH):
        cols = slice(lo, lo + DH)
        later = jnp.zeros((DH, DH), F32)
        for i in reversed(range(tok // chunk)):
            rows = slice(i * chunk, (i + 1) * chunk)
            glocal_ref[i, cols, :] = later
            grad = attn_grad_ref[rows, cols].astype(F32)
            raw = raw_ref[rows, cols]
            inv = lax.rsqrt(jnp.mean(raw * raw, axis=-1, keepdims=True) + EPS)
            normed = raw * inv
            mean = jnp.mean(grad * normed, axis=-1, keepdims=True)
            draw = (inv * (grad - normed * mean)).astype(BF16)
            draw_ref[rows, cols] = draw
            fq = feature(q_ref[rows, cols].astype(F32)).astype(BF16)
            later = later + dot_tn(fq, draw)
        gsum_ref[cols, :] = later.astype(BF16)
    wide = out_ref.shape[1]
    if wide < own_ref.shape[1]:
        local = pl.ds(pl.multiple_of(s_ref[2] * wide, wide), wide)
        weight = jnp.where(s_ref[0] == s_ref[1], own_ref[:, local], rest_ref[:, local])
        out_ref[...] = dot_nn(attn_ref[...], weight)


def cotangent(scal, attn_grad, queries, raw, attn, own, rest, out_width):
    tok, width = queries.shape
    chunks = tok // min(CHUNK, tok)
    return pl.pallas_call(
        cotangent_kernel,
        out_shape=(
            shape_of((tok, width), BF16),
            shape_of((width, DH), BF16),
            shape_of((chunks, width, DH), F32),
            shape_of((tok, out_width), F32),
        ),
        in_specs=smem_then_vmem(6),
        compiler_params=params(16),
        cost_estimate=cost(2 * tok * width * out_width, 16 * queries.size),
    )(scal, attn_grad, queries, raw, attn, own, rest)


def weight_grad_kernel(s_ref, attn_t_ref, grad_ref, other_t_ref, other_grad_ref, out_hbm, late_ref, out_buf, sems):
    width, tok = attn_t_ref.shape
    early, _, block = out_buf.shape
    blocks = early + late_ref.shape[0]
    moves = []
    for j in range(blocks):
        here = slice(j * block, (j + 1) * block)
        place = s_ref[0] * (blocks * block) + j * block
        part = grad_ref[:, pl.ds(pl.multiple_of(place, block), block)]
        acc = dot_nn(attn_t_ref[...], part).astype(BF16).astype(F32)
        for k in range(other_t_ref.shape[0] // width):
            other_t = other_t_ref[k * width : (k + 1) * width, :]
            part = other_grad_ref[k * tok : (k + 1) * tok, here]
            acc += dot_nn(other_t, part).astype(BF16).astype(F32)
        if j < early:
            out_buf[j] = acc
            moves.append(pltpu.make_async_copy(out_buf.at[j], out_hbm.at[:, here], sems.at[j]))
            moves[-1].start()
        else:
            late_ref[j - early] = acc
    for move in moves:
        move.wait()


def own_weight_grad(scal, attn_t, out_grad, other_t, other_grad):
    width = attn_t.shape[0]
    own_width = other_grad.shape[1]
    block = min(256, own_width // 2)
    blocks = own_width // block
    early = blocks // 2
    return pl.pallas_call(
        weight_grad_kernel,
        out_shape=(
            shape_of((width, own_width), F32),
            shape_of((blocks - early, width, block), F32),
        ),
        in_specs=smem_then_vmem(4),
        out_specs=(pl.BlockSpec(memory_space=pl.ANY), pl.BlockSpec(memory_space=pltpu.VMEM)),
        scratch_shapes=[
            pltpu.VMEM((early, width, block), F32),
            pltpu.SemaphoreType.DMA((early,)),
        ],
        compiler_params=params(16),
        cost_estimate=cost(1000, 1000),
    )(scal, attn_t, out_grad, other_t, other_grad)


def backward_kernel(q_ref, k_ref, v_ref, draw_ref, prefix_ref, suffix_ref, glocal_ref, late_ref, early_hbm,
                    dq_hbm, dk_hbm, dv_hbm, grad_hbm, dq_ref, dk_ref, dv_ref, sems, late_sems):
    late, _, block = late_ref.shape
    moves = []
    for j in range(late):
        start = grad_hbm.shape[1] - (late - j) * block
        there = grad_hbm.at[:, start : start + block]
        moves.append(pltpu.make_async_copy(late_ref.at[j], there, late_sems.at[j]))
        moves[-1].start()
    tok, width = q_ref.shape
    chunk = min(CHUNK, tok)
    row = lax.broadcasted_iota(jnp.int32, (chunk, chunk), 0)
    col = lax.broadcasted_iota(jnp.int32, (chunk, chunk), 1)
    lower = row >= col
    upper = row <= col
    for head, lo in enumerate(range(0, width, DH)):
        cols = slice(lo, lo + DH)
        suffix = suffix_ref[cols, :].astype(F32)
        for i in range(tok // chunk):
            rows = slice(i * chunk, (i + 1) * chunk)
            q = q_ref[rows, cols].astype(F32)
            k = k_ref[rows, cols].astype(F32)
            q_slope = jnp.exp(jnp.minimum(q, 0.0))
            k_slope = jnp.exp(jnp.minimum(k, 0.0))
            fq = jnp.where(q > 0, q + 1.0, q_slope).astype(BF16)
            fk = jnp.where(k > 0, k + 1.0, k_slope).astype(BF16)
            v = v_ref[rows, cols]
            draw = draw_ref[rows, cols]
            later = (suffix + glocal_ref[i, cols, :]).astype(BF16)
            dscores = jnp.where(lower, dot_nt(draw, v), 0.0).astype(BF16)
            dfq = dot_nn(dscores, fk) + dot_nt(draw, prefix_ref[i, cols, :])
            dq_ref[rows, cols] = (dfq * q_slope).astype(BF16)
            dscores_t = jnp.where(upper, dot_nt(v, draw), 0.0).astype(BF16)
            dfk = dot_nn(dscores_t, fq) + dot_nt(v, later)
            dk_ref[rows, cols] = (dfk * k_slope).astype(BF16)
            scores_t = jnp.where(upper, dot_nt(fk, fq), 0.0).astype(BF16)
            dv = dot_nn(scores_t, draw) + dot_nn(fk, later)
            dv_ref[rows, cols] = dv.astype(BF16)
        for n, (ref, hbm) in enumerate([(dq_ref, dq_hbm), (dk_ref, dk_hbm), (dv_ref, dv_hbm)]):
            moves.append(pltpu.make_async_copy(ref.at[:, cols], hbm.at[:, cols], sems.at[n, head]))
            moves[-1].start()
    for move in moves:
        move.wait()


def backward(queries, keys, values, draw, prefix, suffix, glocal, late, early):
    tok, width = queries.shape
    out = shape_of(queries.shape, BF16)
    vmem, hbm = pl.BlockSpec(memory_space=pltpu.VMEM), pl.BlockSpec(memory_space=pl.ANY)
    return pl.pallas_call(
        backward_kernel,
        out_shape=(out, out, out, shape_of(early.shape, F32)),
        in_specs=[vmem] * 8 + [hbm],
        out_specs=(hbm,) * 4,
        scratch_shapes=[pltpu.VMEM((tok, width), BF16)] * 3
        + [pltpu.SemaphoreType.DMA((3, width // DH)), pltpu.SemaphoreType.DMA((late.shape[0],))],
        input_output_aliases={8: 3},
        compiler_params=params(16),
        cost_estimate=cost(1000, 1000),
    )(queries, keys, values, draw, prefix, suffix, glocal, late, early)


def halves(s_ref, half):
    first = pl.ds(pl.multiple_of(s_ref[3] * half, half), half)
    second = pl.ds(pl.multiple_of((1 - s_ref[3]) * half, half), half)
    return first, second


def project_near_kernel(s_ref, so_far_ref, a1_ref, a2_ref, m1_ref, z1_ref, o1_ref, oz1_ref, out_ref):
    first, second = halves(s_ref, m1_ref.shape[0])
    acc = so_far_ref[...] + dot_nn(a1_ref[:, first], m1_ref[...])
    acc += dot_nn(a1_ref[:, second], z1_ref[...])
    acc += dot_nn(a2_ref[:, first], o1_ref[...])
    acc += dot_nn(a2_ref[:, second], oz1_ref[...])
    out_ref[...] = acc


def project_near(scal, so_far, attns, pieces):
    return pl.pallas_call(
        project_near_kernel,
        out_shape=shape_of(so_far.shape, F32),
        in_specs=smem_then_vmem(7),
        compiler_params=params(16),
        cost_estimate=cost(1000, 1000),
    )(scal, so_far, *attns, *pieces)


def project_far_kernel(s_ref, near_ref, a_ref, d_ref, od_ref, dz_ref, odz_ref, out_hbm, out_buf, sems):
    first, second = halves(s_ref, d_ref.shape[0])
    blocks, _, block = out_buf.shape
    moves = []
    for j in range(blocks):
        here = slice(j * block, (j + 1) * block)
        acc = near_ref[:, here] + dot_nn(a_ref[:, first], d_ref[:, here] + od_ref[:, here])
        acc += dot_nn(a_ref[:, second], dz_ref[:, here] + odz_ref[:, here])
        out_buf[j] = acc.astype(BF16)
        moves.append(pltpu.make_async_copy(out_buf.at[j], out_hbm.at[:, here], sems.at[j]))
        moves[-1].start()
    for move in moves:
        move.wait()


def project_far(scal, near, attn, pieces):
    tok, out_width = near.shape
    block = 512
    return pl.pallas_call(
        project_far_kernel,
        out_shape=shape_of((tok, out_width), BF16),
        in_specs=smem_then_vmem(6),
        out_specs=pl.BlockSpec(memory_space=pl.ANY),
        scratch_shapes=[
            pltpu.VMEM((out_width // block, tok, block), BF16),
            pltpu.SemaphoreType.DMA((out_width // block,)),
        ],
        compiler_params=params(16),
        cost_estimate=cost(1000, 1000),
    )(scal, near, attn, *pieces)


def in_hbm(array):
    return pltpu.with_memory_space_constraint(array, pltpu.HBM)


def after(array, *needed):
    return lax.optimization_barrier((array, *needed))[0]


def shift(array, axis, count, by, wrap):
    pairs = [(i, (i + by) % count) for i in range(count) if wrap or 0 <= i + by < count]
    return lax.ppermute(array, axis, pairs)


def total(arrays):
    if len(arrays) == 1:
        return arrays[0]
    return functools.reduce(jnp.add, [a.astype(F32) for a in arrays])


def body(n_ctx, n_head, n_rep, queries, keys, values, out_weight, out_grad):
    c, h, z = lax.axis_index("ctx"), lax.axis_index("head"), lax.axis_index("rep")
    x, y, p = h & 1, h >> 1, z & 1
    scal = jnp.stack([c, y, x, p]).astype(jnp.int32)
    paired = n_ctx == 2 and n_head == 4 and n_rep % 2 == 0
    own_width = out_weight.shape[1]
    weight_hbm, grad_hbm = in_hbm(out_weight), in_hbm(out_grad)

    if paired:
        group = ("ctx", "head")
        near = [(4 * (i // 2) + i, i ^ 1) for i in range(4)]
        near += [(4 * (1 - i // 2) + i, 4 + (i ^ 2)) for i in range(4)]
        far = [(4 * (1 - i // 2) + i, i ^ 3) for i in range(4)]
        one = [(i, i ^ 1) for i in range(4)] + [(4 + i, 4 + (i ^ 2)) for i in range(4)]
        two = [(i, i ^ 2) for i in range(4)] + [(4 + i, 4 + (i ^ 1)) for i in range(4)]
        zpair = [(i, i ^ 1) for i in range(n_rep)]
        swap = [(0, 1), (1, 0)]
        state, near_piece, far_piece, turn, queries, keys, values = opening(
            scal, in_hbm(queries), in_hbm(keys), in_hbm(values), weight_hbm, grad_hbm
        )
        near_mine = lax.ppermute(near_piece, group, near)
        far_mine = lax.ppermute(far_piece, group, far)
        other_grad = lax.ppermute(turn, "ctx", swap)
    else:
        state = local_state(keys, values)
        other_grad = []
        for k in range(1, n_ctx):
            start = lax.rem(c + k, n_ctx) * own_width
            turn = lax.dynamic_slice_in_dim(out_grad, start, own_width, 1)
            other_grad.append(shift(turn, "ctx", n_ctx, k, True))
        other_grad = jnp.concatenate(other_grad, 0)

    carried = total([shift(state, "ctx", n_ctx, k, False) for k in range(1, n_ctx)])
    rest = [shift(out_weight, "ctx", n_ctx, -k, True) for k in range(1, n_ctx)]
    rest = rest[0] if n_ctx == 2 else jnp.concatenate(rest, 1)
    attn_grad = attn_gradient(scal, out_weight, out_grad, after(rest, state))
    carried = after(carried, attn_grad)
    attn, attn_t, raw, prefix = forward(queries, keys, values, carried)

    if paired:
        attn_1 = lax.ppermute(attn, group, one)
        attn_2 = lax.ppermute(attn, group, two)
        near_z = lax.ppermute(near_mine, "rep", zpair)
        raw = after(raw, near_mine, other_grad)
    other_attn = [shift(attn_t, "ctx", n_ctx, k, True) for k in range(1, n_ctx)]
    other_attn = other_attn[0] if n_ctx == 2 else jnp.concatenate(other_attn, 0)

    draw, gsum, glocal, own_out = cotangent(
        scal, attn_grad, queries, raw, attn, out_weight, rest, own_width // 2 if paired else own_width
    )
    suffix = total([shift(gsum, "ctx", n_ctx, -k, False) for k in range(1, n_ctx)])

    if paired:
        far_z = lax.ppermute(after(far_mine, gsum), ("ctx", "rep"), zpair)
        other_attn = after(other_attn, gsum, far_mine)

    early, late = own_weight_grad(scal, attn_t, out_grad, other_attn, other_grad)

    if paired:
        near_other = lax.ppermute(after(near_mine, late), "ctx", swap)
        suffix = after(suffix, late, attn_1)

    query_grad, key_grad, value_grad, weight_grad = backward(
        queries, keys, values, draw, prefix, suffix, glocal, late, early
    )

    if paired:
        attn_3 = lax.ppermute(after(attn_1, late), group, two)
        near_other_z = lax.ppermute(after(near_z, late), "ctx", swap)
        far_other = lax.ppermute(after(far_mine, late), "ctx", [(0, 1)])
        near_out = project_near(
            scal, after(own_out, query_grad), (attn_1, attn_2),
            (near_mine, near_z, near_other, near_other_z),
        )
        far_other_z = lax.ppermute(after(far_z, query_grad), "ctx", [(0, 1)])
        layer_out = project_far(scal, near_out, attn_3, (far_mine, far_other, far_z, far_other_z))
    else:
        full = lax.all_gather(out_weight, "ctx", axis=1, tiled=True)
        partial_out = jnp.dot(attn, full, preferred_element_type=F32).astype(BF16)
        layer_out = lax.psum_scatter(partial_out, "head", scatter_dimension=1, tiled=True)
    return layer_out, query_grad, key_grad, value_grad, weight_grad


def solution(mesh):
    tokens = P(("rep", "ctx"), "head")
    sizes = mesh.shape["ctx"], mesh.shape["head"], mesh.shape["rep"]
    return jax.shard_map(
        functools.partial(body, *sizes),
        mesh=mesh,
        in_specs=(tokens, tokens, tokens, P("head", "ctx"), P(("rep", "ctx"), None)),
        out_specs=(tokens, tokens, tokens, tokens, P(("rep", "head"), "ctx")),
        check_vma=False,
    )
```

```python
import functools

import jax
import jax.numpy as jnp
from jax import lax
from jax.experimental import pallas as pl
from jax.experimental.pallas import tpu as pltpu
from jax.sharding import PartitionSpec as P

DH = 128
CHUNK = 256
EPS = 1e-06
F32 = jnp.float32
BF16 = jnp.bfloat16


def feature(x):
    return jnp.where(x > 0, x + 1.0, jnp.exp(jnp.minimum(x, 0.0)))


def dot_nn(a, b):
    return lax.dot_general(a, b, (((1,), (0,)), ((), ())), preferred_element_type=F32)


def dot_nt(a, b):
    return lax.dot_general(a, b, (((1,), (1,)), ((), ())), preferred_element_type=F32)


def dot_tn(a, b):
    return lax.dot_general(a, b, (((0,), (0,)), ((), ())), preferred_element_type=F32)


def shape_of(shape, dtype):
    return jax.ShapeDtypeStruct(shape, dtype)


def params(mib):
    return pltpu.CompilerParams(vmem_limit_bytes=mib * 1024 * 1024)


def cost(flops, moved):
    return pl.CostEstimate(flops=flops, transcendentals=0, bytes_accessed=moved)


def state_kernel(k_ref, v_ref, out_ref):
    for lo in range(0, k_ref.shape[1], DH):
        cols = slice(lo, lo + DH)
        fk = feature(k_ref[:, cols].astype(F32)).astype(BF16)
        out_ref[cols, :] = dot_tn(fk, v_ref[:, cols]).astype(BF16)


def local_state(keys, values):
    width = keys.shape[1]
    return pl.pallas_call(
        state_kernel,
        out_shape=shape_of((width, DH), BF16),
        compiler_params=params(16),
        cost_estimate=cost(2 * keys.size * DH, 4 * keys.size),
    )(keys, values)


def opening_kernel(s_ref, q_hbm, k_hbm, v_hbm, weight_hbm, grad_hbm,
                   state_ref, near_ref, far_ref, turn_ref, q_ref, k_ref, v_ref, sems, slice_sems):
    half, wide = near_ref.shape
    rows = pl.ds(pl.multiple_of(s_ref[3] * half, half), half)
    far_column = 1 - s_ref[2]
    near_column = jnp.where(s_ref[0] == s_ref[1], far_column, s_ref[2])
    loads = []
    for i, lo in enumerate(range(0, k_hbm.shape[1], DH)):
        cols = pl.ds(lo, DH)
        loads.append([
            pltpu.make_async_copy(k_hbm.at[:, cols], k_ref.at[:, cols], sems.at[0, i]),
            pltpu.make_async_copy(v_hbm.at[:, cols], v_ref.at[:, cols], sems.at[1, i]),
        ])
        loads[-1][0].start()
        loads[-1][1].start()
    moves = []
    for i, (column, ref) in enumerate([(near_column, near_ref), (far_column, far_ref)]):
        cols = pl.ds(pl.multiple_of(column * wide, wide), wide)
        moves.append(pltpu.make_async_copy(weight_hbm.at[rows, cols], ref, slice_sems.at[i]))
        moves[-1].start()
    moves.append(pltpu.make_async_copy(q_hbm, q_ref, slice_sems.at[2]))
    moves[-1].start()
    own = turn_ref.shape[1]
    cols = pl.ds(pl.multiple_of((1 - s_ref[0]) * own, own), own)
    moves.append(pltpu.make_async_copy(grad_hbm.at[:, cols], turn_ref, slice_sems.at[3]))
    moves[-1].start()
    for i, lo in enumerate(range(0, k_hbm.shape[1], DH)):
        cols = slice(lo, lo + DH)
        loads[i][0].wait()
        loads[i][1].wait()
        fk = feature(k_ref[:, cols].astype(F32)).astype(BF16)
        state_ref[cols, :] = dot_tn(fk, v_ref[:, cols]).astype(BF16)
    for move in moves:
        move.wait()


def opening(scal, queries, keys, values, weight, out_grad):
    tok, width = keys.shape
    piece = shape_of((weight.shape[0] // 2, weight.shape[1] // 2), BF16)
    hbm = pl.BlockSpec(memory_space=pltpu.HBM)
    vmem = pl.BlockSpec(memory_space=pltpu.VMEM)
    return pl.pallas_call(
        opening_kernel,
        out_shape=(shape_of((width, DH), BF16), piece, piece, shape_of((tok, weight.shape[1]), BF16))
        + (shape_of(keys.shape, BF16),) * 3,
        in_specs=[pl.BlockSpec(memory_space=pltpu.SMEM)] + [hbm] * 5,
        out_specs=(vmem,) * 7,
        scratch_shapes=[
            pltpu.SemaphoreType.DMA((2, width // DH)),
            pltpu.SemaphoreType.DMA((4,)),
        ],
        compiler_params=params(16),
        cost_estimate=cost(2 * keys.size * DH, 4 * keys.size),
    )(scal, queries, keys, values, weight, out_grad)


def forward_kernel(q_ref, k_ref, v_ref, carried_ref, attn_ref, attn_t_ref, raw_ref, prefix_ref):
    tok, width = q_ref.shape
    chunk = min(CHUNK, tok)
    row = lax.broadcasted_iota(jnp.int32, (chunk, chunk), 0)
    col = lax.broadcasted_iota(jnp.int32, (chunk, chunk), 1)
    lower = row >= col
    for lo in range(0, width, DH):
        cols = slice(lo, lo + DH)
        prefix = carried_ref[cols, :].astype(F32)
        for i in range(tok // chunk):
            rows = slice(i * chunk, (i + 1) * chunk)
            fq = feature(q_ref[rows, cols].astype(F32)).astype(BF16)
            fk = feature(k_ref[rows, cols].astype(F32)).astype(BF16)
            v = v_ref[rows, cols]
            low_prefix = prefix.astype(BF16)
            prefix_ref[i, cols, :] = low_prefix
            scores = jnp.where(lower, dot_nt(fq, fk), 0.0).astype(BF16)
            raw = dot_nn(scores, v) + dot_nn(fq, low_prefix)
            raw_ref[rows, cols] = raw
            inv = lax.rsqrt(jnp.mean(raw * raw, axis=-1, keepdims=True) + EPS)
            attn = (raw * inv).astype(BF16)
            attn_ref[rows, cols] = attn
            attn_t_ref[cols, rows] = attn.T
            if i + 1 < tok // chunk:
                prefix = prefix + dot_tn(fk, v)


def forward(queries, keys, values, carried):
    tok, width = queries.shape
    chunks = tok // min(CHUNK, tok)
    return pl.pallas_call(
        forward_kernel,
        out_shape=(
            shape_of((tok, width), BF16),
            shape_of((width, tok), BF16),
            shape_of((tok, width), F32),
            shape_of((chunks, width, DH), BF16),
        ),
        compiler_params=params(16),
        cost_estimate=cost(16 * queries.size * DH, 12 * queries.size),
    )(queries, keys, values, carried)


def smem_then_vmem(count):
    return [pl.BlockSpec(memory_space=pltpu.SMEM)] + [pl.BlockSpec(memory_space=pltpu.VMEM)] * count


def attn_grad_kernel(s_ref, own_ref, grad_ref, rest_ref, out_ref, acc_ref):
    own_width, rest_width = own_ref.shape[1], rest_ref.shape[1]
    count = (own_width + rest_width) // own_width

    def part(k):
        place = lax.rem(s_ref[0] + k, count) * own_width
        return grad_ref[:, pl.ds(pl.multiple_of(place, own_width), own_width)]

    acc_ref[...] = dot_nt(part(0), own_ref[...])
    for k in range(1, count):
        acc_ref[...] += dot_nt(part(k), rest_ref[:, (k - 1) * own_width : k * own_width])
    out_ref[...] = acc_ref[...].astype(BF16)


def attn_gradient(scal, weight, out_grad, rest):
    tok, width = out_grad.shape[0], weight.shape[0]
    return pl.pallas_call(
        attn_grad_kernel,
        out_shape=shape_of((tok, width), BF16),
        in_specs=smem_then_vmem(3),
        scratch_shapes=[pltpu.VMEM((tok, width), F32)],
        compiler_params=params(16),
        cost_estimate=cost(2 * out_grad.size * width, 4 * out_grad.size),
    )(scal, weight, out_grad, rest)


def cotangent_kernel(s_ref, attn_grad_ref, q_ref, raw_ref, attn_ref, own_ref, rest_ref,
                     draw_ref, gsum_ref, glocal_ref, out_ref):
    tok, width = q_ref.shape
    chunk = min(CHUNK, tok)
    for lo in range(0, width, DH):
        cols = slice(lo, lo + DH)
        later = jnp.zeros((DH, DH), F32)
        for i in reversed(range(tok // chunk)):
            rows = slice(i * chunk, (i + 1) * chunk)
            glocal_ref[i, cols, :] = later
            grad = attn_grad_ref[rows, cols].astype(F32)
            raw = raw_ref[rows, cols]
            inv = lax.rsqrt(jnp.mean(raw * raw, axis=-1, keepdims=True) + EPS)
            normed = raw * inv
            mean = jnp.mean(grad * normed, axis=-1, keepdims=True)
            draw = (inv * (grad - normed * mean)).astype(BF16)
            draw_ref[rows, cols] = draw
            fq = feature(q_ref[rows, cols].astype(F32)).astype(BF16)
            later = later + dot_tn(fq, draw)
        gsum_ref[cols, :] = later.astype(BF16)
    wide = out_ref.shape[1]
    if wide < own_ref.shape[1]:
        local = pl.ds(pl.multiple_of(s_ref[2] * wide, wide), wide)
        weight = jnp.where(s_ref[0] == s_ref[1], own_ref[:, local], rest_ref[:, local])
        out_ref[...] = dot_nn(attn_ref[...], weight)


def cotangent(scal, attn_grad, queries, raw, attn, own, rest, out_width):
    tok, width = queries.shape
    chunks = tok // min(CHUNK, tok)
    return pl.pallas_call(
        cotangent_kernel,
        out_shape=(
            shape_of((tok, width), BF16),
            shape_of((width, DH), BF16),
            shape_of((chunks, width, DH), F32),
            shape_of((tok, out_width), F32),
        ),
        in_specs=smem_then_vmem(6),
        compiler_params=params(16),
        cost_estimate=cost(2 * tok * width * out_width, 16 * queries.size),
    )(scal, attn_grad, queries, raw, attn, own, rest)


def weight_grad_kernel(s_ref, attn_t_ref, grad_ref, other_t_ref, other_grad_ref, out_hbm, late_ref, out_buf, sems):
    width, tok = attn_t_ref.shape
    early, _, block = out_buf.shape
    blocks = early + late_ref.shape[0]
    moves = []
    for j in range(blocks):
        here = slice(j * block, (j + 1) * block)
        place = s_ref[0] * (blocks * block) + j * block
        part = grad_ref[:, pl.ds(pl.multiple_of(place, block), block)]
        acc = dot_nn(attn_t_ref[...], part).astype(BF16).astype(F32)
        for k in range(other_t_ref.shape[0] // width):
            other_t = other_t_ref[k * width : (k + 1) * width, :]
            part = other_grad_ref[k * tok : (k + 1) * tok, here]
            acc += dot_nn(other_t, part).astype(BF16).astype(F32)
        if j < early:
            out_buf[j] = acc
            moves.append(pltpu.make_async_copy(out_buf.at[j], out_hbm.at[:, here], sems.at[j]))
            moves[-1].start()
        else:
            late_ref[j - early] = acc
    for move in moves:
        move.wait()


def own_weight_grad(scal, attn_t, out_grad, other_t, other_grad):
    width = attn_t.shape[0]
    own_width = other_grad.shape[1]
    block = min(1024, own_width // 2)
    blocks = own_width // block
    early = blocks // 2
    return pl.pallas_call(
        weight_grad_kernel,
        out_shape=(
            shape_of((width, own_width), F32),
            shape_of((blocks - early, width, block), F32),
        ),
        in_specs=smem_then_vmem(4),
        out_specs=(pl.BlockSpec(memory_space=pl.ANY), pl.BlockSpec(memory_space=pltpu.VMEM)),
        scratch_shapes=[
            pltpu.VMEM((early, width, block), F32),
            pltpu.SemaphoreType.DMA((early,)),
        ],
        compiler_params=params(16),
        cost_estimate=cost(1000, 1000),
    )(scal, attn_t, out_grad, other_t, other_grad)


def backward_kernel(q_ref, k_ref, v_ref, draw_ref, prefix_ref, suffix_ref, glocal_ref, late_ref, early_hbm,
                    dq_hbm, dk_hbm, dv_hbm, grad_hbm, dq_ref, dk_ref, dv_ref, sems, late_sems):
    late, _, block = late_ref.shape
    moves = []
    for j in range(late):
        start = grad_hbm.shape[1] - (late - j) * block
        there = grad_hbm.at[:, start : start + block]
        moves.append(pltpu.make_async_copy(late_ref.at[j], there, late_sems.at[j]))
        moves[-1].start()
    tok, width = q_ref.shape
    chunk = min(CHUNK, tok)
    row = lax.broadcasted_iota(jnp.int32, (chunk, chunk), 0)
    col = lax.broadcasted_iota(jnp.int32, (chunk, chunk), 1)
    lower = row >= col
    upper = row <= col
    for head, lo in enumerate(range(0, width, DH)):
        cols = slice(lo, lo + DH)
        suffix = suffix_ref[cols, :].astype(F32)
        for i in range(tok // chunk):
            rows = slice(i * chunk, (i + 1) * chunk)
            q = q_ref[rows, cols].astype(F32)
            k = k_ref[rows, cols].astype(F32)
            q_slope = jnp.exp(jnp.minimum(q, 0.0))
            k_slope = jnp.exp(jnp.minimum(k, 0.0))
            fq = jnp.where(q > 0, q + 1.0, q_slope).astype(BF16)
            fk = jnp.where(k > 0, k + 1.0, k_slope).astype(BF16)
            v = v_ref[rows, cols]
            draw = draw_ref[rows, cols]
            later = (suffix + glocal_ref[i, cols, :]).astype(BF16)
            dscores = jnp.where(lower, dot_nt(draw, v), 0.0).astype(BF16)
            dfq = dot_nn(dscores, fk) + dot_nt(draw, prefix_ref[i, cols, :])
            dq_ref[rows, cols] = (dfq * q_slope).astype(BF16)
            dscores_t = jnp.where(upper, dot_nt(v, draw), 0.0).astype(BF16)
            dfk = dot_nn(dscores_t, fq) + dot_nt(v, later)
            dk_ref[rows, cols] = (dfk * k_slope).astype(BF16)
            scores_t = jnp.where(upper, dot_nt(fk, fq), 0.0).astype(BF16)
            dv = dot_nn(scores_t, draw) + dot_nn(fk, later)
            dv_ref[rows, cols] = dv.astype(BF16)
        for n, (ref, hbm) in enumerate([(dq_ref, dq_hbm), (dk_ref, dk_hbm), (dv_ref, dv_hbm)]):
            moves.append(pltpu.make_async_copy(ref.at[:, cols], hbm.at[:, cols], sems.at[n, head]))
            moves[-1].start()
    for move in moves:
        move.wait()


def backward(queries, keys, values, draw, prefix, suffix, glocal, late, early):
    tok, width = queries.shape
    out = shape_of(queries.shape, BF16)
    vmem, hbm = pl.BlockSpec(memory_space=pltpu.VMEM), pl.BlockSpec(memory_space=pl.ANY)
    return pl.pallas_call(
        backward_kernel,
        out_shape=(out, out, out, shape_of(early.shape, F32)),
        in_specs=[vmem] * 8 + [hbm],
        out_specs=(hbm,) * 4,
        scratch_shapes=[pltpu.VMEM((tok, width), BF16)] * 3
        + [pltpu.SemaphoreType.DMA((3, width // DH)), pltpu.SemaphoreType.DMA((late.shape[0],))],
        input_output_aliases={8: 3},
        compiler_params=params(16),
        cost_estimate=cost(1000, 1000),
    )(queries, keys, values, draw, prefix, suffix, glocal, late, early)


def halves(s_ref, half):
    first = pl.ds(pl.multiple_of(s_ref[3] * half, half), half)
    second = pl.ds(pl.multiple_of((1 - s_ref[3]) * half, half), half)
    return first, second


def project_near_kernel(s_ref, so_far_ref, a1_ref, a2_ref, m1_ref, z1_ref, o1_ref, oz1_ref, out_ref):
    first, second = halves(s_ref, m1_ref.shape[0])
    acc = so_far_ref[...] + dot_nn(a1_ref[:, first], m1_ref[...])
    acc += dot_nn(a1_ref[:, second], z1_ref[...])
    acc += dot_nn(a2_ref[:, first], o1_ref[...])
    acc += dot_nn(a2_ref[:, second], oz1_ref[...])
    out_ref[...] = acc


def project_near(scal, so_far, attns, pieces):
    return pl.pallas_call(
        project_near_kernel,
        out_shape=shape_of(so_far.shape, F32),
        in_specs=smem_then_vmem(7),
        compiler_params=params(16),
        cost_estimate=cost(1000, 1000),
    )(scal, so_far, *attns, *pieces)


def project_far_kernel(s_ref, near_ref, a_ref, d_ref, od_ref, dz_ref, odz_ref, out_hbm, out_buf, sems):
    first, second = halves(s_ref, d_ref.shape[0])
    blocks, _, block = out_buf.shape
    moves = []
    for j in range(blocks):
        here = slice(j * block, (j + 1) * block)
        acc = near_ref[:, here] + dot_nn(a_ref[:, first], d_ref[:, here] + od_ref[:, here])
        acc += dot_nn(a_ref[:, second], dz_ref[:, here] + odz_ref[:, here])
        out_buf[j] = acc.astype(BF16)
        moves.append(pltpu.make_async_copy(out_buf.at[j], out_hbm.at[:, here], sems.at[j]))
        moves[-1].start()
    for move in moves:
        move.wait()


def project_far(scal, near, attn, pieces):
    tok, out_width = near.shape
    block = 512
    return pl.pallas_call(
        project_far_kernel,
        out_shape=shape_of((tok, out_width), BF16),
        in_specs=smem_then_vmem(6),
        out_specs=pl.BlockSpec(memory_space=pl.ANY),
        scratch_shapes=[
            pltpu.VMEM((out_width // block, tok, block), BF16),
            pltpu.SemaphoreType.DMA((out_width // block,)),
        ],
        compiler_params=params(16),
        cost_estimate=cost(1000, 1000),
    )(scal, near, attn, *pieces)


def in_hbm(array):
    return pltpu.with_memory_space_constraint(array, pltpu.HBM)


def after(array, *needed):
    return lax.optimization_barrier((array, *needed))[0]


def shift(array, axis, count, by, wrap):
    pairs = [(i, (i + by) % count) for i in range(count) if wrap or 0 <= i + by < count]
    return lax.ppermute(array, axis, pairs)


def total(arrays):
    if len(arrays) == 1:
        return arrays[0]
    return functools.reduce(jnp.add, [a.astype(F32) for a in arrays])


def body(n_ctx, n_head, n_rep, queries, keys, values, out_weight, out_grad):
    c, h, z = lax.axis_index("ctx"), lax.axis_index("head"), lax.axis_index("rep")
    x, y, p = h & 1, h >> 1, z & 1
    scal = jnp.stack([c, y, x, p]).astype(jnp.int32)
    paired = n_ctx == 2 and n_head == 4 and n_rep % 2 == 0
    own_width = out_weight.shape[1]
    weight_hbm, grad_hbm = in_hbm(out_weight), in_hbm(out_grad)

    if paired:
        group = ("ctx", "head")
        near = [(4 * (i // 2) + i, i ^ 1) for i in range(4)]
        near += [(4 * (1 - i // 2) + i, 4 + (i ^ 2)) for i in range(4)]
        far = [(4 * (1 - i // 2) + i, 4 + (i ^ 3)) for i in range(4)]
        one = [(i, i ^ 1) for i in range(4)] + [(4 + i, 4 + (i ^ 2)) for i in range(4)]
        two = [(i, i ^ 2) for i in range(4)] + [(4 + i, 4 + (i ^ 1)) for i in range(4)]
        zpair = [(i, i ^ 1) for i in range(n_rep)]
        zfar = [(n_rep + i, n_rep + (i ^ 1)) for i in range(n_rep)]
        swap = [(0, 1), (1, 0)]
        state, near_piece, far_piece, turn, queries, keys, values = opening(
            scal, in_hbm(queries), in_hbm(keys), in_hbm(values), weight_hbm, grad_hbm
        )
        near_mine = lax.ppermute(near_piece, group, near)
        far_mine = lax.ppermute(far_piece, group, far)
        other_grad = lax.ppermute(turn, "ctx", swap)
    else:
        state = local_state(keys, values)
        other_grad = []
        for k in range(1, n_ctx):
            start = lax.rem(c + k, n_ctx) * own_width
            turn = lax.dynamic_slice_in_dim(out_grad, start, own_width, 1)
            other_grad.append(shift(turn, "ctx", n_ctx, k, True))
        other_grad = jnp.concatenate(other_grad, 0)

    carried = total([shift(state, "ctx", n_ctx, k, False) for k in range(1, n_ctx)])
    rest = [shift(out_weight, "ctx", n_ctx, -k, True) for k in range(1, n_ctx)]
    rest = rest[0] if n_ctx == 2 else jnp.concatenate(rest, 1)
    attn_grad = attn_gradient(scal, out_weight, out_grad, after(rest, state))
    carried = after(carried, attn_grad)
    attn, attn_t, raw, prefix = forward(queries, keys, values, carried)

    if paired:
        attn_1 = lax.ppermute(attn, group, one)
        attn_2 = lax.ppermute(attn, group, two)
        near_z = lax.ppermute(near_mine, "rep", zpair)
        raw = after(raw, near_mine, other_grad)
    other_attn = [shift(attn_t, "ctx", n_ctx, k, True) for k in range(1, n_ctx)]
    other_attn = other_attn[0] if n_ctx == 2 else jnp.concatenate(other_attn, 0)

    draw, gsum, glocal, own_out = cotangent(
        scal, attn_grad, queries, raw, attn, out_weight, rest, own_width // 2 if paired else own_width
    )
    suffix = total([shift(gsum, "ctx", n_ctx, -k, False) for k in range(1, n_ctx)])

    if paired:
        far_z = lax.ppermute(after(far_mine, gsum), ("ctx", "rep"), zfar)
        other_attn = after(other_attn, gsum, far_mine)

    early, late = own_weight_grad(scal, attn_t, out_grad, other_attn, other_grad)

    if paired:
        near_other = lax.ppermute(after(near_mine, late), "ctx", swap)
        suffix = after(suffix, late, attn_1)

    query_grad, key_grad, value_grad, weight_grad = backward(
        queries, keys, values, draw, prefix, suffix, glocal, late, early
    )

    if paired:
        attn_3 = lax.ppermute(after(attn_1, late), group, two)
        near_other_z = lax.ppermute(after(near_z, late), "ctx", swap)
        far_other = lax.ppermute(after(far_mine, late), "ctx", [(1, 0)])
        near_out = project_near(
            scal, after(own_out, query_grad), (attn_1, attn_2),
            (near_mine, near_z, near_other, near_other_z),
        )
        far_other_z = lax.ppermute(after(far_z, query_grad), "ctx", [(1, 0)])
        layer_out = project_far(scal, near_out, attn_3, (far_mine, far_other, far_z, far_other_z))
    else:
        full = lax.all_gather(out_weight, "ctx", axis=1, tiled=True)
        partial_out = jnp.dot(attn, full, preferred_element_type=F32).astype(BF16)
        layer_out = lax.psum_scatter(partial_out, "head", scatter_dimension=1, tiled=True)
    return layer_out, query_grad, key_grad, value_grad, weight_grad


def solution(mesh):
    tokens = P(("rep", "ctx"), "head")
    sizes = mesh.shape["ctx"], mesh.shape["head"], mesh.shape["rep"]
    return jax.shard_map(
        functools.partial(body, *sizes),
        mesh=mesh,
        in_specs=(tokens, tokens, tokens, P("head", "ctx"), P(("rep", "ctx"), None)),
        out_specs=(tokens, tokens, tokens, tokens, P(("rep", "head"), "ctx")),
        check_vma=False,
    )
```

```python
import functools

import jax
import jax.numpy as jnp
from jax import lax
from jax.experimental import pallas as pl
from jax.experimental.pallas import tpu as pltpu
from jax.sharding import PartitionSpec as P

DH = 128
CHUNK = 256
EPS = 1e-06
F32 = jnp.float32
BF16 = jnp.bfloat16


def feature(x):
    return jnp.where(x > 0, x + 1.0, jnp.exp(jnp.minimum(x, 0.0)))


def dot_nn(a, b):
    return lax.dot_general(a, b, (((1,), (0,)), ((), ())), preferred_element_type=F32)


def dot_nt(a, b):
    return lax.dot_general(a, b, (((1,), (1,)), ((), ())), preferred_element_type=F32)


def dot_tn(a, b):
    return lax.dot_general(a, b, (((0,), (0,)), ((), ())), preferred_element_type=F32)


def shape_of(shape, dtype):
    return jax.ShapeDtypeStruct(shape, dtype)


def params(mib):
    return pltpu.CompilerParams(vmem_limit_bytes=mib * 1024 * 1024)


def cost(flops, moved):
    return pl.CostEstimate(flops=flops, transcendentals=0, bytes_accessed=moved)


def state_kernel(k_ref, v_ref, out_ref):
    for lo in range(0, k_ref.shape[1], DH):
        cols = slice(lo, lo + DH)
        fk = feature(k_ref[:, cols].astype(F32)).astype(BF16)
        out_ref[cols, :] = dot_tn(fk, v_ref[:, cols]).astype(BF16)


def local_state(keys, values):
    width = keys.shape[1]
    return pl.pallas_call(
        state_kernel,
        out_shape=shape_of((width, DH), BF16),
        compiler_params=params(16),
        cost_estimate=cost(2 * keys.size * DH, 4 * keys.size),
    )(keys, values)


def opening_kernel(s_ref, q_hbm, k_hbm, v_hbm, weight_hbm, grad_hbm,
                   state_ref, near_ref, far_ref, turn_ref, q_ref, k_ref, v_ref, sems, slice_sems):
    half, wide = near_ref.shape
    rows = pl.ds(pl.multiple_of(s_ref[3] * half, half), half)
    far_column = 1 - s_ref[2]
    near_column = jnp.where(s_ref[0] == s_ref[1], far_column, s_ref[2])
    loads = []
    for i, lo in enumerate(range(0, k_hbm.shape[1], DH)):
        cols = pl.ds(lo, DH)
        loads.append([
            pltpu.make_async_copy(k_hbm.at[:, cols], k_ref.at[:, cols], sems.at[0, i]),
            pltpu.make_async_copy(v_hbm.at[:, cols], v_ref.at[:, cols], sems.at[1, i]),
        ])
        loads[-1][0].start()
        loads[-1][1].start()
    moves = []
    for i, (column, ref) in enumerate([(near_column, near_ref), (far_column, far_ref)]):
        cols = pl.ds(pl.multiple_of(column * wide, wide), wide)
        moves.append(pltpu.make_async_copy(weight_hbm.at[rows, cols], ref, slice_sems.at[i]))
        moves[-1].start()
    moves.append(pltpu.make_async_copy(q_hbm, q_ref, slice_sems.at[2]))
    moves[-1].start()
    own = turn_ref.shape[1]
    cols = pl.ds(pl.multiple_of((1 - s_ref[0]) * own, own), own)
    moves.append(pltpu.make_async_copy(grad_hbm.at[:, cols], turn_ref, slice_sems.at[3]))
    moves[-1].start()
    for i, lo in enumerate(range(0, k_hbm.shape[1], DH)):
        cols = slice(lo, lo + DH)
        loads[i][0].wait()
        loads[i][1].wait()
        fk = feature(k_ref[:, cols].astype(F32)).astype(BF16)
        state_ref[cols, :] = dot_tn(fk, v_ref[:, cols]).astype(BF16)
    for move in moves:
        move.wait()


def opening(scal, queries, keys, values, weight, out_grad):
    tok, width = keys.shape
    piece = shape_of((weight.shape[0] // 2, weight.shape[1] // 2), BF16)
    hbm = pl.BlockSpec(memory_space=pltpu.HBM)
    vmem = pl.BlockSpec(memory_space=pltpu.VMEM)
    return pl.pallas_call(
        opening_kernel,
        out_shape=(shape_of((width, DH), BF16), piece, piece, shape_of((tok, weight.shape[1]), BF16))
        + (shape_of(keys.shape, BF16),) * 3,
        in_specs=[pl.BlockSpec(memory_space=pltpu.SMEM)] + [hbm] * 5,
        out_specs=(vmem,) * 7,
        scratch_shapes=[
            pltpu.SemaphoreType.DMA((2, width // DH)),
            pltpu.SemaphoreType.DMA((4,)),
        ],
        compiler_params=params(16),
        cost_estimate=cost(2 * keys.size * DH, 4 * keys.size),
    )(scal, queries, keys, values, weight, out_grad)


def forward_kernel(q_ref, k_ref, v_ref, carried_ref, attn_ref, attn_t_ref, raw_ref, prefix_ref):
    tok, width = q_ref.shape
    chunk = min(CHUNK, tok)
    row = lax.broadcasted_iota(jnp.int32, (chunk, chunk), 0)
    col = lax.broadcasted_iota(jnp.int32, (chunk, chunk), 1)
    lower = row >= col
    for lo in range(0, width, DH):
        cols = slice(lo, lo + DH)
        prefix = carried_ref[cols, :].astype(F32)
        for i in range(tok // chunk):
            rows = slice(i * chunk, (i + 1) * chunk)
            fq = feature(q_ref[rows, cols].astype(F32)).astype(BF16)
            fk = feature(k_ref[rows, cols].astype(F32)).astype(BF16)
            v = v_ref[rows, cols]
            low_prefix = prefix.astype(BF16)
            prefix_ref[i, cols, :] = low_prefix
            scores = jnp.where(lower, dot_nt(fq, fk), 0.0).astype(BF16)
            raw = dot_nn(scores, v) + dot_nn(fq, low_prefix)
            raw_ref[rows, cols] = raw
            inv = lax.rsqrt(jnp.mean(raw * raw, axis=-1, keepdims=True) + EPS)
            attn = (raw * inv).astype(BF16)
            attn_ref[rows, cols] = attn
            attn_t_ref[cols, rows] = attn.T
            if i + 1 < tok // chunk:
                prefix = prefix + dot_tn(fk, v)


def forward(queries, keys, values, carried):
    tok, width = queries.shape
    chunks = tok // min(CHUNK, tok)
    return pl.pallas_call(
        forward_kernel,
        out_shape=(
            shape_of((tok, width), BF16),
            shape_of((width, tok), BF16),
            shape_of((tok, width), F32),
            shape_of((chunks, width, DH), BF16),
        ),
        compiler_params=params(16),
        cost_estimate=cost(16 * queries.size * DH, 12 * queries.size),
    )(queries, keys, values, carried)


def smem_then_vmem(count):
    return [pl.BlockSpec(memory_space=pltpu.SMEM)] + [pl.BlockSpec(memory_space=pltpu.VMEM)] * count


def attn_grad_kernel(s_ref, own_ref, grad_ref, rest_ref, out_ref, acc_ref):
    own_width, rest_width = own_ref.shape[1], rest_ref.shape[1]
    count = (own_width + rest_width) // own_width

    def part(k):
        place = lax.rem(s_ref[0] + k, count) * own_width
        return grad_ref[:, pl.ds(pl.multiple_of(place, own_width), own_width)]

    acc_ref[...] = dot_nt(part(0), own_ref[...])
    for k in range(1, count):
        acc_ref[...] += dot_nt(part(k), rest_ref[:, (k - 1) * own_width : k * own_width])
    out_ref[...] = acc_ref[...].astype(BF16)


def attn_gradient(scal, weight, out_grad, rest):
    tok, width = out_grad.shape[0], weight.shape[0]
    return pl.pallas_call(
        attn_grad_kernel,
        out_shape=shape_of((tok, width), BF16),
        in_specs=smem_then_vmem(3),
        scratch_shapes=[pltpu.VMEM((tok, width), F32)],
        compiler_params=params(16),
        cost_estimate=cost(2 * out_grad.size * width, 4 * out_grad.size),
    )(scal, weight, out_grad, rest)


def cotangent_kernel(s_ref, attn_grad_ref, q_ref, raw_ref, attn_ref, own_ref, rest_ref,
                     draw_ref, gsum_ref, glocal_ref, out_ref):
    tok, width = q_ref.shape
    chunk = min(CHUNK, tok)
    for lo in range(0, width, DH):
        cols = slice(lo, lo + DH)
        later = jnp.zeros((DH, DH), F32)
        for i in reversed(range(tok // chunk)):
            rows = slice(i * chunk, (i + 1) * chunk)
            glocal_ref[i, cols, :] = later
            grad = attn_grad_ref[rows, cols].astype(F32)
            raw = raw_ref[rows, cols]
            inv = lax.rsqrt(jnp.mean(raw * raw, axis=-1, keepdims=True) + EPS)
            normed = raw * inv
            mean = jnp.mean(grad * normed, axis=-1, keepdims=True)
            draw = (inv * (grad - normed * mean)).astype(BF16)
            draw_ref[rows, cols] = draw
            fq = feature(q_ref[rows, cols].astype(F32)).astype(BF16)
            later = later + dot_tn(fq, draw)
        gsum_ref[cols, :] = later.astype(BF16)
    wide = out_ref.shape[1]
    if wide < own_ref.shape[1]:
        local = pl.ds(pl.multiple_of(s_ref[2] * wide, wide), wide)
        weight = jnp.where(s_ref[0] == s_ref[1], own_ref[:, local], rest_ref[:, local])
        out_ref[...] = dot_nn(attn_ref[...], weight)


def cotangent(scal, attn_grad, queries, raw, attn, own, rest, out_width):
    tok, width = queries.shape
    chunks = tok // min(CHUNK, tok)
    return pl.pallas_call(
        cotangent_kernel,
        out_shape=(
            shape_of((tok, width), BF16),
            shape_of((width, DH), BF16),
            shape_of((chunks, width, DH), F32),
            shape_of((tok, out_width), F32),
        ),
        in_specs=smem_then_vmem(6),
        compiler_params=params(16),
        cost_estimate=cost(2 * tok * width * out_width, 16 * queries.size),
    )(scal, attn_grad, queries, raw, attn, own, rest)


def weight_grad_kernel(pieces, s_ref, attn_t_ref, grad_ref, other_t_ref, other_grad_ref, *refs):
    piece_refs, share_refs = refs[:pieces], refs[pieces + 2 : -3]
    out_hbm, late_ref = refs[pieces : pieces + 2]
    out_buf, sems, piece_sems = refs[-3:]
    shares = []
    for n, piece_ref in enumerate(piece_refs):
        shares.append(pltpu.make_async_copy(piece_ref, share_refs[0].at[n], piece_sems.at[n]))
        shares[-1].start()
    width, tok = attn_t_ref.shape
    early, _, block = out_buf.shape
    blocks = early + late_ref.shape[0]
    moves = []
    for j in range(blocks):
        here = slice(j * block, (j + 1) * block)
        place = s_ref[0] * (blocks * block) + j * block
        part = grad_ref[:, pl.ds(pl.multiple_of(place, block), block)]
        acc = dot_nn(attn_t_ref[...], part).astype(BF16).astype(F32)
        for k in range(other_t_ref.shape[0] // width):
            other_t = other_t_ref[k * width : (k + 1) * width, :]
            part = other_grad_ref[k * tok : (k + 1) * tok, here]
            acc += dot_nn(other_t, part).astype(BF16).astype(F32)
        if j < early:
            out_buf[j] = acc
            moves.append(pltpu.make_async_copy(out_buf.at[j], out_hbm.at[:, here], sems.at[j]))
            moves[-1].start()
        else:
            late_ref[j - early] = acc
    for move in moves + shares:
        move.wait()


def own_weight_grad(scal, attn_t, out_grad, other_t, other_grad, pieces):
    width = attn_t.shape[0]
    own_width = other_grad.shape[1]
    block = min(256, own_width // 2)
    blocks = own_width // block
    early = blocks // 2
    vmem = pl.BlockSpec(memory_space=pltpu.VMEM)
    share = [shape_of((len(pieces), *pieces[0].shape), BF16)] if pieces else []
    return pl.pallas_call(
        functools.partial(weight_grad_kernel, len(pieces)),
        out_shape=[
            shape_of((width, own_width), F32),
            shape_of((blocks - early, width, block), F32),
            *share,
        ],
        in_specs=smem_then_vmem(4 + len(pieces)),
        out_specs=[pl.BlockSpec(memory_space=pl.ANY), vmem] + [vmem] * len(share),
        scratch_shapes=[
            pltpu.VMEM((early, width, block), F32),
            pltpu.SemaphoreType.DMA((early,)),
            pltpu.SemaphoreType.DMA((max(1, len(pieces)),)),
        ],
        compiler_params=params(16),
        cost_estimate=cost(1000, 1000),
    )(scal, attn_t, out_grad, other_t, other_grad, *pieces)


def backward_kernel(q_ref, k_ref, v_ref, draw_ref, prefix_ref, suffix_ref, glocal_ref, late_ref, early_hbm,
                    dq_hbm, dk_hbm, dv_hbm, grad_hbm, dq_ref, dk_ref, dv_ref, sems, late_sems):
    late, _, block = late_ref.shape
    moves = []
    for j in range(late):
        start = grad_hbm.shape[1] - (late - j) * block
        there = grad_hbm.at[:, start : start + block]
        moves.append(pltpu.make_async_copy(late_ref.at[j], there, late_sems.at[j]))
        moves[-1].start()
    tok, width = q_ref.shape
    chunk = min(CHUNK, tok)
    row = lax.broadcasted_iota(jnp.int32, (chunk, chunk), 0)
    col = lax.broadcasted_iota(jnp.int32, (chunk, chunk), 1)
    lower = row >= col
    upper = row <= col
    for head, lo in enumerate(range(0, width, DH)):
        cols = slice(lo, lo + DH)
        suffix = suffix_ref[cols, :].astype(F32)
        for i in range(tok // chunk):
            rows = slice(i * chunk, (i + 1) * chunk)
            q = q_ref[rows, cols].astype(F32)
            k = k_ref[rows, cols].astype(F32)
            q_slope = jnp.exp(jnp.minimum(q, 0.0))
            k_slope = jnp.exp(jnp.minimum(k, 0.0))
            fq = jnp.where(q > 0, q + 1.0, q_slope).astype(BF16)
            fk = jnp.where(k > 0, k + 1.0, k_slope).astype(BF16)
            v = v_ref[rows, cols]
            draw = draw_ref[rows, cols]
            later = (suffix + glocal_ref[i, cols, :]).astype(BF16)
            dscores = jnp.where(lower, dot_nt(draw, v), 0.0).astype(BF16)
            dfq = dot_nn(dscores, fk) + dot_nt(draw, prefix_ref[i, cols, :])
            dq_ref[rows, cols] = (dfq * q_slope).astype(BF16)
            dscores_t = jnp.where(upper, dot_nt(v, draw), 0.0).astype(BF16)
            dfk = dot_nn(dscores_t, fq) + dot_nt(v, later)
            dk_ref[rows, cols] = (dfk * k_slope).astype(BF16)
            scores_t = jnp.where(upper, dot_nt(fk, fq), 0.0).astype(BF16)
            dv = dot_nn(scores_t, draw) + dot_nn(fk, later)
            dv_ref[rows, cols] = dv.astype(BF16)
        for n, (ref, hbm) in enumerate([(dq_ref, dq_hbm), (dk_ref, dk_hbm), (dv_ref, dv_hbm)]):
            moves.append(pltpu.make_async_copy(ref.at[:, cols], hbm.at[:, cols], sems.at[n, head]))
            moves[-1].start()
    for move in moves:
        move.wait()


def backward(queries, keys, values, draw, prefix, suffix, glocal, late, early):
    tok, width = queries.shape
    out = shape_of(queries.shape, BF16)
    vmem, hbm = pl.BlockSpec(memory_space=pltpu.VMEM), pl.BlockSpec(memory_space=pl.ANY)
    return pl.pallas_call(
        backward_kernel,
        out_shape=(out, out, out, shape_of(early.shape, F32)),
        in_specs=[vmem] * 8 + [hbm],
        out_specs=(hbm,) * 4,
        scratch_shapes=[pltpu.VMEM((tok, width), BF16)] * 3
        + [pltpu.SemaphoreType.DMA((3, width // DH)), pltpu.SemaphoreType.DMA((late.shape[0],))],
        input_output_aliases={8: 3},
        compiler_params=params(16),
        cost_estimate=cost(256 * queries.size * DH, 64 * queries.size),
    )(queries, keys, values, draw, prefix, suffix, glocal, late, early)


def halves(s_ref, half):
    first = pl.ds(pl.multiple_of(s_ref[3] * half, half), half)
    second = pl.ds(pl.multiple_of((1 - s_ref[3]) * half, half), half)
    return first, second


def project_near_kernel(s_ref, so_far_ref, a1_ref, a2_ref, m1_ref, z1_ref, o1_ref, oz1_ref, out_ref):
    first, second = halves(s_ref, m1_ref.shape[0])
    acc = so_far_ref[...] + dot_nn(a1_ref[:, first], m1_ref[...])
    acc += dot_nn(a1_ref[:, second], z1_ref[...])
    acc += dot_nn(a2_ref[:, first], o1_ref[0])
    acc += dot_nn(a2_ref[:, second], oz1_ref[...])
    out_ref[...] = acc


def project_near(scal, so_far, attns, pieces):
    return pl.pallas_call(
        project_near_kernel,
        out_shape=shape_of(so_far.shape, F32),
        in_specs=smem_then_vmem(7),
        compiler_params=params(16),
        cost_estimate=cost(1000, 1000),
    )(scal, so_far, *attns, *pieces)


def project_far_kernel(s_ref, near_ref, a_ref, d_ref, od_ref, dz_ref, odz_ref, out_hbm, out_buf, sems):
    first, second = halves(s_ref, d_ref.shape[0])
    blocks, _, block = out_buf.shape
    moves = []
    for j in range(blocks):
        here = slice(j * block, (j + 1) * block)
        acc = near_ref[:, here] + dot_nn(a_ref[:, first], d_ref[:, here] + od_ref[1, :, here])
        acc += dot_nn(a_ref[:, second], dz_ref[:, here] + odz_ref[:, here])
        out_buf[j] = acc.astype(BF16)
        moves.append(pltpu.make_async_copy(out_buf.at[j], out_hbm.at[:, here], sems.at[j]))
        moves[-1].start()
    for move in moves:
        move.wait()


def project_far(scal, near, attn, pieces):
    tok, out_width = near.shape
    block = 512
    return pl.pallas_call(
        project_far_kernel,
        out_shape=shape_of((tok, out_width), BF16),
        in_specs=smem_then_vmem(6),
        out_specs=pl.BlockSpec(memory_space=pl.ANY),
        scratch_shapes=[
            pltpu.VMEM((out_width // block, tok, block), BF16),
            pltpu.SemaphoreType.DMA((out_width // block,)),
        ],
        compiler_params=params(16),
        cost_estimate=cost(1000, 1000),
    )(scal, near, attn, *pieces)


def in_hbm(array):
    return pltpu.with_memory_space_constraint(array, pltpu.HBM)


def after(array, *needed):
    return lax.optimization_barrier((array, *needed))[0]


def shift(array, axis, count, by, wrap):
    pairs = [(i, (i + by) % count) for i in range(count) if wrap or 0 <= i + by < count]
    return lax.ppermute(array, axis, pairs)


def total(arrays):
    if len(arrays) == 1:
        return arrays[0]
    return functools.reduce(jnp.add, [a.astype(F32) for a in arrays])


def body(n_ctx, n_head, n_rep, queries, keys, values, out_weight, out_grad):
    c, h, z = lax.axis_index("ctx"), lax.axis_index("head"), lax.axis_index("rep")
    x, y, p = h & 1, h >> 1, z & 1
    scal = jnp.stack([c, y, x, p]).astype(jnp.int32)
    paired = n_ctx == 2 and n_head == 4 and n_rep % 2 == 0
    own_width = out_weight.shape[1]
    weight_hbm, grad_hbm = in_hbm(out_weight), in_hbm(out_grad)

    if paired:
        group = ("ctx", "head")
        near = [(4 * (i // 2) + i, i ^ 1) for i in range(4)]
        near += [(4 * (1 - i // 2) + i, 4 + (i ^ 2)) for i in range(4)]
        far = [(4 * (1 - i // 2) + i, 4 + (i ^ 3)) for i in range(4)]
        one = [(i, i ^ 1) for i in range(4)] + [(4 + i, 4 + (i ^ 2)) for i in range(4)]
        two = [(i, i ^ 2) for i in range(4)] + [(4 + i, 4 + (i ^ 1)) for i in range(4)]
        zpair = [(i, i ^ 1) for i in range(n_rep)]
        zfar = [(n_rep + i, n_rep + (i ^ 1)) for i in range(n_rep)]
        swap = [(0, 1), (1, 0)]
        state, near_piece, far_piece, turn, queries, keys, values = opening(
            scal, in_hbm(queries), in_hbm(keys), in_hbm(values), weight_hbm, grad_hbm
        )
        near_mine = lax.ppermute(near_piece, group, near)
        far_mine = lax.ppermute(far_piece, group, far)
        other_grad = lax.ppermute(turn, "ctx", swap)
    else:
        state = local_state(keys, values)
        other_grad = []
        for k in range(1, n_ctx):
            start = lax.rem(c + k, n_ctx) * own_width
            turn = lax.dynamic_slice_in_dim(out_grad, start, own_width, 1)
            other_grad.append(shift(turn, "ctx", n_ctx, k, True))
        other_grad = jnp.concatenate(other_grad, 0)

    carried = total([shift(state, "ctx", n_ctx, k, False) for k in range(1, n_ctx)])
    rest = [shift(out_weight, "ctx", n_ctx, -k, True) for k in range(1, n_ctx)]
    rest = rest[0] if n_ctx == 2 else jnp.concatenate(rest, 1)
    attn_grad = attn_gradient(scal, out_weight, out_grad, after(rest, state))
    carried = after(carried, attn_grad)
    attn, attn_t, raw, prefix = forward(queries, keys, values, carried)

    if paired:
        attn_1 = lax.ppermute(attn, group, one)
        attn_2 = lax.ppermute(attn, group, two)
        near_z = lax.ppermute(near_mine, "rep", zpair)
        raw = after(raw, near_mine, other_grad)
    other_attn = [shift(attn_t, "ctx", n_ctx, k, True) for k in range(1, n_ctx)]
    other_attn = other_attn[0] if n_ctx == 2 else jnp.concatenate(other_attn, 0)

    draw, gsum, glocal, own_out = cotangent(
        scal, attn_grad, queries, raw, attn, out_weight, rest, own_width // 2 if paired else own_width
    )
    suffix = total([shift(gsum, "ctx", n_ctx, -k, False) for k in range(1, n_ctx)])

    if paired:
        far_z = lax.ppermute(after(far_mine, gsum), ("ctx", "rep"), zfar)
        other_attn = after(other_attn, gsum, far_mine)

    pieces = (near_mine, far_mine) if paired else ()
    early, late, *share = own_weight_grad(scal, attn_t, out_grad, other_attn, other_grad, pieces)

    if paired:
        others = lax.ppermute(share[0], "ctx", swap)
        suffix = after(suffix, late, attn_1)

    query_grad, key_grad, value_grad, weight_grad = backward(
        queries, keys, values, draw, prefix, suffix, glocal, late, early
    )

    if paired:
        attn_3 = lax.ppermute(after(attn_1, late), group, two)
        near_other_z = lax.ppermute(after(near_z, late), "ctx", swap)
        near_out = project_near(
            scal, after(own_out, query_grad), (attn_1, attn_2),
            (near_mine, near_z, others, near_other_z),
        )
        far_other_z = lax.ppermute(after(far_z, query_grad), "ctx", [(1, 0)])
        layer_out = project_far(scal, near_out, attn_3, (far_mine, others, far_z, far_other_z))
    else:
        full = lax.all_gather(out_weight, "ctx", axis=1, tiled=True)
        partial_out = jnp.dot(attn, full, preferred_element_type=F32).astype(BF16)
        layer_out = lax.psum_scatter(partial_out, "head", scatter_dimension=1, tiled=True)
    return layer_out, query_grad, key_grad, value_grad, weight_grad


def solution(mesh):
    tokens = P(("rep", "ctx"), "head")
    sizes = mesh.shape["ctx"], mesh.shape["head"], mesh.shape["rep"]
    return jax.shard_map(
        functools.partial(body, *sizes),
        mesh=mesh,
        in_specs=(tokens, tokens, tokens, P("head", "ctx"), P(("rep", "ctx"), None)),
        out_specs=(tokens, tokens, tokens, tokens, P(("rep", "head"), "ctx")),
        check_vma=False,
    )
```

```python
import functools

import jax
import jax.numpy as jnp
from jax import lax
from jax.experimental import pallas as pl
from jax.experimental.pallas import tpu as pltpu
from jax.sharding import PartitionSpec as P

DH = 128
CHUNK = 256
EPS = 1e-06
F32 = jnp.float32
BF16 = jnp.bfloat16


def feature(x):
    return jnp.where(x > 0, x + 1.0, jnp.exp(jnp.minimum(x, 0.0)))


def dot_nn(a, b):
    return lax.dot_general(a, b, (((1,), (0,)), ((), ())), preferred_element_type=F32)


def dot_nt(a, b):
    return lax.dot_general(a, b, (((1,), (1,)), ((), ())), preferred_element_type=F32)


def dot_tn(a, b):
    return lax.dot_general(a, b, (((0,), (0,)), ((), ())), preferred_element_type=F32)


def shape_of(shape, dtype):
    return jax.ShapeDtypeStruct(shape, dtype)


def params(mib):
    return pltpu.CompilerParams(vmem_limit_bytes=mib * 1024 * 1024)


def cost(flops, moved):
    return pl.CostEstimate(flops=flops, transcendentals=0, bytes_accessed=moved)


def state_kernel(k_ref, v_ref, out_ref):
    for lo in range(0, k_ref.shape[1], DH):
        cols = slice(lo, lo + DH)
        fk = feature(k_ref[:, cols].astype(F32)).astype(BF16)
        out_ref[cols, :] = dot_tn(fk, v_ref[:, cols]).astype(BF16)


def local_state(keys, values):
    width = keys.shape[1]
    return pl.pallas_call(
        state_kernel,
        out_shape=shape_of((width, DH), BF16),
        compiler_params=params(16),
        cost_estimate=cost(2 * keys.size * DH, 4 * keys.size),
    )(keys, values)


def opening_kernel(s_ref, q_hbm, k_hbm, v_hbm, weight_hbm, grad_hbm,
                   state_ref, near_ref, far_ref, turn_ref, q_ref, k_ref, v_ref, sems, slice_sems):
    half, wide = near_ref.shape
    rows = pl.ds(pl.multiple_of(s_ref[3] * half, half), half)
    far_column = 1 - s_ref[2]
    near_column = jnp.where(s_ref[0] == s_ref[1], far_column, s_ref[2])
    loads = []
    for i, lo in enumerate(range(0, k_hbm.shape[1], DH)):
        cols = pl.ds(lo, DH)
        loads.append([
            pltpu.make_async_copy(k_hbm.at[:, cols], k_ref.at[:, cols], sems.at[0, i]),
            pltpu.make_async_copy(v_hbm.at[:, cols], v_ref.at[:, cols], sems.at[1, i]),
        ])
        loads[-1][0].start()
        loads[-1][1].start()
    moves = []
    for i, (column, ref) in enumerate([(near_column, near_ref), (far_column, far_ref)]):
        cols = pl.ds(pl.multiple_of(column * wide, wide), wide)
        moves.append(pltpu.make_async_copy(weight_hbm.at[rows, cols], ref, slice_sems.at[i]))
        moves[-1].start()
    moves.append(pltpu.make_async_copy(q_hbm, q_ref, slice_sems.at[2]))
    moves[-1].start()
    own = turn_ref.shape[1]
    cols = pl.ds(pl.multiple_of((1 - s_ref[0]) * own, own), own)
    moves.append(pltpu.make_async_copy(grad_hbm.at[:, cols], turn_ref, slice_sems.at[3]))
    moves[-1].start()
    for i, lo in enumerate(range(0, k_hbm.shape[1], DH)):
        cols = slice(lo, lo + DH)
        loads[i][0].wait()
        loads[i][1].wait()
        fk = feature(k_ref[:, cols].astype(F32)).astype(BF16)
        state_ref[cols, :] = dot_tn(fk, v_ref[:, cols]).astype(BF16)
    for move in moves:
        move.wait()


def opening(scal, queries, keys, values, weight, out_grad):
    tok, width = keys.shape
    piece = shape_of((weight.shape[0] // 2, weight.shape[1] // 2), BF16)
    hbm = pl.BlockSpec(memory_space=pltpu.HBM)
    vmem = pl.BlockSpec(memory_space=pltpu.VMEM)
    return pl.pallas_call(
        opening_kernel,
        out_shape=(shape_of((width, DH), BF16), piece, piece, shape_of((tok, weight.shape[1]), BF16))
        + (shape_of(keys.shape, BF16),) * 3,
        in_specs=[pl.BlockSpec(memory_space=pltpu.SMEM)] + [hbm] * 5,
        out_specs=(vmem,) * 7,
        scratch_shapes=[
            pltpu.SemaphoreType.DMA((2, width // DH)),
            pltpu.SemaphoreType.DMA((4,)),
        ],
        compiler_params=params(16),
        cost_estimate=cost(2 * keys.size * DH, 4 * keys.size),
    )(scal, queries, keys, values, weight, out_grad)


def forward_kernel(q_ref, k_ref, v_ref, carried_ref, attn_ref, attn_t_ref, raw_ref, prefix_ref):
    tok, width = q_ref.shape
    chunk = min(CHUNK, tok)
    row = lax.broadcasted_iota(jnp.int32, (chunk, chunk), 0)
    col = lax.broadcasted_iota(jnp.int32, (chunk, chunk), 1)
    lower = row >= col
    for lo in range(0, width, DH):
        cols = slice(lo, lo + DH)
        prefix = carried_ref[cols, :].astype(F32)
        for i in range(tok // chunk):
            rows = slice(i * chunk, (i + 1) * chunk)
            fq = feature(q_ref[rows, cols].astype(F32)).astype(BF16)
            fk = feature(k_ref[rows, cols].astype(F32)).astype(BF16)
            v = v_ref[rows, cols]
            low_prefix = prefix.astype(BF16)
            prefix_ref[i, cols, :] = low_prefix
            scores = jnp.where(lower, dot_nt(fq, fk), 0.0).astype(BF16)
            raw = dot_nn(scores, v) + dot_nn(fq, low_prefix)
            raw_ref[rows, cols] = raw
            inv = lax.rsqrt(jnp.mean(raw * raw, axis=-1, keepdims=True) + EPS)
            attn = (raw * inv).astype(BF16)
            attn_ref[rows, cols] = attn
            attn_t_ref[cols, rows] = attn.T
            if i + 1 < tok // chunk:
                prefix = prefix + dot_tn(fk, v)


def forward(queries, keys, values, carried):
    tok, width = queries.shape
    chunks = tok // min(CHUNK, tok)
    return pl.pallas_call(
        forward_kernel,
        out_shape=(
            shape_of((tok, width), BF16),
            shape_of((width, tok), BF16),
            shape_of((tok, width), F32),
            shape_of((chunks, width, DH), BF16),
        ),
        compiler_params=params(16),
        cost_estimate=cost(16 * queries.size * DH, 12 * queries.size),
    )(queries, keys, values, carried)


def smem_then_vmem(count):
    return [pl.BlockSpec(memory_space=pltpu.SMEM)] + [pl.BlockSpec(memory_space=pltpu.VMEM)] * count


def attn_grad_kernel(s_ref, own_ref, grad_ref, rest_ref, out_ref, acc_ref):
    own_width, rest_width = own_ref.shape[1], rest_ref.shape[1]
    count = (own_width + rest_width) // own_width

    def part(k):
        place = lax.rem(s_ref[0] + k, count) * own_width
        return grad_ref[:, pl.ds(pl.multiple_of(place, own_width), own_width)]

    acc_ref[...] = dot_nt(part(0), own_ref[...])
    for k in range(1, count):
        acc_ref[...] += dot_nt(part(k), rest_ref[:, (k - 1) * own_width : k * own_width])
    out_ref[...] = acc_ref[...].astype(BF16)


def attn_gradient(scal, weight, out_grad, rest):
    tok, width = out_grad.shape[0], weight.shape[0]
    return pl.pallas_call(
        attn_grad_kernel,
        out_shape=shape_of((tok, width), BF16),
        in_specs=smem_then_vmem(3),
        scratch_shapes=[pltpu.VMEM((tok, width), F32)],
        compiler_params=params(16),
        cost_estimate=cost(2 * out_grad.size * width, 4 * out_grad.size),
    )(scal, weight, out_grad, rest)


def cotangent_kernel(s_ref, attn_grad_ref, q_ref, raw_ref, attn_ref, own_ref, rest_ref,
                     draw_ref, gsum_ref, glocal_ref, out_ref):
    tok, width = q_ref.shape
    chunk = min(CHUNK, tok)
    for lo in range(0, width, DH):
        cols = slice(lo, lo + DH)
        later = jnp.zeros((DH, DH), F32)
        for i in reversed(range(tok // chunk)):
            rows = slice(i * chunk, (i + 1) * chunk)
            glocal_ref[i, cols, :] = later
            grad = attn_grad_ref[rows, cols].astype(F32)
            raw = raw_ref[rows, cols]
            inv = lax.rsqrt(jnp.mean(raw * raw, axis=-1, keepdims=True) + EPS)
            normed = raw * inv
            mean = jnp.mean(grad * normed, axis=-1, keepdims=True)
            draw = (inv * (grad - normed * mean)).astype(BF16)
            draw_ref[rows, cols] = draw
            fq = feature(q_ref[rows, cols].astype(F32)).astype(BF16)
            later = later + dot_tn(fq, draw)
        gsum_ref[cols, :] = later.astype(BF16)
    wide = out_ref.shape[1]
    if wide < own_ref.shape[1]:
        local = pl.ds(pl.multiple_of(s_ref[2] * wide, wide), wide)
        weight = jnp.where(s_ref[0] == s_ref[1], own_ref[:, local], rest_ref[:, local])
        out_ref[...] = dot_nn(attn_ref[...], weight)


def cotangent(scal, attn_grad, queries, raw, attn, own, rest, out_width):
    tok, width = queries.shape
    chunks = tok // min(CHUNK, tok)
    return pl.pallas_call(
        cotangent_kernel,
        out_shape=(
            shape_of((tok, width), BF16),
            shape_of((width, DH), BF16),
            shape_of((chunks, width, DH), F32),
            shape_of((tok, out_width), F32),
        ),
        in_specs=smem_then_vmem(6),
        compiler_params=params(16),
        cost_estimate=cost(2 * tok * width * out_width, 16 * queries.size),
    )(scal, attn_grad, queries, raw, attn, own, rest)


def weight_grad_kernel(pieces, s_ref, attn_t_ref, grad_ref, other_t_ref, other_grad_ref, *refs):
    piece_refs, share_refs = refs[:pieces], refs[pieces + 2 : -3]
    out_hbm, late_ref = refs[pieces : pieces + 2]
    out_buf, sems, piece_sems = refs[-3:]
    shares = []
    for n, piece_ref in enumerate(piece_refs):
        shares.append(pltpu.make_async_copy(piece_ref, share_refs[0].at[n], piece_sems.at[n]))
        shares[-1].start()
    width, tok = attn_t_ref.shape
    early, _, block = out_buf.shape
    blocks = early + late_ref.shape[0]
    moves = []
    for j in range(blocks):
        here = slice(j * block, (j + 1) * block)
        place = s_ref[0] * (blocks * block) + j * block
        part = grad_ref[:, pl.ds(pl.multiple_of(place, block), block)]
        acc = dot_nn(attn_t_ref[...], part).astype(BF16).astype(F32)
        for k in range(other_t_ref.shape[0] // width):
            other_t = other_t_ref[k * width : (k + 1) * width, :]
            part = other_grad_ref[k * tok : (k + 1) * tok, here]
            acc += dot_nn(other_t, part).astype(BF16).astype(F32)
        if j < early:
            out_buf[j] = acc
            moves.append(pltpu.make_async_copy(out_buf.at[j], out_hbm.at[:, here], sems.at[j]))
            moves[-1].start()
        else:
            late_ref[j - early] = acc
    for move in moves + shares:
        move.wait()


def own_weight_grad(scal, attn_t, out_grad, other_t, other_grad, pieces):
    width = attn_t.shape[0]
    own_width = other_grad.shape[1]
    block = min(256, own_width // 2)
    blocks = own_width // block
    early = blocks // 2
    vmem = pl.BlockSpec(memory_space=pltpu.VMEM)
    share = [shape_of((len(pieces), *pieces[0].shape), BF16)] if pieces else []
    return pl.pallas_call(
        functools.partial(weight_grad_kernel, len(pieces)),
        out_shape=[
            shape_of((width, own_width), F32),
            shape_of((blocks - early, width, block), F32),
            *share,
        ],
        in_specs=smem_then_vmem(4 + len(pieces)),
        out_specs=[pl.BlockSpec(memory_space=pl.ANY), vmem] + [vmem] * len(share),
        scratch_shapes=[
            pltpu.VMEM((early, width, block), F32),
            pltpu.SemaphoreType.DMA((early,)),
            pltpu.SemaphoreType.DMA((max(1, len(pieces)),)),
        ],
        compiler_params=params(16),
        cost_estimate=cost(1000, 1000),
    )(scal, attn_t, out_grad, other_t, other_grad, *pieces)


def backward_kernel(q_ref, k_ref, v_ref, draw_ref, prefix_ref, suffix_ref, glocal_ref, late_ref, early_hbm,
                    dq_hbm, dk_hbm, dv_hbm, grad_hbm, dq_ref, dk_ref, dv_ref, sems, late_sems):
    late, _, block = late_ref.shape
    moves = []
    for j in range(late):
        start = grad_hbm.shape[1] - (late - j) * block
        there = grad_hbm.at[:, start : start + block]
        moves.append(pltpu.make_async_copy(late_ref.at[j], there, late_sems.at[j]))
        moves[-1].start()
    tok, width = q_ref.shape
    chunk = min(CHUNK, tok)
    row = lax.broadcasted_iota(jnp.int32, (chunk, chunk), 0)
    col = lax.broadcasted_iota(jnp.int32, (chunk, chunk), 1)
    lower = row >= col
    upper = row <= col
    for head, lo in enumerate(range(0, width, DH)):
        cols = slice(lo, lo + DH)
        suffix = suffix_ref[cols, :].astype(F32)
        for i in range(tok // chunk):
            rows = slice(i * chunk, (i + 1) * chunk)
            q = q_ref[rows, cols].astype(F32)
            k = k_ref[rows, cols].astype(F32)
            q_slope = jnp.exp(jnp.minimum(q, 0.0))
            k_slope = jnp.exp(jnp.minimum(k, 0.0))
            fq = jnp.where(q > 0, q + 1.0, q_slope).astype(BF16)
            fk = jnp.where(k > 0, k + 1.0, k_slope).astype(BF16)
            v = v_ref[rows, cols]
            draw = draw_ref[rows, cols]
            later = (suffix + glocal_ref[i, cols, :]).astype(BF16)
            dscores = jnp.where(lower, dot_nt(draw, v), 0.0).astype(BF16)
            dfq = dot_nn(dscores, fk) + dot_nt(draw, prefix_ref[i, cols, :])
            dq_ref[rows, cols] = (dfq * q_slope).astype(BF16)
            dscores_t = jnp.where(upper, dot_nt(v, draw), 0.0).astype(BF16)
            dfk = dot_nn(dscores_t, fq) + dot_nt(v, later)
            dk_ref[rows, cols] = (dfk * k_slope).astype(BF16)
            scores_t = jnp.where(upper, dot_nt(fk, fq), 0.0).astype(BF16)
            dv = dot_nn(scores_t, draw) + dot_nn(fk, later)
            dv_ref[rows, cols] = dv.astype(BF16)
        for n, (ref, hbm) in enumerate([(dq_ref, dq_hbm), (dk_ref, dk_hbm), (dv_ref, dv_hbm)]):
            moves.append(pltpu.make_async_copy(ref.at[:, cols], hbm.at[:, cols], sems.at[n, head]))
            moves[-1].start()
    for move in moves:
        move.wait()


def backward(queries, keys, values, draw, prefix, suffix, glocal, late, early):
    tok, width = queries.shape
    out = shape_of(queries.shape, BF16)
    vmem, hbm = pl.BlockSpec(memory_space=pltpu.VMEM), pl.BlockSpec(memory_space=pl.ANY)
    return pl.pallas_call(
        backward_kernel,
        out_shape=(out, out, out, shape_of(early.shape, F32)),
        in_specs=[vmem] * 8 + [hbm],
        out_specs=(hbm,) * 4,
        scratch_shapes=[pltpu.VMEM((tok, width), BF16)] * 3
        + [pltpu.SemaphoreType.DMA((3, width // DH)), pltpu.SemaphoreType.DMA((late.shape[0],))],
        input_output_aliases={8: 3},
        compiler_params=params(16),
        cost_estimate=cost(256 * queries.size * DH, 64 * queries.size),
    )(queries, keys, values, draw, prefix, suffix, glocal, late, early)


def halves(s_ref, half):
    first = pl.ds(pl.multiple_of(s_ref[3] * half, half), half)
    second = pl.ds(pl.multiple_of((1 - s_ref[3]) * half, half), half)
    return first, second


def project_near_kernel(s_ref, so_far_ref, a1_ref, a2_ref, m1_ref, z1_ref, o1_ref, oz1_ref, out_ref):
    first, second = halves(s_ref, m1_ref.shape[0])
    acc = so_far_ref[...] + dot_nn(a1_ref[:, first], m1_ref[...])
    acc += dot_nn(a1_ref[:, second], z1_ref[...])
    acc += dot_nn(a2_ref[:, first], o1_ref[0])
    acc += dot_nn(a2_ref[:, second], oz1_ref[...])
    out_ref[...] = acc


def project_near(scal, so_far, attns, pieces):
    return pl.pallas_call(
        project_near_kernel,
        out_shape=shape_of(so_far.shape, F32),
        in_specs=smem_then_vmem(7),
        compiler_params=params(16),
        cost_estimate=cost(1000, 1000),
    )(scal, so_far, *attns, *pieces)


def project_far_kernel(s_ref, near_ref, a_ref, d_ref, od_ref, dz_ref, odz_ref, out_hbm, out_buf, sems):
    first, second = halves(s_ref, d_ref.shape[0])
    blocks, _, block = out_buf.shape
    moves = []
    for j in range(blocks):
        here = slice(j * block, (j + 1) * block)
        acc = near_ref[:, here] + dot_nn(a_ref[:, first], d_ref[:, here] + od_ref[1, :, here])
        acc += dot_nn(a_ref[:, second], dz_ref[:, here] + odz_ref[:, here])
        out_buf[j] = acc.astype(BF16)
        moves.append(pltpu.make_async_copy(out_buf.at[j], out_hbm.at[:, here], sems.at[j]))
        moves[-1].start()
    for move in moves:
        move.wait()


def project_far(scal, near, attn, pieces):
    tok, out_width = near.shape
    block = 512
    return pl.pallas_call(
        project_far_kernel,
        out_shape=shape_of((tok, out_width), BF16),
        in_specs=smem_then_vmem(6),
        out_specs=pl.BlockSpec(memory_space=pl.ANY),
        scratch_shapes=[
            pltpu.VMEM((out_width // block, tok, block), BF16),
            pltpu.SemaphoreType.DMA((out_width // block,)),
        ],
        compiler_params=params(16),
        cost_estimate=cost(1000, 1000),
    )(scal, near, attn, *pieces)


def in_hbm(array):
    return pltpu.with_memory_space_constraint(array, pltpu.HBM)


def after(array, *needed):
    return lax.optimization_barrier((array, *needed))[0]


def shift(array, axis, count, by, wrap):
    pairs = [(i, (i + by) % count) for i in range(count) if wrap or 0 <= i + by < count]
    return lax.ppermute(array, axis, pairs)


def total(arrays):
    if len(arrays) == 1:
        return arrays[0]
    return functools.reduce(jnp.add, [a.astype(F32) for a in arrays])


def body(n_ctx, n_head, n_rep, queries, keys, values, out_weight, out_grad):
    c, h, z = lax.axis_index("ctx"), lax.axis_index("head"), lax.axis_index("rep")
    x, y, p = h & 1, h >> 1, z & 1
    scal = jnp.stack([c, y, x, p]).astype(jnp.int32)
    paired = n_ctx == 2 and n_head == 4 and n_rep % 2 == 0
    own_width = out_weight.shape[1]
    weight_hbm, grad_hbm = in_hbm(out_weight), in_hbm(out_grad)

    if paired:
        group = ("ctx", "head")
        near = [(4 * (i // 2) + i, i ^ 1) for i in range(4)]
        near += [(4 * (1 - i // 2) + i, 4 + (i ^ 2)) for i in range(4)]
        far = [(4 * (1 - i // 2) + i, 4 + (i ^ 3)) for i in range(4)]
        one = [(i, i ^ 1) for i in range(4)] + [(4 + i, 4 + (i ^ 2)) for i in range(4)]
        two = [(i, i ^ 2) for i in range(4)] + [(4 + i, 4 + (i ^ 1)) for i in range(4)]
        zpair = [(i, i ^ 1) for i in range(n_rep)]
        zfar = [(n_rep + i, n_rep + (i ^ 1)) for i in range(n_rep)]
        swap = [(0, 1), (1, 0)]
        state, near_piece, far_piece, turn, queries, keys, values = opening(
            scal, in_hbm(queries), in_hbm(keys), in_hbm(values), weight_hbm, grad_hbm
        )
        near_mine = lax.ppermute(near_piece, group, near)
        far_mine = lax.ppermute(far_piece, group, far)
        other_grad = lax.ppermute(turn, "ctx", swap)
    else:
        state = local_state(keys, values)
        other_grad = []
        for k in range(1, n_ctx):
            start = lax.rem(c + k, n_ctx) * own_width
            turn = lax.dynamic_slice_in_dim(out_grad, start, own_width, 1)
            other_grad.append(shift(turn, "ctx", n_ctx, k, True))
        other_grad = jnp.concatenate(other_grad, 0)

    carried = total([shift(state, "ctx", n_ctx, k, False) for k in range(1, n_ctx)])
    rest = [shift(out_weight, "ctx", n_ctx, -k, True) for k in range(1, n_ctx)]
    rest = rest[0] if n_ctx == 2 else jnp.concatenate(rest, 1)
    attn_grad = attn_gradient(scal, out_weight, out_grad, after(rest, state))
    carried = after(carried, attn_grad)
    attn, attn_t, raw, prefix = forward(queries, keys, values, carried)

    if paired:
        attn_1 = lax.ppermute(attn, group, one)
        attn_2 = lax.ppermute(attn, group, two)
        near_z = lax.ppermute(near_mine, "rep", zpair)
        raw = after(raw, near_mine, other_grad)
    other_attn = [shift(attn_t, "ctx", n_ctx, k, True) for k in range(1, n_ctx)]
    other_attn = other_attn[0] if n_ctx == 2 else jnp.concatenate(other_attn, 0)

    draw, gsum, glocal, own_out = cotangent(
        scal, attn_grad, queries, raw, attn, out_weight, rest, own_width // 2 if paired else own_width
    )
    suffix = total([shift(gsum, "ctx", n_ctx, -k, False) for k in range(1, n_ctx)])

    if paired:
        far_z = lax.ppermute(after(far_mine, gsum), ("ctx", "rep"), zfar)
        other_attn = after(other_attn, gsum, far_mine)

    pieces = (near_mine, far_mine) if paired else ()
    early, late, *share = own_weight_grad(scal, attn_t, out_grad, other_attn, other_grad, pieces)

    if paired:
        others = lax.ppermute(share[0], "ctx", swap)
        suffix = after(suffix, late, attn_1)

    query_grad, key_grad, value_grad, weight_grad = backward(
        queries, keys, values, draw, prefix, suffix, glocal, late, early
    )

    if paired:
        attn_3 = lax.ppermute(after(attn_1, late), group, two)
        near_other_z = lax.ppermute(after(near_z, late), "ctx", swap)
        near_out = project_near(
            scal, after(own_out, query_grad, attn_3), (attn_1, attn_2),
            (near_mine, near_z, others, near_other_z),
        )
        far_other_z = lax.ppermute(after(far_z, query_grad), "ctx", [(1, 0)])
        layer_out = project_far(scal, near_out, attn_3, (far_mine, others, far_z, far_other_z))
    else:
        full = lax.all_gather(out_weight, "ctx", axis=1, tiled=True)
        partial_out = jnp.dot(attn, full, preferred_element_type=F32).astype(BF16)
        layer_out = lax.psum_scatter(partial_out, "head", scatter_dimension=1, tiled=True)
    return layer_out, query_grad, key_grad, value_grad, weight_grad


def solution(mesh):
    tokens = P(("rep", "ctx"), "head")
    sizes = mesh.shape["ctx"], mesh.shape["head"], mesh.shape["rep"]
    return jax.shard_map(
        functools.partial(body, *sizes),
        mesh=mesh,
        in_specs=(tokens, tokens, tokens, P("head", "ctx"), P(("rep", "ctx"), None)),
        out_specs=(tokens, tokens, tokens, tokens, P(("rep", "head"), "ctx")),
        check_vma=False,
    )
```
